32 devices in a mesh: dp: 8 (over z, y), fsdp: 4 (over x, core).
Axes of the slice: x: 2, y: 2, z: 4, core: 2. Of those that a mesh axis runs over, the one named last changes fastest.
Arguments:
- inputs: bfloat16 [16, 1024, 1024], P('dp', 'fsdp'), may hold values from -6 to 6
- teacher: bfloat16 [16, 1024, 1024], P('dp', 'fsdp'), may hold values from -16 to 16
- valid_mask: int32 [16, 1024], P('dp', 'fsdp'), may hold values from 0 to 1, as said below
- time_steps: int32 [16], P('dp'), may hold values from 0 to 999
- qkv_weight: float32 [1024, 3072], P(('dp', 'fsdp')), may hold values from -0.1875 to 0.1875
- out_weight: float32 [1024, 1024], P(('dp', 'fsdp')), may hold values from -4 to 4
- up_weight: float32 [1024, 4096], P(('dp', 'fsdp')), may hold values from -0.1875 to 0.1875
- down_weight: float32 [4096, 1024], P(('dp', 'fsdp')), may hold values from -0.09375 to 0.09375
- time_weight: float32 [256, 2048], P(('dp', 'fsdp')), may hold values from -0.375 to 0.375
- time_bias: float32 [2048], P(('dp', 'fsdp')), may hold values from -4 to 4
- norm_gain: float32 [1024], P(('dp', 'fsdp')), may hold values from 0.25 to 1.75
- norm_bias: float32 [1024], P(('dp', 'fsdp')), may hold values from -4 to 4
- up_bias: float32 [4096], P(('dp', 'fsdp')), may hold values from -6 to 6
- down_bias: float32 [1024], P(('dp', 'fsdp')), may hold values from -4 to 4
Outputs:
- activations: bfloat16 [16, 1024, 1024], P('dp', 'fsdp')
- loss: float32 [1], replicated
- input_grad: float32 [16, 1024, 1024], P('dp', 'fsdp')
- qkv_weight_grad: float32 [1024, 3072], P(('dp', 'fsdp'))
- out_weight_grad: float32 [1024, 1024], P(('dp', 'fsdp'))
- up_weight_grad: float32 [1024, 4096], P(('dp', 'fsdp'))
- down_weight_grad: float32 [4096, 1024], P(('dp', 'fsdp'))
- time_weight_grad: float32 [256, 2048], P(('dp', 'fsdp'))
- time_bias_grad: float32 [2048], P(('dp', 'fsdp'))
- norm_gain_grad: float32 [1024], P(('dp', 'fsdp'))
- norm_bias_grad: float32 [1024], P(('dp', 'fsdp'))
- up_bias_grad: float32 [4096], P(('dp', 'fsdp'))
- down_bias_grad: float32 [1024], P(('dp', 'fsdp'))
The draws below stay inside these ranges and needn't reach their ends.
Inputs may be any that keep to these rules, and one draw needn't show every extreme that they name: `valid_mask`: 1 marks a token whose output counts in the loss; the first token of every sequence counts.
All inputs are finite; a program needn't handle non-finite values.
Results may differ from the reference program's by a relative error of at most 0.012.
The reference program's roundings to bfloat16 on the way count: a program that leaves them out, or rounds other values in their place, can miss the bound.
Values may be sent and summed in bfloat16 or wider, within the bound.
No kernel may reach another device: no remote copies, remote signals or barrier semaphores. Data moves between devices by JAX's collectives and lax.ppermute only.
A program may use at most 192 MiB of HBM per device.

```python
import math
import jax
import jax.numpy as jnp
from jax import lax

D = 1024
H = 16
HD = 64
FF = 4096
TE = 256
LEN = 1024
SEQS = 16


def draw_valid_mask(key, part):
    draws = jax.random.randint(key, (SEQS, LEN), 0, 1000, dtype=jnp.int32)
    order = jnp.arange(SEQS, dtype=jnp.int32)[:, None] * LEN + jnp.arange(LEN, dtype=jnp.int32)[None, :]
    limit = 250 + 500 * order // (SEQS * LEN)
    leading = jnp.arange(LEN, dtype=jnp.int32)[None, :] == 0
    return jnp.where(jnp.logical_or(draws < limit, leading), 1, 0).astype(jnp.int32)


def draw_teacher(key, part):
    offset_key = jax.random.fold_in(key, 11)
    token_key = jax.random.fold_in(key, 12)
    offsets = jnp.clip(4.0 * jax.random.normal(offset_key, (SEQS, 1, D), jnp.float32), -11.0, 11.0)
    noise = jnp.clip(jax.random.normal(token_key, (SEQS, LEN, D), jnp.float32), -4.5, 4.5)
    return (offsets + noise).astype(jnp.bfloat16)


def place_ends(array, key, least, high):
    dims = array.shape
    spot = [jax.random.randint(jax.random.fold_in(key, axis), (), 0, dims[axis]) for axis in range(len(dims))]
    array = array.at[tuple(spot)].set(least)
    longest = dims.index(max(dims))
    spot[longest] = (spot[longest] + 1) % dims[longest]
    return array.at[tuple(spot)].set(high)


def shard_levels(stream_key, dims, cuts, least, top_value):
    level = 1.0
    for dim, blocks in cuts:
        steps = jax.random.uniform(jax.random.fold_in(jax.random.fold_in(stream_key, 6), dim), (blocks,), jnp.float32, least / len(cuts), top_value / len(cuts))
        level = level * jnp.repeat(jnp.exp(steps), dims[dim] // blocks).reshape((-1,) + (1,) * (len(dims) - 1 - dim))
    return level


def bell_draw(own_key, extent, width, reach, pieces=(), kind=jnp.bfloat16):
    array = width * jax.random.normal(own_key, extent, jnp.float32)
    if pieces:
        array = array * shard_levels(own_key, extent, pieces, -0.22, 0.18)
    return jnp.clip(array, -reach, reach).astype(kind)


def setup_inputs(seed: int = 0) -> dict:
    key_list = jax.random.split(jax.random.key(seed), 15)
    return {
        "inputs": bell_draw(key_list[0], (SEQS, LEN, D), 1.0, 6.0, ((0, 8), (1, 4))),
        "teacher": draw_teacher(jax.random.fold_in(key_list[14], 71), 0),
        "valid_mask": draw_valid_mask(jax.random.fold_in(key_list[14], 71), 0),
        "time_steps": place_ends(jax.random.randint(key_list[3], (SEQS,), 0, 1000), jax.random.fold_in(key_list[3], 1), 0, 999).astype(jnp.int32),
        "qkv_weight": bell_draw(key_list[4], (D, 3 * D), D ** -0.5, 0.1875, ((0, 32),), jnp.float32),
        "out_weight": bell_draw(key_list[5], (D, D), (max(2 * D // LEN, 1)) ** -0.5, 4.0, ((0, 32),), jnp.float32),
        "up_weight": bell_draw(key_list[6], (D, FF), D ** -0.5, 0.1875, ((0, 32),), jnp.float32),
        "down_weight": bell_draw(key_list[7], (FF, D), FF ** -0.5, 0.09375, ((0, 32),), jnp.float32),
        "time_weight": bell_draw(key_list[8], (TE, 2 * D), TE ** -0.5, 0.375, ((0, 32),), jnp.float32),
        "time_bias": bell_draw(key_list[9], (2 * D,), 0.3, 4.0, ((0, 32),), jnp.float32),
        "norm_gain": jnp.clip(1.0 + 0.15 * jax.random.normal(key_list[10], (D,), jnp.float32), 0.25, 1.75),
        "norm_bias": bell_draw(key_list[11], (D,), 0.3, 4.0, ((0, 32),), jnp.float32),
        "up_bias": bell_draw(key_list[12], (FF,), 0.5, 6.0, ((0, 32),), jnp.float32),
        "down_bias": bell_draw(key_list[13], (D,), 0.3, 4.0, ((0, 32),), jnp.float32),
    }


@jax.custom_vjp
def low(v):
    return lax.optimization_barrier(v.astype(jnp.bfloat16)).astype(jnp.float32)

@jax.custom_vjp
def low_back(v):
    return v

def low_keep(v):
    return (low(v), None)

def low_pass(kept, grad):
    return (grad,)

def back_keep(v):
    return (v, None)

def back_low(kept, grad):
    return (low(grad),)
low.defvjp(low_keep, low_pass)
low_back.defvjp(back_keep, back_low)
highest = lax.Precision.HIGHEST
epsilon = 1e-05

def rotation(length):
    half_width = HD // 2
    spread = jnp.exp(jnp.arange(half_width, dtype=jnp.float32) * (-2.0 * math.log(10000.0) / HD))
    angles = jnp.arange(length, dtype=jnp.float32)[:, None] * spread[None, :]
    return (jnp.cos(angles)[:, None, :], jnp.sin(angles)[:, None, :])

def rotate(values, cosine, sine_part):
    half_width = HD // 2
    first_half = values[..., :half_width]
    second_half = values[..., half_width:]
    return jnp.concatenate([first_half * cosine - second_half * sine_part, second_half * cosine + first_half * sine_part], axis=-1)

def time_features(time_steps):
    half_width = TE // 2
    spread = jnp.exp(jnp.arange(half_width, dtype=jnp.float32) * (-math.log(10000.0) / half_width))
    angles = time_steps.astype(jnp.float32)[:, None] * spread[None, :]
    return jnp.concatenate([jnp.sin(angles), jnp.cos(angles)], axis=-1)

def normalize(values):
    centre = values - lax.optimization_barrier(jnp.mean(values, axis=-1, keepdims=True))
    return centre * lax.rsqrt(lax.optimization_barrier(jnp.mean(centre * centre, axis=-1, keepdims=True)) + epsilon)

def layer(source, condition, weights):
    qkv_full, out_full, up_full, down_full, gain_full, shift_full, up_bias_full, down_bias_full = weights
    length = source.shape[0]
    cosine, sine_part = rotation(length)
    hidden = low(normalize(source) * (1.0 + condition[:D]) + condition[D:])
    project = low_back(jnp.dot(hidden, qkv_full, precision=highest))
    queries = low(rotate(project[:, :D].reshape(length, H, HD), cosine, sine_part))
    key_vectors = low(rotate(project[:, D:2 * D].reshape(length, H, HD), cosine, sine_part))
    values = low(project[:, 2 * D:].reshape(length, H, HD))
    scores = low_back(jnp.einsum('qhd,khd->hqk', queries, key_vectors, precision=highest) * 0.125)
    probs = low(jax.nn.softmax(scores, axis=-1))
    mixture = low(low_back(jnp.einsum('hqk,khd->qhd', probs, values, precision=highest))).reshape(length, D)
    middle = source + low_back(jnp.dot(mixture, out_full, precision=highest))
    second = low(normalize(middle) * gain_full + shift_full)
    inner_sum = low_back(jnp.dot(second, up_full, precision=highest) + up_bias_full)
    active = low(jax.nn.gelu(inner_sum, approximate=False))
    return middle + low_back(jnp.dot(active, down_full, precision=highest) + down_bias_full)

def reference(inputs, teacher, valid_mask, time_steps, qkv_weight, out_weight, up_weight, down_weight, time_weight, time_bias, norm_gain, norm_bias, up_bias, down_bias):
    source = inputs.astype(jnp.float32)
    target = teacher.astype(jnp.float32)
    valid_marks = valid_mask.astype(jnp.float32)
    valid_total = jnp.sum(valid_marks)
    features = low(time_features(time_steps))
    loss_scale = SEQS * LEN * D / 2

    def objective(source, qkv_weight, out_weight, up_weight, down_weight, time_weight, time_bias, norm_gain, norm_bias, up_bias, down_bias):
        condition = jnp.dot(features, low(time_weight), precision=highest) + low(time_bias)
        weights = (low(qkv_weight), low(out_weight), low(up_weight), low(down_weight), low(norm_gain), low(norm_bias), low(up_bias), low(down_bias))
        layer_step = jax.checkpoint(layer)

        def advance(running, element):
            return (running, layer_step(element[0], element[1], weights))
        running_out, outputs = lax.scan(advance, None, (source, condition))
        differ = outputs - target
        loss_value = jnp.sum(valid_marks[:, :, None] * differ * differ) / (valid_total * D)
        return (loss_value * loss_scale, (outputs, loss_value))
    operands = (source, qkv_weight, out_weight, up_weight, down_weight, time_weight, time_bias, norm_gain, norm_bias, up_bias, down_bias)
    scaled, pullback, extras = jax.vjp(objective, *operands, has_aux=True)
    gradients = pullback(jnp.ones_like(scaled))
    return (extras[0].astype(jnp.bfloat16), extras[1].reshape(1), gradients[0], gradients[1], gradients[2], gradients[3], gradients[4], gradients[5], gradients[6], gradients[7], gradients[8], gradients[9], gradients[10])
```

```python
import math

import jax
import jax.numpy as jnp
from jax import lax
from jax.sharding import PartitionSpec as P

HD = 64
TE = 256

b16 = jnp.bfloat16
f32 = jnp.float32
highest = lax.Precision.HIGHEST
epsilon = 1e-05
core_pairs = [(i, i ^ 1) for i in range(4)]
x_pairs = [(i, i ^ 2) for i in range(4)]


def swap_core(v):
    return lax.ppermute(v, "fsdp", core_pairs)


def swap_x(v):
    return lax.ppermute(v, "fsdp", x_pairs)


def swap_y(v):
    return lax.ppermute(v, "dp", [(i, i ^ 1) for i in range(lax.axis_size("dp"))])


def shift_z(v, k):
    size = lax.axis_size("dp")
    depth = size // 2
    return lax.ppermute(v, "dp", [(i, ((i // 2 + k) % depth) * 2 + i % 2) for i in range(size)])


def place():
    f = lax.axis_index("fsdp")
    d = lax.axis_index("dp")
    return f // 2, f % 2, d % 2, d // 2, lax.axis_size("dp") // 2


def pick(v, index, axis=0):
    return lax.dynamic_index_in_dim(v, index, axis, False)


def gather_chips(piece):
    x, c, y, z, depth = place()
    rows, cols = piece.shape
    half = rows // 2
    stack = jnp.zeros((depth, rows, cols), piece.dtype)
    stack = lax.dynamic_update_slice(stack, piece[None], (z, 0, 0))
    for k in range(1, depth):
        got = shift_z(piece, k)
        stack = lax.dynamic_update_slice(stack, got[None], ((z - k) % depth, 0, 0))
    top = stack[:, :half]
    low = stack[:, half:]
    top_x = swap_x(top)
    low_y = swap_y(low)
    top_far = swap_y(jnp.stack([top, top_x]))
    low_far = swap_x(jnp.stack([low, low_y]))
    whole = jnp.zeros((depth, 2, 2, rows, cols), piece.dtype)

    def put(whole, part, yy, xx, at):
        return lax.dynamic_update_slice(whole, part[:, None, None], (0, yy, xx, at, 0))

    whole = put(whole, top, y, x, 0)
    whole = put(whole, top_x, y, 1 - x, 0)
    whole = put(whole, top_far[0], 1 - y, x, 0)
    whole = put(whole, top_far[1], 1 - y, 1 - x, 0)
    whole = put(whole, low, y, x, half)
    whole = put(whole, low_y, 1 - y, x, half)
    whole = put(whole, low_far[0], y, 1 - x, half)
    whole = put(whole, low_far[1], 1 - y, 1 - x, half)
    return whole.reshape(4 * depth, rows, cols)


def add_low(a, b):
    return (a.astype(f32) + b.astype(f32)).astype(a.dtype)


def scatter_chips(parts):
    x, c, y, z, depth = place()
    chips, rows, cols = parts.shape
    half = rows // 2
    grid = parts.reshape(depth, 2, 2, rows, cols)
    top = grid[:, :, :, :half]
    low = grid[:, :, :, half:]
    top = add_low(pick(top, x, 2), swap_x(pick(top, 1 - x, 2)))
    low = add_low(pick(low, y, 1), swap_y(pick(low, 1 - y, 1)))
    top = add_low(pick(top, y, 1), swap_y(pick(top, 1 - y, 1)))
    low = add_low(pick(low, x, 1), swap_x(pick(low, 1 - x, 1)))
    both = jnp.concatenate([top, low], axis=1)
    total = pick(both, z).astype(f32)
    for k in range(1, depth):
        total = total + shift_z(pick(both, (z + k) % depth), k).astype(f32)
    return total


def scatter_small(parts):
    x, c, y, z, depth = place()
    grid = parts.reshape(depth, 2, 2, 1, parts.shape[-1])
    grid = pick(grid, x, 2) + swap_x(pick(grid, 1 - x, 2))
    grid = pick(grid, y, 1) + swap_y(pick(grid, 1 - y, 1))
    total = pick(grid, z)
    for k in range(1, depth):
        total = total + shift_z(pick(grid, (z + k) % depth), k)
    return total[0]


def stats(v):
    mean = jnp.mean(v, axis=-1, keepdims=True)
    centre = v - mean
    rate = lax.rsqrt(jnp.mean(centre * centre, axis=-1, keepdims=True) + epsilon)
    return centre * rate, rate


def norm_back(g, n, rate):
    return (g - jnp.mean(g, -1, keepdims=True) - n * jnp.mean(g * n, -1, keepdims=True)) * rate


def rotate(v, cosine, sine):
    a, b = jnp.split(v, 2, axis=-1)
    return jnp.concatenate([a * cosine - b * sine, b * cosine + a * sine], axis=-1)


def dot(a, b, da, db):
    return lax.dot_general(a, b, (((da,), (db,)), ((), ())), preferred_element_type=f32)


def attend(q, k, v):
    scores = jnp.einsum("qhd,khd->hqk", q, k, preferred_element_type=f32) * 0.125
    log_total = jax.nn.logsumexp(scores, axis=-1, keepdims=True)
    probs = jnp.exp(scores - log_total).astype(b16)
    return jnp.einsum("hqk,khd->qhd", probs, v, preferred_element_type=f32), log_total


def attend_back(q, k, v, log_total, mixture_grad):
    scores = jnp.einsum("qhd,khd->hqk", q, k, preferred_element_type=f32) * 0.125
    full = jnp.exp(scores - log_total)
    prob_grad = jnp.einsum("qhd,khd->hqk", mixture_grad, v, preferred_element_type=f32)
    score_grad = (full * (prob_grad - jnp.sum(full * prob_grad, -1, keepdims=True))).astype(b16)
    dq = jnp.einsum("hqk,khd->qhd", score_grad, k, preferred_element_type=f32) * 0.125
    dk = jnp.einsum("hqk,qhd->khd", score_grad, q, preferred_element_type=f32) * 0.125
    dv = jnp.einsum("hqk,qhd->khd", full.astype(b16), mixture_grad, preferred_element_type=f32)
    return dq, dk, dv


def body(
    inputs, teacher, valid_mask, time_steps, qkv_weight, out_weight, up_weight, down_weight,
    time_weight, time_bias, norm_gain, norm_bias, up_bias, down_bias,
):
    x, c, y, z, depth = place()
    chips = 4 * depth
    seqs, block, width = inputs.shape
    rows = qkv_weight.shape[0]
    hidden_width = up_weight.shape[1]
    half = width // 2
    core_heads = half // HD
    tokens = 4 * block
    mine = 2 * block
    f = 2 * x + c
    ff = hidden_width // 2

    def collect(v):
        return jnp.concatenate([pick(v, x), swap_x(pick(v, 1 - x))], axis=0)

    source_low = collect(inputs)
    source_all = jnp.concatenate([source_low, swap_core(source_low)], axis=0)
    marks = valid_mask.astype(b16)
    target_marks = collect(
        jnp.concatenate([teacher, jnp.broadcast_to(marks[:, :, None], (seqs, block, 128))], axis=2)
    )
    target = target_marks[:, :width].astype(f32)
    mark = target_marks[:, width : width + 1].astype(f32)
    blocks = jnp.stack([f, f ^ 2, f ^ 1, f ^ 3])
    positions = (blocks[:, None] * block + jnp.arange(block)[None, :]).reshape(tokens).astype(f32)

    def own_other(v):
        return pick(v, c, 2), pick(v, 1 - c, 2)

    count = jnp.sum(valid_mask)
    counts = jnp.stack([count // 256, count % 256]).astype(b16)
    vector = jnp.concatenate(
        [v.astype(b16) for v in (time_bias, norm_gain, norm_bias, up_bias, down_bias)] + [counts]
    )
    vector = jnp.pad(vector, (0, 384 - vector.shape[0])).reshape(3, 128)
    vector = jnp.pad(vector, ((0, rows - 3), (0, 0)))
    qkv_own, qkv_other = own_other(qkv_weight.astype(b16).reshape(rows, 3, 2, half))
    up_own, up_other = own_other(up_weight.astype(b16).reshape(rows, -1, 2, down_weight.shape[0]))
    shape = (rows, -1)
    own = jnp.concatenate([vector, qkv_own.reshape(shape), up_own.reshape(shape)], axis=1)
    other = swap_core(
        jnp.concatenate([vector, qkv_other.reshape(shape), up_other.reshape(shape)], axis=1)
    )
    first = jnp.where(c == 0, own, other)
    second_rows = jnp.where(c == 0, other, own)
    chip = jnp.concatenate([first, second_rows], axis=0)
    cut = 128 + 3 * half
    group_1 = jnp.concatenate(
        [chip[:, :cut], time_weight.astype(b16).reshape(2 * rows, -1)], axis=1
    )
    group_2 = jnp.concatenate(
        [chip[:, cut:], out_weight.astype(b16).reshape(2 * rows, -1)], axis=1
    )
    group_3 = down_weight.astype(b16)
    all_1 = gather_chips(group_1)
    all_2 = gather_chips(group_2)
    all_3 = gather_chips(group_3)
    qkv_full = all_1[:, :, 128:cut].reshape(width, 3 * half)
    time_full = all_1[:, :, cut:].reshape(TE // 2, 2 * width)
    up_full = all_2[:, :, :ff].reshape(width, ff)
    out_half = all_2[:, :, ff:].reshape(chips, 1, rows, width)
    out_far = swap_core(out_half)
    out_full = jnp.concatenate(
        [jnp.where(c == 0, out_half, out_far), jnp.where(c == 0, out_far, out_half)], axis=1
    ).reshape(width, width)
    down_full = all_3.reshape(ff, width)
    vectors = all_1[:, :, :128].reshape(chips, 2, rows, 128)[:, :, :3].reshape(chips, 2, 384)
    vectors = vectors.astype(f32)
    at = 0

    def take(n):
        nonlocal at
        at += n
        return vectors[:, :, at - n : at]

    bias_time = take(time_bias.shape[0]).reshape(2 * width)
    gain = take(rows).reshape(width)
    shift = take(rows).reshape(width)
    bias_up = pick(take(up_bias.shape[0]), c, 1).reshape(ff)
    bias_down = take(rows).reshape(width)
    counted = take(2).reshape(-1, 2)
    valid_total = jnp.sum(counted[:, 0]) * 256.0 + jnp.sum(counted[:, 1])
    token_total = lax.axis_size("dp") * seqs * tokens
    factor = (token_total * width / 2) / (valid_total * width)

    spread = jnp.exp(jnp.arange(TE // 2, dtype=f32) * (-math.log(10000.0) / (TE // 2)))
    angle = pick(time_steps, x).astype(f32) * spread
    features = jnp.concatenate([jnp.sin(angle), jnp.cos(angle)]).astype(b16)
    feature_core = pick(features.reshape(chips, 2, -1), c, 1).reshape(1, TE // 2)
    part = dot(feature_core, time_full, 1, 0)
    condition = (part + swap_core(part))[0] + bias_time
    scale = 1.0 + condition[:width]
    n1, rate1 = stats(source_all.astype(f32))
    hidden = (n1 * scale + condition[width:]).astype(b16)
    n1 = n1[:mine]
    rate1 = rate1[:mine]
    project = dot(hidden, qkv_full, 1, 0)
    turn = jnp.exp(jnp.arange(HD // 2, dtype=f32) * (-2.0 * math.log(10000.0) / HD))
    angles = positions[:, None] * turn[None, :]
    cosine = jnp.cos(angles)[:, None]
    sine = jnp.sin(angles)[:, None]
    heads = (tokens, core_heads, HD)
    q = rotate(project[:, :half].reshape(heads), cosine, sine).astype(b16)
    k = rotate(project[:, half : 2 * half].reshape(heads), cosine, sine).astype(b16)
    v = project[:, 2 * half :].reshape(heads).astype(b16)
    mixed, log_total = attend(q, k, v)
    mixed = mixed.astype(b16).reshape(tokens, half)
    mixed_far = swap_core(mixed[mine:])
    mixture = jnp.where(
        c == 0,
        jnp.concatenate([mixed[:mine], mixed_far], axis=1),
        jnp.concatenate([mixed_far, mixed[:mine]], axis=1),
    )
    middle = source_low.astype(f32) + dot(mixture, out_full, 1, 0)
    n2, rate2 = stats(middle)
    second = (n2 * gain + shift).astype(b16)
    second_all = jnp.concatenate([second, swap_core(second)], axis=0)
    inner = dot(second_all, up_full, 1, 0) + bias_up
    flat = 0.5 * (1.0 + lax.erf(inner * (2.0**-0.5)))
    active = (inner * flat).astype(b16)
    slope = flat + inner * jnp.exp(-0.5 * inner * inner) * ((2.0 * math.pi) ** -0.5)
    down = dot(active, down_full, 1, 0)
    result = middle + (down[:mine] + swap_core(down[mine:].astype(b16)).astype(f32) + bias_down)

    differ = result - target
    loss_part = jnp.sum(mark * differ * differ)
    result_grad = 2.0 * mark * differ * factor

    def spread_out(v):
        far = swap_x(v[block:])
        near = v[:block]
        return jnp.stack([jnp.where(x == 0, near, far), jnp.where(x == 0, far, near)])

    activations = spread_out(result.astype(b16))

    down_in = result_grad.astype(b16)
    down_in_all = jnp.concatenate([down_in, swap_core(down_in)], axis=0)
    down_bias_part = jnp.sum(down_in.astype(f32), axis=0)
    inner_grad = (dot(down_in_all, down_full, 1, 1) * slope).astype(b16)
    second_part = dot(inner_grad, up_full, 1, 1)
    second_grad = second_part[:mine] + swap_core(second_part[mine:].astype(b16)).astype(f32)
    down_term = dot(active, down_in_all, 0, 0).astype(b16)
    down_sum = scatter_chips(down_term.reshape(chips, -1, width))
    up_bias_part = jnp.sum(inner_grad.astype(f32), axis=0)
    up_term = dot(second_all, inner_grad, 0, 0).astype(b16)
    up_sum = scatter_chips(up_term.reshape(chips, -1, ff))
    gain_part = jnp.sum(second_grad * n2, axis=0)
    shift_part = jnp.sum(second_grad, axis=0)
    middle_grad = result_grad + norm_back(second_grad * gain, n2, rate2)
    branch = middle_grad.astype(b16)
    mixture_grad = dot(branch, out_full, 1, 1).astype(b16).reshape(mine, 2, half)
    mixture_grad = jnp.concatenate(
        [pick(mixture_grad, c, 1), swap_core(pick(mixture_grad, 1 - c, 1))], axis=0
    )
    out_term = dot(mixture, branch, 0, 0).astype(b16).reshape(chips, 2, rows, width)
    out_term = add_low(pick(out_term, c, 1), swap_core(pick(out_term, 1 - c, 1)))
    dq, dk, dv = attend_back(q, k, v, log_total, mixture_grad.reshape(heads))
    dq = rotate(dq, cosine, -sine)
    dk = rotate(dk, cosine, -sine)
    flat_shape = (tokens, half)
    project_grad = jnp.concatenate(
        [dq.reshape(flat_shape), dk.reshape(flat_shape), dv.reshape(flat_shape)], axis=1
    ).astype(b16)
    qkv_term = dot(hidden, project_grad, 0, 0).astype(b16)
    hidden_part = dot(project_grad, qkv_full, 1, 1)
    hidden_grad = hidden_part[:mine] + swap_core(hidden_part[mine:].astype(b16)).astype(f32)
    input_grad = spread_out(middle_grad + norm_back(hidden_grad * scale, n1, rate1))
    condition_part = jnp.concatenate([jnp.sum(hidden_grad * n1, 0), jnp.sum(hidden_grad, 0)])
    condition_grad = condition_part + swap_core(condition_part)
    time_term = (feature_core.reshape(-1, 1).astype(f32) * condition_grad[None]).astype(b16)
    last = jnp.concatenate(
        [
            qkv_term.reshape(chips, 2 * rows, 3 * half),
            out_term.reshape(chips, 2 * rows, half),
            time_term.reshape(chips, 2 * rows, -1),
        ],
        axis=2,
    )
    last_sum = scatter_chips(last)
    qkv_sum = last_sum[:, : 3 * half]
    out_sum = last_sum[:, 3 * half : 4 * half].reshape(rows, width)
    time_sum = last_sum[:, 4 * half :].reshape(-1, 2 * width)

    small = jnp.concatenate(
        [
            v.reshape(chips, 2, -1)
            for v in (condition_part, gain_part, shift_part, down_bias_part)
        ],
        axis=2,
    ).reshape(chips, -1)
    small_count = small.shape[1]
    small = jnp.concatenate(
        [small, up_bias_part.reshape(chips, -1), jnp.broadcast_to(loss_part, (chips, 64))], axis=1
    )
    small_sum = scatter_small(small)
    pairs = small_sum[:small_count].reshape(2, -1)
    up_bias_sum = small_sum[small_count : small_count + up_bias.shape[0]]
    loss_sum = small_sum[small_count + up_bias.shape[0] :]
    lead = pairs.shape[1]
    far = swap_core(jnp.concatenate([pick(pairs, 1 - c), loss_sum]))
    vec = pick(pairs, c) + far[:lead]
    loss = ((loss_sum[0] + far[lead]) / (valid_total * width)).reshape(1)

    def columns(total, inner_size):
        total = total.reshape(2, rows, -1, inner_size)
        near = pick(total, c)
        far = swap_core(pick(total, 1 - c))
        return jnp.stack(
            [jnp.where(c == 0, near, far), jnp.where(c == 0, far, near)], axis=2
        ).reshape(rows, -1)

    r2 = 2 * rows
    return (
        activations,
        loss,
        input_grad,
        columns(qkv_sum, half),
        out_sum,
        columns(up_sum, down_weight.shape[0]),
        down_sum,
        time_sum,
        vec[:r2],
        vec[r2 : r2 + rows],
        vec[r2 + rows : r2 + 2 * rows],
        up_bias_sum,
        vec[r2 + 2 * rows :],
    )


def solution(mesh):
    both = ("dp", "fsdp")
    tokens = P("dp", "fsdp", None)
    weight = P(both, None)
    vector = P(both)
    return jax.shard_map(
        body,
        mesh=mesh,
        in_specs=(tokens, tokens, P("dp", "fsdp"), P("dp")) + (weight,) * 5 + (vector,) * 5,
        out_specs=(tokens, P(), tokens) + (weight,) * 5 + (vector,) * 5,
        check_vma=False,
    )
```

```python
import math

import jax
import jax.numpy as jnp
from jax import lax
from jax.experimental import pallas as pl
from jax.experimental.pallas import tpu as pltpu
from jax.sharding import PartitionSpec as P

HD = 64
TE = 256

b16 = jnp.bfloat16
f32 = jnp.float32
highest = lax.Precision.HIGHEST
epsilon = 1e-05
little = pl.CostEstimate(flops=1, transcendentals=0, bytes_accessed=1)


def swap_core(v):
    return lax.ppermute(v, "core", [(0, 1), (1, 0)])


def swap_x(v):
    return lax.ppermute(v, "x", [(0, 1), (1, 0)])


def swap_y(v):
    return lax.ppermute(v, "y", [(0, 1), (1, 0)])


def shift_z(v, k):
    depth = lax.axis_size("z")
    return lax.ppermute(v, "z", [(i, (i + k) % depth) for i in range(depth)])


def place():
    return tuple(lax.axis_index(a) for a in ("x", "core", "y", "z")) + (lax.axis_size("z"),)


def pick(v, index, axis=0):
    return lax.dynamic_index_in_dim(v, index, axis, False)


def unread(deps):
    return [pl.BlockSpec(memory_space=pl.ANY)] * len(deps)


def move(place_of, sources, outs, copies, deps=()):
    def kernel(where, *refs):
        x, c, y, z = (where[i] for i in range(4))
        given = refs[: len(sources)]
        made = refs[len(sources) + len(deps) :]
        for source, read, out, write in copies(x, c, y, z):
            made[out][write] = given[source][read]

    near = pl.BlockSpec(memory_space=pltpu.VMEM)
    return pl.pallas_call(
        kernel,
        in_specs=[pl.BlockSpec(memory_space=pltpu.SMEM)] + [near] * len(sources) + unread(deps),
        out_specs=[near] * len(outs),
        out_shape=outs,
        compiler_params=pltpu.CompilerParams(vmem_limit_bytes=32 << 20),
        cost_estimate=little,
        name="move",
    )(place_of, *sources, *deps)


def tie(*values):
    return lax.optimization_barrier(values)


def gather_z(piece, tiled=False):
    return [piece] + [shift_z(piece, k) for k in range(1, place()[4])]


def stack_z(pieces, tiled=False, deps=()):
    x, c, y, z, depth = place()
    rows, cols = pieces[0].shape
    half = rows // 2
    if tiled:

        def copies(x, c, y, z):
            return [
                (k, pl.ds(h * half, half), h, lax.rem(z - k + depth, depth))
                for k in range(depth)
                for h in range(2)
            ]

        shape = jax.ShapeDtypeStruct((depth, half, cols), b16)
        return list(move(jnp.stack([x, c, y, z]), pieces, [shape, shape], copies, deps))
    stack = jnp.zeros((depth, rows, cols), b16)
    for k in range(depth):
        stack = lax.dynamic_update_slice(stack, pieces[k][None], ((z - k) % depth, 0, 0))
    return [stack[:, :half], stack[:, half:]]


def gather_near(stacks):
    top, low = stacks
    return top, low, swap_x(top), swap_y(low)


def gather_far(near):
    top, low, top_x, low_y = near
    return swap_y(jnp.stack([top, top_x])), swap_x(jnp.stack([low, low_y]))


def assemble(near, far, cuts, tiled=False):
    x, c, y, z, depth = place()
    top, low, top_x, low_y = near
    top_far, low_far = far
    half, cols = top.shape[1:]
    rows = 2 * half
    if tiled:
        every = slice(None)

        def copies(x, c, y, z):
            made = []
            for n in range(len(cuts) - 1):
                run = pl.ds(cuts[n], cuts[n + 1] - cuts[n])
                one = (every, every, run)
                up, down = pl.ds(0, half), pl.ds(half, half)
                made += [
                    (0, one, n, (every, y, x, up)),
                    (2, one, n, (every, y, 1 - x, up)),
                    (4, (0,) + one, n, (every, 1 - y, x, up)),
                    (4, (1,) + one, n, (every, 1 - y, 1 - x, up)),
                    (1, one, n, (every, y, x, down)),
                    (3, one, n, (every, 1 - y, x, down)),
                    (5, (0,) + one, n, (every, y, 1 - x, down)),
                    (5, (1,) + one, n, (every, 1 - y, 1 - x, down)),
                ]
            return made

        shapes = [
            jax.ShapeDtypeStruct((depth, 2, 2, rows, cuts[n + 1] - cuts[n]), top.dtype)
            for n in range(len(cuts) - 1)
        ]
        parts = move(
            jnp.stack([x, c, y, z]), [top, low, top_x, low_y, top_far, low_far], shapes, copies
        )
        return [p.reshape(4 * depth, rows, -1) for p in parts]
    whole = jnp.zeros((depth, 2, 2, rows, cols), top.dtype)

    def put(whole, part, yy, xx, at):
        return lax.dynamic_update_slice(whole, part[:, None, None], (0, yy, xx, at, 0))

    whole = put(whole, top, y, x, 0)
    whole = put(whole, top_x, y, 1 - x, 0)
    whole = put(whole, top_far[0], 1 - y, x, 0)
    whole = put(whole, top_far[1], 1 - y, 1 - x, 0)
    whole = put(whole, low, y, x, half)
    whole = put(whole, low_y, 1 - y, x, half)
    whole = put(whole, low_far[0], y, 1 - x, half)
    whole = put(whole, low_far[1], 1 - y, 1 - x, half)
    whole = whole.reshape(4 * depth, rows, cols)
    return [whole[:, :, cuts[n] : cuts[n + 1]] for n in range(len(cuts) - 1)]


def add_low(a, b):
    return (a.astype(f32) + b.astype(f32)).astype(a.dtype)


def exchange(v, axes):
    return lax.all_to_all(v, axes, 0, 0, tiled=True)


def add_up(v):
    total = v[0].astype(f32)
    for i in range(1, len(v)):
        total = total + v[i].astype(f32)
    return total


def add_near(got, where, tiled):
    depth = got.shape[1]
    if not tiled:
        z = lax.axis_index("z")
        both = add_up(got).astype(b16)
        return [pick(both, (z + k) % depth) for k in range(depth)]

    def kernel(where, got, *outs):
        for k in range(depth):
            at = lax.rem(where[3] + k, depth)
            total = got[0, at].astype(f32)
            for i in range(1, got.shape[0]):
                total = total + got[i, at].astype(f32)
            outs[k][...] = total.astype(b16)

    near = pl.BlockSpec(memory_space=pltpu.VMEM)
    return pl.pallas_call(
        kernel,
        in_specs=[pl.BlockSpec(memory_space=pltpu.SMEM), near],
        out_specs=[near] * depth,
        out_shape=[jax.ShapeDtypeStruct(got.shape[2:], b16)] * depth,
        compiler_params=pltpu.CompilerParams(vmem_limit_bytes=32 << 20),
        cost_estimate=little,
        name="add_near",
    )(where, got)


def stack_terms(first, second):
    chips, top, width = first.shape
    rows, runs = second.shape[1], second.shape[2] // width
    shape = (chips, top + runs * rows, width)
    if top % 16 or rows % 16:
        return jnp.concatenate([first] + jnp.split(second, runs, axis=2), axis=1)

    def kernel(first, second, made):
        made[:, :top] = first[...]
        for n in range(runs):
            made[:, top + n * rows : top + (n + 1) * rows] = second[
                :, :, n * width : (n + 1) * width
            ]

    near = pl.BlockSpec(memory_space=pltpu.VMEM)
    return pl.pallas_call(
        kernel,
        in_specs=[near, near],
        out_specs=near,
        out_shape=jax.ShapeDtypeStruct(shape, first.dtype),
        compiler_params=pltpu.CompilerParams(vmem_limit_bytes=40 << 20),
        cost_estimate=little,
        name="stack_terms",
    )(first, second)


def send_z(parts):
    return [parts[0]] + [shift_z(v, k) for k, v in enumerate(parts) if k]


def regroup(v, cuts):
    runs = [slice(cuts[n], cuts[n + 1]) for n in range(len(cuts) - 1)]
    if v.shape[2] % 16 or v.shape[3] % 128:
        return [jnp.swapaxes(v[..., run], 0, 1) for run in runs]

    def kernel(given, *made):
        for out, run in zip(made, runs):
            for i in range(v.shape[0]):
                for j in range(v.shape[1]):
                    out[j, i] = given[i, j, :, run]

    near = pl.BlockSpec(memory_space=pltpu.VMEM)
    return pl.pallas_call(
        kernel,
        in_specs=[near],
        out_specs=[near] * len(runs),
        out_shape=[
            jax.ShapeDtypeStruct((v.shape[1], v.shape[0], v.shape[2], r.stop - r.start), v.dtype)
            for r in runs
        ],
        compiler_params=pltpu.CompilerParams(vmem_limit_bytes=32 << 20),
        cost_estimate=little,
        name="regroup",
    )(v)


def swap_order(v):
    return regroup(v, [0, v.shape[3]])[0]


def scatter_send(parts, where, tiled, deps=()):
    x, c, y, z, depth = place()
    chips, rows, cols = parts.shape
    half = rows // 2
    if not tiled:
        grid = parts.reshape(depth, 2, 2, rows, cols)
        return [pick(grid[:, :, :, :half], 1 - x, 2), pick(grid[:, :, :, half:], 1 - y, 1)]

    def copies(x, c, y, z):
        return [
            (0, (slice(None), slice(None), 1 - x, 0), 0, slice(None)),
            (0, (slice(None), 1 - y, slice(None), 1), 1, slice(None)),
        ]

    shape = jax.ShapeDtypeStruct((depth, 2, half, cols), parts.dtype)
    grid = parts.reshape(depth, 2, 2, 2, half, cols)
    return list(move(where, [grid], [shape, shape], copies, deps))


def scatter_near(parts, got, where, tiled):
    x, c, y, z, depth = place()
    chips, rows, cols = parts.shape
    half = rows // 2
    if not tiled:
        grid = parts.reshape(depth, 2, 2, rows, cols)
        top = add_low(pick(grid[:, :, :, :half], x, 2), got[0])
        low = add_low(pick(grid[:, :, :, half:], y, 1), got[1])
        return pick(top, y, 1), pick(top, 1 - y, 1), pick(low, x, 1), pick(low, 1 - x, 1)

    def kernel(where, grid, top, low, keep_t, send_t, keep_l, send_l):
        x, y = where[0], where[2]
        for out, yy in ((keep_t, y), (send_t, 1 - y)):
            out[...] = add_low(grid[:, yy, x, 0], top[:, yy])
        for out, xx in ((keep_l, x), (send_l, 1 - x)):
            out[...] = add_low(grid[:, y, xx, 1], low[:, xx])

    near = pl.BlockSpec(memory_space=pltpu.VMEM)
    shape = jax.ShapeDtypeStruct((depth, half, cols), parts.dtype)
    return pl.pallas_call(
        kernel,
        in_specs=[pl.BlockSpec(memory_space=pltpu.SMEM)] + [near] * 3,
        out_specs=[near] * 4,
        out_shape=[shape] * 4,
        compiler_params=pltpu.CompilerParams(vmem_limit_bytes=32 << 20),
        cost_estimate=little,
        name="scatter_near",
    )(where, parts.reshape(depth, 2, 2, 2, half, cols), got[0], got[1])


def scatter_far(keep, got, where, tiled):
    x, c, y, z, depth = place()
    half, cols = keep[0].shape[1:]
    if not tiled:
        both = jnp.concatenate([add_low(k, g) for k, g in zip(keep, got)], axis=1)
        return [pick(both, (z + k) % depth) for k in range(depth)]

    def kernel(where, top, low, top_got, low_got, *outs):
        for k in range(depth):
            at = lax.rem(where[3] + k, depth)
            outs[k][:half] = add_low(top[at], top_got[at])
            outs[k][half:] = add_low(low[at], low_got[at])

    near = pl.BlockSpec(memory_space=pltpu.VMEM)
    shape = jax.ShapeDtypeStruct((2 * half, cols), keep[0].dtype)
    return pl.pallas_call(
        kernel,
        in_specs=[pl.BlockSpec(memory_space=pltpu.SMEM)] + [near] * 4,
        out_specs=[near] * depth,
        out_shape=[shape] * depth,
        compiler_params=pltpu.CompilerParams(vmem_limit_bytes=32 << 20),
        cost_estimate=little,
        name="scatter_far",
    )(where, keep[0], keep[1], got[0], got[1])


class Scatter:
    def __init__(self, parts, where, tiled, deps=()):
        self.parts, self.where, self.tiled = parts, where, tiled
        self.got = scatter_send(parts, where, tiled, deps)

    def near(self):
        top, low = self.got
        self.got = [swap_x(top), swap_y(low)]

    def add_near(self):
        keep_t, send_t, keep_l, send_l = scatter_near(self.parts, self.got, self.where, self.tiled)
        self.keep, self.got = [keep_t, keep_l], [send_t, send_l]

    def far(self):
        self.got = [swap_y(self.got[0]), swap_x(self.got[1])]

    def add_far(self):
        self.got = list(scatter_far(self.keep, self.got, self.where, self.tiled))

    def along(self):
        self.got = [self.got[0]] + [shift_z(v, k) for k, v in enumerate(self.got) if k]

    def total(self):
        return sum(v.astype(f32) for v in self.got)


def gather_small(v):
    chips = 4 * lax.axis_size("z")
    return exchange(jnp.broadcast_to(v, (chips,) + v.shape), ("z", "y", "x"))


def project_kernel(source, scale, shift, weight, hidden_out, project_out):
    v = source[...].astype(f32)
    centre = v - jnp.mean(v, axis=1, keepdims=True)
    rate = lax.rsqrt(jnp.mean(centre * centre, axis=1, keepdims=True) + epsilon)
    hidden = (centre * rate * scale[...] + shift[...]).astype(b16)
    hidden_out[...] = hidden
    project_out[...] = jnp.dot(hidden, weight[...], preferred_element_type=f32)


def project_tokens(source, scale, shift, weight):
    tokens, width = source.shape
    cols = weight.shape[1]
    step = 256
    row = pl.BlockSpec((1, width), lambda i: (0, 0))
    return pl.pallas_call(
        project_kernel,
        grid=(tokens // step,),
        in_specs=[
            pl.BlockSpec((step, width), lambda i: (i, 0)),
            row,
            row,
            pl.BlockSpec((width, cols), lambda i: (0, 0)),
        ],
        out_specs=[
            pl.BlockSpec((step, width), lambda i: (i, 0)),
            pl.BlockSpec((step, cols), lambda i: (i, 0)),
        ],
        out_shape=[
            jax.ShapeDtypeStruct((tokens, width), b16),
            jax.ShapeDtypeStruct((tokens, cols), f32),
        ],
        compiler_params=pltpu.CompilerParams(vmem_limit_bytes=48 << 20),
        cost_estimate=little,
        name="project",
    )(source, scale, shift, weight)


def stats(v):
    mean = jnp.mean(v, axis=-1, keepdims=True)
    centre = v - mean
    rate = lax.rsqrt(jnp.mean(centre * centre, axis=-1, keepdims=True) + epsilon)
    return centre * rate, rate


def norm_back(g, n, rate):
    return (g - jnp.mean(g, -1, keepdims=True) - n * jnp.mean(g * n, -1, keepdims=True)) * rate


def dot(a, b, da, db):
    return lax.dot_general(a, b, (((da,), (db,)), ((), ())), preferred_element_type=f32)


LOG2E = 1.4426950408889634
CHUNK = 512


def nn(a, b):
    return lax.dot_general(a, b, (((1,), (0,)), ((), ())), preferred_element_type=f32)


def nt(a, b):
    return lax.dot_general(a, b, (((1,), (1,)), ((), ())), preferred_element_type=f32)


def lane_halves(v):
    lane = lax.broadcasted_iota(jnp.int32, v.shape, 1)
    zero = jnp.zeros_like(v)
    return jnp.where(lane < HD, v, zero), jnp.where(lane < HD, zero, v)


def turn(v, cosine, sine):
    width = v.shape[1]
    lane = lax.broadcasted_iota(jnp.int32, v.shape, 1)
    swapped = jnp.where(
        lane % HD < HD // 2,
        pltpu.roll(v, width - HD // 2, 1),
        pltpu.roll(v, HD // 2, 1),
    )
    return v * cosine + swapped * sine


def attend_kernel(project_in, cos_in, sin_in, *refs):
    turned_out, mix_out, log_out = refs[-3:]
    cosine = cos_in[...]
    sine = sin_in[...]
    tokens = cosine.shape[0]
    q = turn(project_in[:, :128], cosine, sine).astype(b16)
    k = turn(project_in[:, 128:256], cosine, sine).astype(b16)
    v = project_in[:, 256:].astype(b16)
    turned_out[:, :128] = q
    turned_out[:, 128:256] = k
    turned_out[:, 256:] = v
    keys = lane_halves(k)
    v_turned = v.astype(f32).T.astype(b16)
    for at in range(0, tokens, CHUNK):
        part = q[at : at + CHUNK]
        mixed = []
        for h in range(2):
            scores = nt(keys[h], part) * (0.125 * LOG2E)
            top = jnp.max(scores, axis=0, keepdims=True)
            weight = jnp.exp2(scores - top)
            total = jnp.sum(weight, axis=0, keepdims=True)
            log_out[0, h : h + 1, at : at + CHUNK] = top + jnp.log2(total)
            probs = (weight * (1.0 / total)).astype(b16)
            mixed.append(nn(v_turned[h * HD : (h + 1) * HD], probs))
        mix_out[at : at + CHUNK] = jnp.concatenate(mixed, axis=0).T.astype(b16)


def attend(project, cosine, sine, start, pairs, deps=()):
    tokens = project.shape[0]
    table = pl.BlockSpec((tokens, 128), lambda p: (0, 0))
    return pl.pallas_call(
        attend_kernel,
        grid=(pairs,),
        in_specs=[pl.BlockSpec((tokens, 384), lambda p: (0, start + p)), table, table]
        + unread(deps),
        out_specs=[
            pl.BlockSpec((tokens, 384), lambda p: (0, p)),
            pl.BlockSpec((tokens, 128), lambda p: (0, p)),
            pl.BlockSpec((1, 2, tokens), lambda p: (p, 0, 0)),
        ],
        out_shape=[
            jax.ShapeDtypeStruct((tokens, 384 * pairs), b16),
            jax.ShapeDtypeStruct((tokens, 128 * pairs), b16),
            jax.ShapeDtypeStruct((pairs, 2, tokens), f32),
        ],
        compiler_params=pltpu.CompilerParams(vmem_limit_bytes=48 << 20),
        cost_estimate=little,
        name="attend",
    )(project, cosine, sine, *deps)


def attend_back_kernel(
    turned_in, grad_in, log_in, cos_in, sin_in, *refs
):
    grad_out, dk_sum, dv_sum, dq_turned = refs[-4:]
    q = turned_in[:, :128]
    k = turned_in[:, 128:256]
    tokens = q.shape[0]
    keys = lane_halves(k)
    values = lane_halves(turned_in[:, 256:])
    k_turned = k.astype(f32).T.astype(b16)
    for at in range(0, tokens, CHUNK):
        q_part = q[at : at + CHUNK]
        g_part = grad_in[at : at + CHUNK]
        q_halves = lane_halves(q_part)
        g_halves = lane_halves(g_part)
        for h in range(2):
            scores = nt(keys[h], q_part) * (0.125 * LOG2E)
            full = jnp.exp2(scores - log_in[0, h : h + 1, at : at + CHUNK])
            prob_grad = nt(values[h], g_part)
            product = full * prob_grad
            total = jnp.sum(product, axis=0, keepdims=True)
            score_grad = (product - full * total).astype(b16)
            dv_h = nn(full.astype(b16), g_halves[h])
            dk_h = nn(score_grad, q_halves[h])
            dq_turned[h * HD : (h + 1) * HD, at : at + CHUNK] = nn(
                k_turned[h * HD : (h + 1) * HD], score_grad
            )
            dk = dk_h if h == 0 else dk + dk_h
            dv = dv_h if h == 0 else dv + dv_h
        if at == 0:
            dk_sum[...] = dk
            dv_sum[...] = dv
        else:
            dk_sum[...] += dk
            dv_sum[...] += dv
    cosine = cos_in[...]
    sine = -sin_in[...]
    grad_out[:, :128] = turn(dq_turned[...].T * 0.125, cosine, sine).astype(b16)
    grad_out[:, 128:256] = turn(dk_sum[...] * 0.125, cosine, sine).astype(b16)
    grad_out[:, 256:] = dv_sum[...].astype(b16)


def attend_back(turned, log_total, mixture_grad, cosine, sine, start, grad_start, pairs, deps=()):
    tokens = turned.shape[0]
    table = pl.BlockSpec((tokens, 128), lambda p: (0, 0))
    return pl.pallas_call(
        attend_back_kernel,
        grid=(pairs,),
        in_specs=[
            pl.BlockSpec((tokens, 384), lambda p: (0, start + p)),
            pl.BlockSpec((tokens, 128), lambda p: (0, grad_start + p)),
            pl.BlockSpec((1, 2, tokens), lambda p: (start + p, 0, 0)),
            table,
            table,
        ]
        + unread(deps),
        out_specs=pl.BlockSpec((tokens, 384), lambda p: (0, p)),
        out_shape=jax.ShapeDtypeStruct((tokens, 384 * pairs), b16),
        scratch_shapes=[
            pltpu.VMEM((tokens, 128), f32),
            pltpu.VMEM((tokens, 128), f32),
            pltpu.VMEM((128, tokens), f32),
        ],
        compiler_params=pltpu.CompilerParams(vmem_limit_bytes=48 << 20),
        cost_estimate=little,
        name="attend_back",
    )(turned, mixture_grad, log_total, cosine, sine, *deps)


def prepare_kernel(where, vector, qkv, up, out, time, own, other, out_low, time_low):
    c = where[1]
    rows, width = out.shape
    half = width // 2
    step = 128
    for there, made in ((c, own), (1 - c, other)):
        made[:, :128] = jnp.zeros((rows, 128), b16)
        made[:3, :128] = vector[...].astype(b16)
        for p in range(half // 128):
            for n in range(3):
                at = pl.multiple_of(n * width + there * half + p * 128, 128)
                to = 128 + (3 * p + n) * 128
                made[:, to : to + 128] = qkv[:, pl.ds(at, 128)].astype(b16)
        to = 128 + 3 * half
        for n in range(up.shape[1] // (2 * step)):
            at = pl.multiple_of((2 * n + there) * step, 128)
            made[:, to + n * step : to + (n + 1) * step] = up[:, pl.ds(at, step)].astype(b16)
    for n in range(2):
        out_low[n * rows : (n + 1) * rows] = out[:, n * half : (n + 1) * half].astype(b16)
    te_rows = time.shape[0]
    folds = 2 * rows // te_rows
    cols = time.shape[1] // folds
    for n in range(0, folds, 2):
        pair = [time[:, (n + i) * cols : (n + i + 1) * cols] for i in range(2)]
        time_low[n * te_rows : (n + 2) * te_rows] = jnp.concatenate(pair, axis=0).astype(b16)


def prepare(where, vector, qkv, up, out, time):
    rows, width = out.shape
    cols = 128 + 3 * width // 2 + up.shape[1] // 2
    near = pl.BlockSpec(memory_space=pltpu.VMEM)
    return pl.pallas_call(
        prepare_kernel,
        in_specs=[pl.BlockSpec(memory_space=pltpu.SMEM)] + [near] * 5,
        out_specs=[near] * 4,
        out_shape=[
            jax.ShapeDtypeStruct((rows, cols), b16),
            jax.ShapeDtypeStruct((rows, cols), b16),
            jax.ShapeDtypeStruct((2 * rows, width // 2), b16),
            jax.ShapeDtypeStruct((2 * rows, time.size // (2 * rows)), b16),
        ],
        cost_estimate=little,
        name="prepare",
    )(where, vector, qkv, up, out, time)


def body(
    inputs, teacher, valid_mask, time_steps, qkv_weight, out_weight, up_weight, down_weight,
    time_weight, time_bias, norm_gain, norm_bias, up_bias, down_bias,
):
    x, c, y, z, depth = place()
    chips = 4 * depth
    k_chip = 4 * z + 2 * y + x
    seqs, block, width = inputs.shape
    rows = qkv_weight.shape[0]
    ff_rows = down_weight.shape[0]
    half = width // 2
    tokens = 4 * block
    mine = 2 * block
    ff = up_weight.shape[1] // 2
    pairs = half // 128

    tiled = rows % 32 == 0 and ff_rows % 128 == 0
    where = jnp.stack([x, c, y, z])

    count = jnp.sum(valid_mask)
    step = pick(time_steps, x)
    whole_numbers = jnp.stack([count // 256, count % 256, step // 32, step % 32]).astype(f32)
    vector = jnp.concatenate([time_bias, norm_gain, norm_bias, up_bias, down_bias, whole_numbers])
    vector = jnp.pad(vector, (0, 384 - vector.shape[0])).reshape(3, 128)
    te_rows = time_weight.shape[0]
    te_folds = 2 * rows // te_rows
    cut = 128 + 3 * half
    if tiled:
        own, other, out_low, time_low = prepare(
            where, vector, qkv_weight, up_weight, out_weight, time_weight
        )
    else:

        def own_other(v):
            return [pick(v, i, 2).reshape(rows, -1).astype(b16) for i in (c, 1 - c)]

        def fold(v, n):
            return jnp.concatenate(jnp.split(v.astype(b16), n, axis=1), axis=0)

        vector = jnp.pad(vector.astype(b16), ((0, rows - 3), (0, 0)))
        qkv_cut = qkv_weight.reshape(rows, 3, 2, pairs, 128).transpose(0, 3, 2, 1, 4)
        qkv_own, qkv_other = own_other(qkv_cut.reshape(rows, pairs, 2, 3 * 128))
        up_own, up_other = own_other(up_weight.reshape(rows, -1, 2, ff_rows))
        own = jnp.concatenate([vector, qkv_own, up_own], axis=1)
        other = jnp.concatenate([vector, qkv_other, up_other], axis=1)
        out_low, time_low = fold(out_weight, 2), fold(time_weight, te_folds)
    other = swap_core(other)
    last = own.shape[1]
    if tiled:
        first_half, second_half = pl.ds(0, rows), pl.ds(rows, rows)

        def copies(x, c, y, z):
            made = []
            for source, at in ((0, c), (1, 1 - c)):
                made.append((source, (slice(None), pl.ds(0, cut)), 0, (at, slice(None), pl.ds(0, cut))))
                made.append((source, (slice(None), pl.ds(cut, ff)), 1, (at, slice(None), pl.ds(0, ff))))
            for at, half_rows in enumerate((first_half, second_half)):
                made.append((3, (half_rows,), 0, (at, slice(None), pl.ds(cut, time_low.shape[1]))))
                made.append((2, (half_rows,), 1, (at, slice(None), pl.ds(ff, half))))
            return made

        shapes = [
            jax.ShapeDtypeStruct((2, rows, cut + time_low.shape[1]), b16),
            jax.ShapeDtypeStruct((2, rows, ff + half), b16),
        ]
        piece_1, piece_2 = move(where, [own, other, out_low, time_low], shapes, copies)
        piece_1 = piece_1.reshape(2 * rows, -1)
        piece_2 = piece_2.reshape(2 * rows, -1)
    else:
        chip = jnp.concatenate(
            [jnp.where(c == 0, own, other), jnp.where(c == 0, other, own)], axis=0
        )
        piece_1 = jnp.concatenate([chip[:, :cut], time_low], axis=1)
        piece_2 = jnp.concatenate([chip[:, cut:], out_low], axis=1)
    down_full = lax.all_gather(down_weight.astype(b16), ("z", "y", "x"), axis=0, tiled=True)

    source_far = swap_x(pick(inputs, 1 - x))
    piece_1, source_far = tie(piece_1, source_far)
    marks = valid_mask.astype(b16)
    target_marks = jnp.concatenate(
        [teacher, jnp.broadcast_to(marks[:, :, None], (seqs, block, 128))], axis=2
    )
    target_far, source_far = tie(pick(target_marks, 1 - x), source_far)
    target_far = swap_x(target_far)
    pieces_1 = gather_z(piece_1, tiled)
    stack_1 = stack_z(pieces_1, tiled)
    target_far, stack_1[0] = tie(target_far, stack_1[0])
    piece_2, stack_1[1] = tie(piece_2, stack_1[1])
    pieces_2 = gather_z(piece_2, tiled)
    near_1 = list(gather_near(stack_1))
    near_1[2], near_1[3], pieces_2[1] = tie(near_1[2], near_1[3], pieces_2[1])
    source_far, near_1[0] = tie(source_far, near_1[0])
    source_low = jnp.concatenate([pick(inputs, x), source_far], axis=0)
    source_all = jnp.concatenate([source_low, swap_core(source_low)], axis=0)
    far_1 = list(gather_far(near_1))
    vectors, qkv_full, time_full = assemble(
        near_1, far_1, [0, 128, cut, piece_1.shape[1]], tiled
    )
    qkv_full = qkv_full.reshape(width, 3 * half)
    near_2 = list(gather_near(stack_z(pieces_2, tiled, tuple(far_1))))
    f = 2 * x + c
    blocks = jnp.stack([f, f ^ 2, f ^ 1, f ^ 3])
    positions = (blocks[:, None] * block + jnp.arange(block)[None, :]).reshape(tokens).astype(f32)
    pace = jnp.exp(jnp.arange(HD // 2, dtype=f32) * (-2.0 * math.log(10000.0) / HD))
    angles = positions[:, None] * pace[None, :]
    cosine = jnp.tile(jnp.cos(angles), (1, 4))
    sine = jnp.sin(angles)
    sine = jnp.tile(jnp.concatenate([-sine, sine], axis=1), (1, 2))

    vectors = vectors.reshape(chips, 2, rows, 128)[:, :, :3].reshape(chips, 2, 384)
    vectors = vectors.astype(f32)
    at = 0

    def take(n):
        nonlocal at
        at += n
        return vectors[:, :, at - n : at]

    bias_time = take(time_bias.shape[0]).reshape(2 * width)
    gain = take(rows).reshape(width)
    shift = take(rows).reshape(width)
    bias_up = pick(take(ff_rows), c, 1).reshape(ff)
    bias_down = take(rows).reshape(width)
    numbers = take(4)
    valid_total = jnp.sum(numbers[:, :, 0]) * 256.0 + jnp.sum(numbers[:, :, 1])
    steps = numbers[:, 0, 2] * 32.0 + numbers[:, 0, 3]
    token_total = 2 * depth * seqs * tokens
    factor = (token_total * width / 2) / (valid_total * width)

    spread = jnp.exp(jnp.arange(TE // 2, dtype=f32) * (-math.log(10000.0) / (TE // 2)))
    angle = steps[:, None] * spread[None]
    features = jnp.concatenate([jnp.sin(angle), jnp.cos(angle)], axis=1).astype(b16)
    feature_core = pick(pick(features, k_chip).reshape(chips, 2, te_rows), c, 1)
    time_parts = time_full.reshape(chips, te_folds, te_rows, -1).astype(f32)
    part = jnp.sum(feature_core.astype(f32)[:, None, :, None] * time_parts, axis=(0, 2))
    part = part.reshape(-1, 128)
    condition = (part + swap_core(part)).reshape(2, width) + bias_time.reshape(2, width)
    scale = 1.0 + condition[:1]
    hidden, project = project_tokens(source_all, scale, condition[1:], qkv_full)
    near_2[2], near_2[3], project = tie(near_2[2], near_2[3], project)
    far_2 = list(gather_far(near_2))
    ahead = pairs // 2
    turned_a, mixed_a, log_a = attend(project, cosine, sine, 0, ahead)
    turned_b, mixed_b, log_b = attend(project, cosine, sine, ahead, pairs - ahead, (mixed_a,))
    far_2[0], mixed_a, mixed_b = tie(far_2[0], mixed_a, mixed_b)
    up_full, out_half = assemble(near_2, far_2, [0, ff, ff + half], tiled)
    up_full = up_full.reshape(width, ff)
    out_far = swap_core(out_half)
    if tiled:

        def copies(x, c, y, z):
            every = slice(None)
            return [
                (n, (every, pl.ds(h * rows, rows)), 0, (every, at, every, pl.ds(h * half, half)))
                for n, at in ((0, c), (1, 1 - c))
                for h in range(2)
            ]

        shape = jax.ShapeDtypeStruct((chips, 2, rows, width), b16)
        out_full = move(where, [out_half, out_far], [shape], copies)[0]
    else:
        out_both = jnp.stack(
            [jnp.where(c == 0, out_half, out_far), jnp.where(c == 0, out_far, out_half)], axis=1
        ).reshape(chips, 2, 2, rows, half)
        out_full = jnp.concatenate([out_both[:, :, 0], out_both[:, :, 1]], axis=-1)
    out_full = out_full.reshape(width, width)
    mixed = jnp.concatenate([mixed_a, mixed_b], axis=1)
    mixed_far = swap_core(mixed[mine:])
    mixture = jnp.where(
        c == 0,
        jnp.concatenate([mixed[:mine], mixed_far], axis=1),
        jnp.concatenate([mixed_far, mixed[:mine]], axis=1),
    )
    middle = source_low.astype(f32) + dot(mixture, out_full, 1, 0)
    n2, rate2 = stats(middle)
    second = (n2 * gain + shift).astype(b16)
    second_all = jnp.concatenate([second, swap_core(second)], axis=0)
    inner = dot(second_all, up_full, 1, 0) + bias_up
    flat = 0.5 * (1.0 + lax.erf(inner * (2.0**-0.5)))
    active = (inner * flat).astype(b16)
    slope = flat + inner * jnp.exp(-0.5 * inner * inner) * ((2.0 * math.pi) ** -0.5)
    down = dot(active, down_full, 1, 0)
    result = middle + (down[:mine] + swap_core(down[mine:].astype(b16)).astype(f32) + bias_down)

    target_marks = jnp.concatenate([pick(target_marks, x), target_far], axis=0)
    target = target_marks[:, :width].astype(f32)
    mark = target_marks[:, width : width + 1].astype(f32)
    differ = result - target
    loss_part = jnp.sum(mark * differ * differ)
    result_grad = 2.0 * mark * differ * factor

    def spread_out(v):
        far = swap_x(v[block:].astype(b16)).astype(v.dtype)
        near = v[:block]
        return jnp.stack([jnp.where(x == 0, near, far), jnp.where(x == 0, far, near)])

    down_in = result_grad.astype(b16)
    down_in_all = jnp.concatenate([down_in, swap_core(down_in)], axis=0)
    near_axes = ("y", "x")
    result_low = result.astype(b16)
    result_far = swap_x(result_low[block:])
    down_term = dot(active, down_in_all, 0, 0).astype(b16)
    down_in_all, down_term = tie(down_in_all, down_term)
    down_sum = lax.psum_scatter(down_term, ("z", "y", "x"), scatter_dimension=0, tiled=True)
    inner_grad = (dot(down_in_all, down_full, 1, 1) * slope).astype(b16)
    second_part = dot(inner_grad, up_full, 1, 1)
    second_send, second_all = tie(second_part[mine:].astype(b16), second_all)
    second_got = swap_core(second_send)
    up_term = dot(second_all, inner_grad, 0, 0).astype(b16)
    up_sum = Scatter(up_term.reshape(chips, -1, ff), where, tiled)
    second_got, up_sum.got[0] = tie(second_got, up_sum.got[0])
    up_sum.near()
    second_grad = second_part[:mine] + second_got.astype(f32)
    middle_grad = result_grad + norm_back(second_grad * gain, n2, rate2)
    branch = middle_grad.astype(b16)
    mixture_grad = dot(branch, out_full, 1, 1).astype(b16)
    mixture_far, branch = tie(
        lax.dynamic_slice_in_dim(mixture_grad, (1 - c) * half, half, 1), branch
    )
    mixture_far = swap_core(mixture_far)
    out_term = dot(mixture, branch, 0, 0).astype(b16).reshape(chips, 2, rows, width)
    mixture_far, out_send, out_keep = tie(
        mixture_far, pick(out_term, 1 - c, 1), pick(out_term, c, 1)
    )
    out_got = swap_core(out_send)
    mixture_grad = jnp.concatenate(
        [lax.dynamic_slice_in_dim(mixture_grad, c * half, half, 1), mixture_far], axis=0
    )

    def pair_back(p, deps):
        turned, log = (turned_a, log_a) if p < ahead else (turned_b, log_b)
        at = p if p < ahead else p - ahead
        return attend_back(turned, log, mixture_grad, cosine, sine, at, p, 1, deps)

    grads = [pair_back(0, ())]
    for p in range(1, pairs - 1):
        grads.append(pair_back(p, (grads[-1],)))
    up_sum.got[0], up_sum.got[1], grads[-1] = tie(up_sum.got[0], up_sum.got[1], grads[-1])
    up_sum.add_near()
    grads.append(pair_back(pairs - 1, (grads[-1], up_sum.keep[0])))
    up_sum.far()
    project_grad = jnp.concatenate(grads, axis=1)
    qkv_term = dot(hidden, project_grad, 0, 0).astype(b16).reshape(chips, 2 * rows, -1)
    qkv_cols = qkv_term.shape[2]
    out_term = add_low(out_keep, out_got)
    out_term = jnp.concatenate([out_term[:, :, :half], out_term[:, :, half:]], axis=1)
    last_sum = Scatter(jnp.concatenate([qkv_term, out_term], axis=2), where, tiled)
    project_grad, last_sum.got[0] = tie(project_grad, last_sum.got[0])
    last_sum.near()
    hidden_part = dot(project_grad, qkv_full, 1, 1)
    hidden_got, hidden_keep, *up_sum.got = tie(
        hidden_part[mine:].astype(b16), hidden_part[:mine], *up_sum.got
    )
    hidden_got = swap_core(hidden_got)
    up_sum.add_far()
    up_sum.got[0], hidden_got = tie(up_sum.got[0], hidden_got)
    up_sum.along()
    hidden_grad = hidden_keep + hidden_got.astype(f32)
    n1, rate1 = stats(source_low.astype(f32))
    activations = jnp.stack(
        [
            jnp.where(x == 0, result_low[:block], result_far),
            jnp.where(x == 0, result_far, result_low[:block]),
        ]
    )
    input_grad = middle_grad + norm_back(hidden_grad * scale, n1, rate1)

    small = jnp.concatenate(
        [
            jnp.sum(hidden_grad * n1, 0),
            jnp.sum(hidden_grad, 0),
            jnp.sum(second_grad * n2, 0),
            jnp.sum(second_grad, 0),
            jnp.sum(down_in.astype(f32), 0),
            jnp.full((128,), loss_part),
        ]
    )
    small = small.reshape(-1, 128)
    small_got = swap_core(small)
    last_sum.got[0], input_grad = tie(last_sum.got[0], input_grad)
    last_sum.add_near()
    small_got, input_grad, last_sum.got[0] = tie(small_got, input_grad, last_sum.got[0])
    last_sum.far()
    small = small + small_got
    up_bias_part = jnp.sum(inner_grad.astype(f32), 0).reshape(-1, 128)
    fill = jnp.zeros((-(small.shape[0] + up_bias_part.shape[0]) % 8, 128), f32)
    small = jnp.concatenate([small, up_bias_part, fill], axis=0)
    small = gather_small(small)
    input_grad = spread_out(input_grad)
    up_sum = up_sum.total()
    last_sum.add_far()
    last_sum.along()
    last_sum = last_sum.total()
    down_sum = down_sum.astype(f32)
    index = 2 * k_chip + c
    feature_rows = lax.dynamic_slice_in_dim(features, index * te_rows, te_rows, 1).astype(f32)
    time_sum = lax.dot_general(
        feature_rows,
        small[:, : 2 * width // 128].reshape(chips, -1),
        (((0,), (0,)), ((), ())),
        precision=highest,
    )
    sums = jnp.sum(small, axis=0).reshape(-1)

    def share(start, size, index):
        return lax.dynamic_slice_in_dim(sums[start:], index * size, size, 0)

    time_bias_sum = share(0, 2 * rows, index)
    gain_sum = share(2 * width, rows, index)
    shift_sum = share(3 * width, rows, index)
    down_bias_sum = share(4 * width, rows, index)
    up_bias_sum = share(5 * width + 128, ff_rows, k_chip)
    loss = (sums[5 * width] / (valid_total * width)).reshape(1)

    def columns(total, inner_size):
        total = total.reshape(2, rows, -1, inner_size)
        near = pick(total, c)
        far = swap_core(pick(total, 1 - c))
        return jnp.stack(
            [jnp.where(c == 0, near, far), jnp.where(c == 0, far, near)], axis=2
        ).reshape(rows, -1)

    out_sum = last_sum[:, qkv_cols:]
    out_sum = jnp.concatenate([out_sum[:rows], out_sum[rows:]], axis=1)
    qkv_sum = last_sum[:, :qkv_cols].reshape(2 * rows, pairs, 3, 128)
    qkv_sum = qkv_sum.transpose(0, 2, 1, 3).reshape(2 * rows, -1)
    return (
        activations,
        loss,
        input_grad,
        columns(qkv_sum, half),
        out_sum,
        columns(up_sum, ff_rows),
        down_sum,
        time_sum,
        time_bias_sum,
        gain_sum,
        shift_sum,
        up_bias_sum,
        down_bias_sum,
    )


def solution(mesh):
    split = mesh.devices.reshape(-1, 2, 2, 2)
    finer = jax.sharding.Mesh(split, ("z", "y", "x", "core"))
    both = ("z", "y", "x", "core")
    tokens = P(("z", "y"), ("x", "core"), None)
    weight = P(both, None)
    vector = P(both)
    return jax.shard_map(
        body,
        mesh=finer,
        in_specs=(tokens, tokens, P(("z", "y"), ("x", "core")), P(("z", "y"))) + (weight,) * 5 + (vector,) * 5,
        out_specs=(tokens, P(), tokens) + (weight,) * 5 + (vector,) * 5,
        check_vma=False,
    )
```

```python
import math

import jax
import jax.numpy as jnp
from jax import lax
from jax.experimental import pallas as pl
from jax.experimental.pallas import tpu as pltpu
from jax.sharding import PartitionSpec as P

HD = 64
TE = 256

b16 = jnp.bfloat16
f32 = jnp.float32
highest = lax.Precision.HIGHEST
epsilon = 1e-05
little = pl.CostEstimate(flops=1, transcendentals=0, bytes_accessed=1)


def swap_core(v):
    return lax.ppermute(v, "core", [(0, 1), (1, 0)])


def swap_x(v):
    return lax.ppermute(v, "x", [(0, 1), (1, 0)])


def swap_y(v):
    return lax.ppermute(v, "y", [(0, 1), (1, 0)])


def shift_z(v, k):
    depth = lax.axis_size("z")
    return lax.ppermute(v, "z", [(i, (i + k) % depth) for i in range(depth)])


def place():
    return tuple(lax.axis_index(a) for a in ("x", "core", "y", "z")) + (lax.axis_size("z"),)


def pick(v, index, axis=0):
    return lax.dynamic_index_in_dim(v, index, axis, False)


def unread(deps):
    return [pl.BlockSpec(memory_space=pl.ANY)] * len(deps)


def move(place_of, sources, outs, copies, deps=()):
    def kernel(where, *refs):
        x, c, y, z = (where[i] for i in range(4))
        given = refs[: len(sources)]
        made = refs[len(sources) + len(deps) :]
        for source, read, out, write in copies(x, c, y, z):
            made[out][write] = given[source][read]

    near = pl.BlockSpec(memory_space=pltpu.VMEM)
    return pl.pallas_call(
        kernel,
        in_specs=[pl.BlockSpec(memory_space=pltpu.SMEM)] + [near] * len(sources) + unread(deps),
        out_specs=[near] * len(outs),
        out_shape=outs,
        compiler_params=pltpu.CompilerParams(vmem_limit_bytes=32 << 20),
        cost_estimate=little,
        name="move",
    )(place_of, *sources, *deps)


def tie(*values):
    return lax.optimization_barrier(values)


def gather_z(piece, tiled=False):
    return [piece] + [shift_z(piece, k) for k in range(1, place()[4])]


def stack_z(pieces, tiled=False, deps=()):
    x, c, y, z, depth = place()
    rows, cols = pieces[0].shape
    half = rows // 2
    if tiled:

        def copies(x, c, y, z):
            return [
                (k, pl.ds(h * half, half), h, lax.rem(z - k + depth, depth))
                for k in range(depth)
                for h in range(2)
            ]

        shape = jax.ShapeDtypeStruct((depth, half, cols), b16)
        return list(move(jnp.stack([x, c, y, z]), pieces, [shape, shape], copies, deps))
    stack = jnp.zeros((depth, rows, cols), b16)
    for k in range(depth):
        stack = lax.dynamic_update_slice(stack, pieces[k][None], ((z - k) % depth, 0, 0))
    return [stack[:, :half], stack[:, half:]]


def gather_near(stacks):
    top, low = stacks
    return top, low, swap_x(top), swap_y(low)


def gather_far(near):
    top, low, top_x, low_y = near
    return swap_y(jnp.stack([top, top_x])), swap_x(jnp.stack([low, low_y]))


def assemble(near, far, cuts, tiled=False):
    x, c, y, z, depth = place()
    top, low, top_x, low_y = near
    top_far, low_far = far
    half, cols = top.shape[1:]
    rows = 2 * half
    if tiled:
        every = slice(None)

        def copies(x, c, y, z):
            made = []
            for n in range(len(cuts) - 1):
                run = pl.ds(cuts[n], cuts[n + 1] - cuts[n])
                one = (every, every, run)
                up, down = pl.ds(0, half), pl.ds(half, half)
                made += [
                    (0, one, n, (every, y, x, up)),
                    (2, one, n, (every, y, 1 - x, up)),
                    (4, (0,) + one, n, (every, 1 - y, x, up)),
                    (4, (1,) + one, n, (every, 1 - y, 1 - x, up)),
                    (1, one, n, (every, y, x, down)),
                    (3, one, n, (every, 1 - y, x, down)),
                    (5, (0,) + one, n, (every, y, 1 - x, down)),
                    (5, (1,) + one, n, (every, 1 - y, 1 - x, down)),
                ]
            return made

        shapes = [
            jax.ShapeDtypeStruct((depth, 2, 2, rows, cuts[n + 1] - cuts[n]), top.dtype)
            for n in range(len(cuts) - 1)
        ]
        parts = move(
            jnp.stack([x, c, y, z]), [top, low, top_x, low_y, top_far, low_far], shapes, copies
        )
        return [p.reshape(4 * depth, rows, -1) for p in parts]
    whole = jnp.zeros((depth, 2, 2, rows, cols), top.dtype)

    def put(whole, part, yy, xx, at):
        return lax.dynamic_update_slice(whole, part[:, None, None], (0, yy, xx, at, 0))

    whole = put(whole, top, y, x, 0)
    whole = put(whole, top_x, y, 1 - x, 0)
    whole = put(whole, top_far[0], 1 - y, x, 0)
    whole = put(whole, top_far[1], 1 - y, 1 - x, 0)
    whole = put(whole, low, y, x, half)
    whole = put(whole, low_y, 1 - y, x, half)
    whole = put(whole, low_far[0], y, 1 - x, half)
    whole = put(whole, low_far[1], 1 - y, 1 - x, half)
    whole = whole.reshape(4 * depth, rows, cols)
    return [whole[:, :, cuts[n] : cuts[n + 1]] for n in range(len(cuts) - 1)]


def add_low(a, b):
    return (a.astype(f32) + b.astype(f32)).astype(a.dtype)


def exchange(v, axes):
    return lax.all_to_all(v, axes, 0, 0, tiled=True)


def add_up(v):
    total = v[0].astype(f32)
    for i in range(1, len(v)):
        total = total + v[i].astype(f32)
    return total


def add_near(got, where, tiled):
    depth = got.shape[1]
    if not tiled:
        z = lax.axis_index("z")
        both = add_up(got).astype(b16)
        return [pick(both, (z + k) % depth) for k in range(depth)]

    def kernel(where, got, *outs):
        for k in range(depth):
            at = lax.rem(where[3] + k, depth)
            total = got[0, at].astype(f32)
            for i in range(1, got.shape[0]):
                total = total + got[i, at].astype(f32)
            outs[k][...] = total.astype(b16)

    near = pl.BlockSpec(memory_space=pltpu.VMEM)
    return pl.pallas_call(
        kernel,
        in_specs=[pl.BlockSpec(memory_space=pltpu.SMEM), near],
        out_specs=[near] * depth,
        out_shape=[jax.ShapeDtypeStruct(got.shape[2:], b16)] * depth,
        compiler_params=pltpu.CompilerParams(vmem_limit_bytes=32 << 20),
        cost_estimate=little,
        name="add_near",
    )(where, got)


def stack_terms(first, second):
    chips, top, width = first.shape
    rows, runs = second.shape[1], second.shape[2] // width
    shape = (chips, top + runs * rows, width)
    if top % 16 or rows % 16:
        return jnp.concatenate([first] + jnp.split(second, runs, axis=2), axis=1)

    def kernel(first, second, made):
        made[:, :top] = first[...]
        for n in range(runs):
            made[:, top + n * rows : top + (n + 1) * rows] = second[
                :, :, n * width : (n + 1) * width
            ]

    near = pl.BlockSpec(memory_space=pltpu.VMEM)
    return pl.pallas_call(
        kernel,
        in_specs=[near, near],
        out_specs=near,
        out_shape=jax.ShapeDtypeStruct(shape, first.dtype),
        compiler_params=pltpu.CompilerParams(vmem_limit_bytes=40 << 20),
        cost_estimate=little,
        name="stack_terms",
    )(first, second)


def send_z(parts):
    return [parts[0]] + [shift_z(v, k) for k, v in enumerate(parts) if k]


def regroup(v, cuts):
    runs = [slice(cuts[n], cuts[n + 1]) for n in range(len(cuts) - 1)]
    if v.shape[2] % 16 or v.shape[3] % 128:
        return [jnp.swapaxes(v[..., run], 0, 1) for run in runs]

    def kernel(given, *made):
        for out, run in zip(made, runs):
            for i in range(v.shape[0]):
                for j in range(v.shape[1]):
                    out[j, i] = given[i, j, :, run]

    near = pl.BlockSpec(memory_space=pltpu.VMEM)
    return pl.pallas_call(
        kernel,
        in_specs=[near],
        out_specs=[near] * len(runs),
        out_shape=[
            jax.ShapeDtypeStruct((v.shape[1], v.shape[0], v.shape[2], r.stop - r.start), v.dtype)
            for r in runs
        ],
        compiler_params=pltpu.CompilerParams(vmem_limit_bytes=32 << 20),
        cost_estimate=little,
        name="regroup",
    )(v)


def swap_order(v):
    return regroup(v, [0, v.shape[3]])[0]


def scatter_send(parts, where, tiled, deps=()):
    x, c, y, z, depth = place()
    chips, rows, cols = parts.shape
    half = rows // 2
    if not tiled:
        grid = parts.reshape(depth, 2, 2, rows, cols)
        return [pick(grid[:, :, :, :half], 1 - x, 2), pick(grid[:, :, :, half:], 1 - y, 1)]

    def copies(x, c, y, z):
        return [
            (0, (slice(None), slice(None), 1 - x, 0), 0, slice(None)),
            (0, (slice(None), 1 - y, slice(None), 1), 1, slice(None)),
        ]

    shape = jax.ShapeDtypeStruct((depth, 2, half, cols), parts.dtype)
    grid = parts.reshape(depth, 2, 2, 2, half, cols)
    return list(move(where, [grid], [shape, shape], copies, deps))


def scatter_near(parts, got, where, tiled):
    x, c, y, z, depth = place()
    chips, rows, cols = parts.shape
    half = rows // 2
    if not tiled:
        grid = parts.reshape(depth, 2, 2, rows, cols)
        top = add_low(pick(grid[:, :, :, :half], x, 2), got[0])
        low = add_low(pick(grid[:, :, :, half:], y, 1), got[1])
        return pick(top, y, 1), pick(top, 1 - y, 1), pick(low, x, 1), pick(low, 1 - x, 1)

    def kernel(where, grid, top, low, keep_t, send_t, keep_l, send_l):
        x, y = where[0], where[2]
        for out, yy in ((keep_t, y), (send_t, 1 - y)):
            out[...] = add_low(grid[:, yy, x, 0], top[:, yy])
        for out, xx in ((keep_l, x), (send_l, 1 - x)):
            out[...] = add_low(grid[:, y, xx, 1], low[:, xx])

    near = pl.BlockSpec(memory_space=pltpu.VMEM)
    shape = jax.ShapeDtypeStruct((depth, half, cols), parts.dtype)
    return pl.pallas_call(
        kernel,
        in_specs=[pl.BlockSpec(memory_space=pltpu.SMEM)] + [near] * 3,
        out_specs=[near] * 4,
        out_shape=[shape] * 4,
        compiler_params=pltpu.CompilerParams(vmem_limit_bytes=32 << 20),
        cost_estimate=little,
        name="scatter_near",
    )(where, parts.reshape(depth, 2, 2, 2, half, cols), got[0], got[1])


def scatter_far(keep, got, where, tiled, ordered=False):
    x, c, y, z, depth = place()
    half, cols = keep[0].shape[1:]
    if not tiled:
        both = jnp.concatenate([add_low(k, g) for k, g in zip(keep, got)], axis=1)
        return [both] if ordered else [pick(both, (z + k) % depth) for k in range(depth)]

    def kernel(where, top, low, top_got, low_got, *outs):
        if ordered:
            outs[0][:, :half] = add_low(top[...], top_got[...])
            outs[0][:, half:] = add_low(low[...], low_got[...])
            return
        for k in range(depth):
            at = lax.rem(where[3] + k, depth)
            outs[k][:half] = add_low(top[at], top_got[at])
            outs[k][half:] = add_low(low[at], low_got[at])

    near = pl.BlockSpec(memory_space=pltpu.VMEM)
    shape = jax.ShapeDtypeStruct(((depth,) if ordered else ()) + (2 * half, cols), keep[0].dtype)
    count = 1 if ordered else depth
    return pl.pallas_call(
        kernel,
        in_specs=[pl.BlockSpec(memory_space=pltpu.SMEM)] + [near] * 4,
        out_specs=[near] * count,
        out_shape=[shape] * count,
        compiler_params=pltpu.CompilerParams(vmem_limit_bytes=32 << 20),
        cost_estimate=little,
        name="scatter_far",
    )(where, keep[0], keep[1], got[0], got[1])


class Scatter:
    def __init__(self, parts, where, tiled, deps=()):
        self.parts, self.where, self.tiled = parts, where, tiled
        self.got = scatter_send(parts, where, tiled, deps)

    def near(self):
        top, low = self.got
        self.got = [swap_x(top), swap_y(low)]

    def add_near(self):
        keep_t, send_t, keep_l, send_l = scatter_near(self.parts, self.got, self.where, self.tiled)
        self.keep, self.got = [keep_t, keep_l], [send_t, send_l]

    def far(self):
        self.got = [swap_y(self.got[0]), swap_x(self.got[1])]

    def add_far(self, ordered=False):
        self.got = list(scatter_far(self.keep, self.got, self.where, self.tiled, ordered))

    def scatter_along(self):
        self.got = [lax.psum_scatter(self.got[0], "z", scatter_dimension=0, tiled=True)[0]]

    def along(self):
        self.got = [self.got[0]] + [shift_z(v, k) for k, v in enumerate(self.got) if k]

    def total(self):
        return sum(v.astype(f32) for v in self.got)


def gather_small(v):
    x, c, y, z, depth = place()
    pieces = [v] + [shift_z(v, k) for k in range(1, depth)]
    stack = jnp.zeros((depth,) + v.shape, v.dtype)
    for k in range(depth):
        stack = lax.dynamic_update_slice(stack, pieces[k][None], ((z - k) % depth, 0, 0))
    other = swap_x(stack)
    pair = jnp.stack([jnp.where(x == 0, stack, other), jnp.where(x == 0, other, stack)], axis=1)
    other = swap_y(pair)
    quad = jnp.stack([jnp.where(y == 0, pair, other), jnp.where(y == 0, other, pair)], axis=1)
    return quad.reshape((4 * depth,) + v.shape)


def finish(place_of, small, features, wide, rows, ff_rows):
    chips = small.shape[0]
    te_rows = features.shape[0]
    blocks = wide // 128
    starts = [0, blocks, 3 * blocks // 2, 2 * blocks, 5 * blocks // 2 + 1]
    sizes = [2 * rows, rows, rows, rows, ff_rows]

    def kernel(where, small, features, time_out, *refs):
        outs, loss_out, sums = refs[:5], refs[5], refs[6]
        sums[...] = jnp.sum(small[...], axis=0)
        for n in range(blocks):
            total = features[:, :1] * small[0, n : n + 1]
            for k in range(1, chips):
                total += features[:, k : k + 1] * small[k, n : n + 1]
            time_out[:, n * 128 : (n + 1) * 128] = total
        for start, size, out, at in zip(starts, sizes, outs, (0, 0, 0, 0, 1)):
            first = where[at] * size
            row = sums[pl.ds(start + first // 128, 1)]
            out[...] = pltpu.roll(row, lax.rem(128 - lax.rem(first, 128), 128), 1)[:, :size]
        loss_out[...] = sums[5 * blocks // 2 : 5 * blocks // 2 + 1, :1]

    near = pl.BlockSpec(memory_space=pltpu.VMEM)
    lines = [jax.ShapeDtypeStruct((1, n), f32) for n in sizes + [1]]
    made = pl.pallas_call(
        kernel,
        in_specs=[pl.BlockSpec(memory_space=pltpu.SMEM), near, near],
        out_specs=[near] * 7,
        out_shape=[jax.ShapeDtypeStruct((te_rows, wide), f32)] + lines,
        scratch_shapes=[pltpu.VMEM(small.shape[1:], f32)],
        cost_estimate=little,
        name="finish",
    )(place_of, small, features)
    return [made[0]] + [v.reshape(-1) for v in made[1:]]


def project_kernel(source, scale, shift, weight, hidden_out, project_out):
    v = source[...].astype(f32)
    centre = v - jnp.mean(v, axis=1, keepdims=True)
    rate = lax.rsqrt(jnp.mean(centre * centre, axis=1, keepdims=True) + epsilon)
    hidden = (centre * rate * scale[...] + shift[...]).astype(b16)
    hidden_out[...] = hidden
    project_out[...] = jnp.dot(hidden, weight[...], preferred_element_type=f32)


def project_tokens(source, scale, shift, weight):
    tokens, width = source.shape
    cols = weight.shape[1]
    step = 256
    row = pl.BlockSpec((1, width), lambda i: (0, 0))
    return pl.pallas_call(
        project_kernel,
        grid=(tokens // step,),
        in_specs=[
            pl.BlockSpec((step, width), lambda i: (i, 0)),
            row,
            row,
            pl.BlockSpec((width, cols), lambda i: (0, 0)),
        ],
        out_specs=[
            pl.BlockSpec((step, width), lambda i: (i, 0)),
            pl.BlockSpec((step, cols), lambda i: (i, 0)),
        ],
        out_shape=[
            jax.ShapeDtypeStruct((tokens, width), b16),
            jax.ShapeDtypeStruct((tokens, cols), f32),
        ],
        compiler_params=pltpu.CompilerParams(vmem_limit_bytes=48 << 20),
        cost_estimate=little,
        name="project",
    )(source, scale, shift, weight)


def stats(v):
    mean = jnp.mean(v, axis=-1, keepdims=True)
    centre = v - mean
    rate = lax.rsqrt(jnp.mean(centre * centre, axis=-1, keepdims=True) + epsilon)
    return centre * rate, rate


def norm_back(g, n, rate):
    return (g - jnp.mean(g, -1, keepdims=True) - n * jnp.mean(g * n, -1, keepdims=True)) * rate


def dot(a, b, da, db):
    return lax.dot_general(a, b, (((da,), (db,)), ((), ())), preferred_element_type=f32)


LOG2E = 1.4426950408889634
CHUNK = 512


def nn(a, b):
    return lax.dot_general(a, b, (((1,), (0,)), ((), ())), preferred_element_type=f32)


def nt(a, b):
    return lax.dot_general(a, b, (((1,), (1,)), ((), ())), preferred_element_type=f32)


def lane_halves(v):
    lane = lax.broadcasted_iota(jnp.int32, v.shape, 1)
    zero = jnp.zeros_like(v)
    return jnp.where(lane < HD, v, zero), jnp.where(lane < HD, zero, v)


def turn(v, cosine, sine):
    width = v.shape[1]
    lane = lax.broadcasted_iota(jnp.int32, v.shape, 1)
    swapped = jnp.where(
        lane % HD < HD // 2,
        pltpu.roll(v, width - HD // 2, 1),
        pltpu.roll(v, HD // 2, 1),
    )
    return v * cosine + swapped * sine


def attend_kernel(project_in, cos_in, sin_in, *refs):
    turned_out, mix_out, log_out = refs[-3:]
    cosine = cos_in[...]
    sine = sin_in[...]
    tokens = cosine.shape[0]
    q = turn(project_in[:, :128], cosine, sine).astype(b16)
    k = turn(project_in[:, 128:256], cosine, sine).astype(b16)
    v = project_in[:, 256:].astype(b16)
    turned_out[:, :128] = q
    turned_out[:, 128:256] = k
    turned_out[:, 256:] = v
    keys = lane_halves(k)
    v_turned = v.astype(f32).T.astype(b16)
    for at in range(0, tokens, CHUNK):
        part = q[at : at + CHUNK]
        mixed = []
        for h in range(2):
            scores = nt(keys[h], part) * (0.125 * LOG2E)
            top = jnp.max(scores, axis=0, keepdims=True)
            weight = jnp.exp2(scores - top)
            total = jnp.sum(weight, axis=0, keepdims=True)
            log_out[0, h : h + 1, at : at + CHUNK] = top + jnp.log2(total)
            probs = (weight * (1.0 / total)).astype(b16)
            mixed.append(nn(v_turned[h * HD : (h + 1) * HD], probs))
        mix_out[at : at + CHUNK] = jnp.concatenate(mixed, axis=0).T.astype(b16)


def attend(project, cosine, sine, start, pairs, deps=()):
    tokens = project.shape[0]
    table = pl.BlockSpec((tokens, 128), lambda p: (0, 0))
    return pl.pallas_call(
        attend_kernel,
        grid=(pairs,),
        in_specs=[pl.BlockSpec((tokens, 384), lambda p: (0, start + p)), table, table]
        + unread(deps),
        out_specs=[
            pl.BlockSpec((tokens, 384), lambda p: (0, p)),
            pl.BlockSpec((tokens, 128), lambda p: (0, p)),
            pl.BlockSpec((1, 2, tokens), lambda p: (p, 0, 0)),
        ],
        out_shape=[
            jax.ShapeDtypeStruct((tokens, 384 * pairs), b16),
            jax.ShapeDtypeStruct((tokens, 128 * pairs), b16),
            jax.ShapeDtypeStruct((pairs, 2, tokens), f32),
        ],
        compiler_params=pltpu.CompilerParams(vmem_limit_bytes=48 << 20),
        cost_estimate=little,
        name="attend",
    )(project, cosine, sine, *deps)


def attend_back_kernel(
    turned_in, grad_in, log_in, cos_in, sin_in, *refs
):
    grad_out, dk_sum, dv_sum, dq_turned = refs[-4:]
    q = turned_in[:, :128]
    k = turned_in[:, 128:256]
    tokens = q.shape[0]
    keys = lane_halves(k)
    values = lane_halves(turned_in[:, 256:])
    k_turned = k.astype(f32).T.astype(b16)
    for at in range(0, tokens, CHUNK):
        q_part = q[at : at + CHUNK]
        g_part = grad_in[at : at + CHUNK]
        q_halves = lane_halves(q_part)
        g_halves = lane_halves(g_part)
        for h in range(2):
            scores = nt(keys[h], q_part) * (0.125 * LOG2E)
            full = jnp.exp2(scores - log_in[0, h : h + 1, at : at + CHUNK])
            prob_grad = nt(values[h], g_part)
            product = full * prob_grad
            total = jnp.sum(product, axis=0, keepdims=True)
            score_grad = (product - full * total).astype(b16)
            dv_h = nn(full.astype(b16), g_halves[h])
            dk_h = nn(score_grad, q_halves[h])
            dq_turned[h * HD : (h + 1) * HD, at : at + CHUNK] = nn(
                k_turned[h * HD : (h + 1) * HD], score_grad
            )
            dk = dk_h if h == 0 else dk + dk_h
            dv = dv_h if h == 0 else dv + dv_h
        if at == 0:
            dk_sum[...] = dk
            dv_sum[...] = dv
        else:
            dk_sum[...] += dk
            dv_sum[...] += dv
    cosine = cos_in[...]
    sine = -sin_in[...]
    grad_out[:, :128] = turn(dq_turned[...].T * 0.125, cosine, sine).astype(b16)
    grad_out[:, 128:256] = turn(dk_sum[...] * 0.125, cosine, sine).astype(b16)
    grad_out[:, 256:] = dv_sum[...].astype(b16)


def attend_back(turned, log_total, mixture_grad, cosine, sine, start, grad_start, pairs, deps=()):
    tokens = turned.shape[0]
    table = pl.BlockSpec((tokens, 128), lambda p: (0, 0))
    return pl.pallas_call(
        attend_back_kernel,
        grid=(pairs,),
        in_specs=[
            pl.BlockSpec((tokens, 384), lambda p: (0, start + p)),
            pl.BlockSpec((tokens, 128), lambda p: (0, grad_start + p)),
            pl.BlockSpec((1, 2, tokens), lambda p: (start + p, 0, 0)),
            table,
            table,
        ]
        + unread(deps),
        out_specs=pl.BlockSpec((tokens, 384), lambda p: (0, p)),
        out_shape=jax.ShapeDtypeStruct((tokens, 384 * pairs), b16),
        scratch_shapes=[
            pltpu.VMEM((tokens, 128), f32),
            pltpu.VMEM((tokens, 128), f32),
            pltpu.VMEM((128, tokens), f32),
        ],
        compiler_params=pltpu.CompilerParams(vmem_limit_bytes=48 << 20),
        cost_estimate=little,
        name="attend_back",
    )(turned, mixture_grad, log_total, cosine, sine, *deps)


def prepare_kernel(
    where, steps, bias_time, gain, shift, bias_up, bias_down, mask, qkv, up, out, time,
    own, other, out_low, time_low, lines,
):
    c = where[1]
    rows, width = out.shape
    count = jnp.sum(mask[...].astype(f32), axis=1, keepdims=True)
    count = jnp.sum(count, axis=0, keepdims=True)
    high = jnp.floor(count * (1.0 / 256.0))
    step = steps[where[0]]
    lane = lax.broadcasted_iota(jnp.int32, (1, 128), 1)
    numbers = jnp.where(lane == 0, high, count - 256.0 * high)
    numbers = jnp.where(lane == 2, (step // 32).astype(f32), numbers)
    numbers = jnp.where(lane == 3, lax.rem(step, 32).astype(f32), numbers)
    half = width // 2
    step = 128
    for there, made in ((c, own), (1 - c, other)):
        lines[...] = jnp.zeros((rows, 128), f32)
        for n, v in enumerate((bias_time, gain, shift, bias_up, bias_down)):
            lines[n : n + 1, : v.shape[1]] = v[...]
        lines[5:6] = numbers
        made[:, :128] = lines[...].astype(b16)
        for p in range(half // 128):
            for n in range(3):
                at = pl.multiple_of(n * width + there * half + p * 128, 128)
                to = 128 + (3 * p + n) * 128
                made[:, to : to + 128] = qkv[:, pl.ds(at, 128)].astype(b16)
        to = 128 + 3 * half
        for n in range(up.shape[1] // (2 * step)):
            at = pl.multiple_of((2 * n + there) * step, 128)
            made[:, to + n * step : to + (n + 1) * step] = up[:, pl.ds(at, step)].astype(b16)
    for n in range(2):
        out_low[n * rows : (n + 1) * rows] = out[:, n * half : (n + 1) * half].astype(b16)
    te_rows = time.shape[0]
    folds = 2 * rows // te_rows
    cols = time.shape[1] // folds
    for n in range(0, folds, 2):
        pair = [time[:, (n + i) * cols : (n + i + 1) * cols] for i in range(2)]
        time_low[n * te_rows : (n + 2) * te_rows] = jnp.concatenate(pair, axis=0).astype(b16)


def prepare(where, steps, vectors, mask, qkv, up, out, time):
    rows, width = out.shape
    cols = 128 + 3 * width // 2 + up.shape[1] // 2
    near = pl.BlockSpec(memory_space=pltpu.VMEM)
    return pl.pallas_call(
        prepare_kernel,
        in_specs=[pl.BlockSpec(memory_space=pltpu.SMEM)] * 2 + [near] * 10,
        out_specs=[near] * 4,
        scratch_shapes=[pltpu.VMEM((rows, 128), f32)],
        out_shape=[
            jax.ShapeDtypeStruct((rows, cols), b16),
            jax.ShapeDtypeStruct((rows, cols), b16),
            jax.ShapeDtypeStruct((2 * rows, width // 2), b16),
            jax.ShapeDtypeStruct((2 * rows, time.size // (2 * rows)), b16),
        ],
        cost_estimate=little,
        name="prepare",
    )(where, steps, *[v.reshape(1, -1) for v in vectors], mask, qkv, up, out, time)


def body(
    inputs, teacher, valid_mask, time_steps, qkv_weight, out_weight, up_weight, down_weight,
    time_weight, time_bias, norm_gain, norm_bias, up_bias, down_bias,
):
    x, c, y, z, depth = place()
    chips = 4 * depth
    k_chip = 4 * z + 2 * y + x
    seqs, block, width = inputs.shape
    rows = qkv_weight.shape[0]
    ff_rows = down_weight.shape[0]
    half = width // 2
    tokens = 4 * block
    mine = 2 * block
    ff = up_weight.shape[1] // 2
    pairs = half // 128

    tiled = rows % 32 == 0 and ff_rows % 128 == 0
    where = jnp.stack([x, c, y, z])

    te_rows = time_weight.shape[0]
    te_folds = 2 * rows // te_rows
    cut = 128 + 3 * half
    if tiled:
        own, other, out_low, time_low = prepare(
            where, time_steps, (time_bias, norm_gain, norm_bias, up_bias, down_bias), valid_mask,
            qkv_weight, up_weight, out_weight, time_weight,
        )
    else:

        def own_other(v):
            return [pick(v, i, 2).reshape(rows, -1).astype(b16) for i in (c, 1 - c)]

        def fold(v, n):
            return jnp.concatenate(jnp.split(v.astype(b16), n, axis=1), axis=0)

        count = jnp.sum(valid_mask)
        step = pick(time_steps, x)
        whole_numbers = jnp.stack([count // 256, count % 256, step // 32, step % 32]).astype(f32)
        vector = jnp.concatenate([time_bias, norm_gain, norm_bias, up_bias, down_bias, whole_numbers])
        vector = jnp.pad(vector, (0, 384 - vector.shape[0])).reshape(3, 128)
        vector = jnp.pad(vector.astype(b16), ((0, rows - 3), (0, 0)))
        qkv_cut = qkv_weight.reshape(rows, 3, 2, pairs, 128).transpose(0, 3, 2, 1, 4)
        qkv_own, qkv_other = own_other(qkv_cut.reshape(rows, pairs, 2, 3 * 128))
        up_own, up_other = own_other(up_weight.reshape(rows, -1, 2, ff_rows))
        own = jnp.concatenate([vector, qkv_own, up_own], axis=1)
        other = jnp.concatenate([vector, qkv_other, up_other], axis=1)
        out_low, time_low = fold(out_weight, 2), fold(time_weight, te_folds)
    other = swap_core(other)
    last = own.shape[1]
    if tiled:
        first_half, second_half = pl.ds(0, rows), pl.ds(rows, rows)

        def copies(x, c, y, z):
            made = []
            for source, at in ((0, c), (1, 1 - c)):
                made.append((source, (slice(None), pl.ds(0, cut)), 0, (at, slice(None), pl.ds(0, cut))))
                made.append((source, (slice(None), pl.ds(cut, ff)), 1, (at, slice(None), pl.ds(0, ff))))
            for at, half_rows in enumerate((first_half, second_half)):
                made.append((3, (half_rows,), 0, (at, slice(None), pl.ds(cut, time_low.shape[1]))))
                made.append((2, (half_rows,), 1, (at, slice(None), pl.ds(ff, half))))
            return made

        shapes = [
            jax.ShapeDtypeStruct((2, rows, cut + time_low.shape[1]), b16),
            jax.ShapeDtypeStruct((2, rows, ff + half), b16),
        ]
        piece_1, piece_2 = move(where, [own, other, out_low, time_low], shapes, copies)
        piece_1 = piece_1.reshape(2 * rows, -1)
        piece_2 = piece_2.reshape(2 * rows, -1)
    else:
        chip = jnp.concatenate(
            [jnp.where(c == 0, own, other), jnp.where(c == 0, other, own)], axis=0
        )
        piece_1 = jnp.concatenate([chip[:, :cut], time_low], axis=1)
        piece_2 = jnp.concatenate([chip[:, cut:], out_low], axis=1)
    down_full = lax.all_gather(down_weight.astype(b16), ("z", "y", "x"), axis=0, tiled=True)

    source_far = swap_x(pick(inputs, 1 - x))
    marks = valid_mask.astype(b16)
    target_marks = jnp.concatenate(
        [teacher, jnp.broadcast_to(marks[:, :, None], (seqs, block, 128))], axis=2
    )
    pieces_1 = gather_z(piece_1, tiled)
    stack_1 = stack_z(pieces_1, tiled)
    source_far, stack_1[0] = tie(source_far, stack_1[0])
    piece_2, stack_1[1] = tie(piece_2, stack_1[1])
    pieces_2 = gather_z(piece_2, tiled)
    near_1 = list(gather_near(stack_1))
    near_1[2], near_1[3], pieces_2[1] = tie(near_1[2], near_1[3], pieces_2[1])
    source_far, near_1[0] = tie(source_far, near_1[0])
    source_low = jnp.concatenate([pick(inputs, x), source_far], axis=0)
    source_all = jnp.concatenate([source_low, swap_core(source_low)], axis=0)
    far_1 = list(gather_far(near_1))
    vectors, qkv_full, time_full = assemble(
        near_1, far_1, [0, 128, cut, piece_1.shape[1]], tiled
    )
    qkv_full = qkv_full.reshape(width, 3 * half)
    near_2 = list(gather_near(stack_z(pieces_2, tiled, tuple(far_1))))
    f = 2 * x + c
    blocks = jnp.stack([f, f ^ 2, f ^ 1, f ^ 3])
    positions = (blocks[:, None] * block + jnp.arange(block)[None, :]).reshape(tokens).astype(f32)
    pace = jnp.exp(jnp.arange(HD // 2, dtype=f32) * (-2.0 * math.log(10000.0) / HD))
    angles = positions[:, None] * pace[None, :]
    cosine = jnp.tile(jnp.cos(angles), (1, 4))
    sine = jnp.sin(angles)
    sine = jnp.tile(jnp.concatenate([-sine, sine], axis=1), (1, 2))

    vectors = vectors.reshape(chips, 2, rows, 128).astype(f32)
    packed = vectors[:, :, :3].reshape(chips, 2, 384)
    at = 0

    def take(n):
        nonlocal at
        at += 1 if tiled else n
        return vectors[:, :, at - 1, :n] if tiled else packed[:, :, at - n : at]

    bias_time = take(time_bias.shape[0]).reshape(2 * width)
    gain = take(rows).reshape(width)
    shift = take(rows).reshape(width)
    bias_up = pick(take(ff_rows), c, 1).reshape(ff)
    bias_down = take(rows).reshape(width)
    numbers = take(4)
    valid_total = jnp.sum(numbers[:, :, 0]) * 256.0 + jnp.sum(numbers[:, :, 1])
    steps = numbers[:, 0, 2] * 32.0 + numbers[:, 0, 3]
    token_total = 2 * depth * seqs * tokens
    factor = (token_total * width / 2) / (valid_total * width)

    spread = jnp.exp(jnp.arange(TE // 2, dtype=f32) * (-math.log(10000.0) / (TE // 2)))
    angle = steps[:, None] * spread[None]
    features = jnp.concatenate([jnp.sin(angle), jnp.cos(angle)], axis=1).astype(b16)
    feature_core = pick(pick(features, k_chip).reshape(chips, 2, te_rows), c, 1)
    time_parts = time_full.reshape(chips, te_folds, te_rows, -1).astype(f32)
    part = jnp.sum(feature_core.astype(f32)[:, None, :, None] * time_parts, axis=(0, 2))
    part = part.reshape(-1, 128)
    condition = (part + swap_core(part)).reshape(2, width) + bias_time.reshape(2, width)
    scale = 1.0 + condition[:1]
    hidden, project = project_tokens(source_all, scale, condition[1:], qkv_full)
    near_2[2], near_2[3], project = tie(near_2[2], near_2[3], project)
    far_2 = list(gather_far(near_2))
    ahead = pairs // 2
    turned_a, mixed_a, log_a = attend(project, cosine, sine, 0, ahead)
    turned_b, mixed_b, log_b = attend(project, cosine, sine, ahead, pairs - ahead, (mixed_a,))
    far_2[0], mixed_a, mixed_b = tie(far_2[0], mixed_a, mixed_b)
    target_far, far_2[1] = tie(pick(target_marks, 1 - x), far_2[1])
    target_far = swap_x(target_far)
    up_full, out_half = assemble(near_2, far_2, [0, ff, ff + half], tiled)
    up_full = up_full.reshape(width, ff)
    out_far = swap_core(out_half)
    if tiled:

        def copies(x, c, y, z):
            every = slice(None)
            return [
                (n, (every, pl.ds(h * rows, rows)), 0, (every, at, every, pl.ds(h * half, half)))
                for n, at in ((0, c), (1, 1 - c))
                for h in range(2)
            ]

        shape = jax.ShapeDtypeStruct((chips, 2, rows, width), b16)
        out_full = move(where, [out_half, out_far], [shape], copies)[0]
    else:
        out_both = jnp.stack(
            [jnp.where(c == 0, out_half, out_far), jnp.where(c == 0, out_far, out_half)], axis=1
        ).reshape(chips, 2, 2, rows, half)
        out_full = jnp.concatenate([out_both[:, :, 0], out_both[:, :, 1]], axis=-1)
    out_full = out_full.reshape(width, width)
    mixed = jnp.concatenate([mixed_a, mixed_b], axis=1)
    mixed_far = swap_core(mixed[mine:])
    mixture = jnp.where(
        c == 0,
        jnp.concatenate([mixed[:mine], mixed_far], axis=1),
        jnp.concatenate([mixed_far, mixed[:mine]], axis=1),
    )
    middle = source_low.astype(f32) + dot(mixture, out_full, 1, 0)
    n2, rate2 = stats(middle)
    second = (n2 * gain + shift).astype(b16)
    second_all = jnp.concatenate([second, swap_core(second)], axis=0)
    inner = dot(second_all, up_full, 1, 0) + bias_up
    flat = 0.5 * (1.0 + lax.erf(inner * (2.0**-0.5)))
    active = (inner * flat).astype(b16)
    slope = flat + inner * jnp.exp(-0.5 * inner * inner) * ((2.0 * math.pi) ** -0.5)
    active, target_far = tie(active, target_far)
    down = dot(active, down_full, 1, 0)
    result = middle + (down[:mine] + swap_core(down[mine:].astype(b16)).astype(f32) + bias_down)

    target_marks = jnp.concatenate([pick(target_marks, x), target_far], axis=0)
    target = target_marks[:, :width].astype(f32)
    mark = target_marks[:, width : width + 1].astype(f32)
    differ = result - target
    loss_part = jnp.sum(mark * differ * differ)
    result_grad = 2.0 * mark * differ * factor

    down_in = result_grad.astype(b16)
    down_in_all = jnp.concatenate([down_in, swap_core(down_in)], axis=0)
    near_axes = ("y", "x")
    result_low = result.astype(b16)
    down_term = dot(active, down_in_all, 0, 0).astype(b16)
    down_sum = Scatter(down_term.reshape(chips, -1, width), where, tiled)
    down_in_all, down_sum.got[0] = tie(down_in_all, down_sum.got[0])
    down_sum.near()
    inner_grad = (dot(down_in_all, down_full, 1, 1) * slope).astype(b16)
    second_part = dot(inner_grad, up_full, 1, 1)
    second_send, second_all = tie(second_part[mine:].astype(b16), second_all)
    second_got = swap_core(second_send)
    up_term = dot(second_all, inner_grad, 0, 0).astype(b16)
    up_sum = Scatter(up_term.reshape(chips, -1, ff), where, tiled)
    second_got, up_sum.got[0], *down_sum.got = tie(second_got, up_sum.got[0], *down_sum.got)
    up_sum.near()
    down_sum.add_near()
    second_got, down_sum.got[0] = tie(second_got, down_sum.got[0])
    down_sum.far()
    second_grad = second_part[:mine] + second_got.astype(f32)
    middle_grad = result_grad + norm_back(second_grad * gain, n2, rate2)
    branch = middle_grad.astype(b16)
    mixture_grad = dot(branch, out_full, 1, 1).astype(b16)
    mixture_far, branch = tie(
        lax.dynamic_slice_in_dim(mixture_grad, (1 - c) * half, half, 1), branch
    )
    mixture_far = swap_core(mixture_far)
    out_term = dot(mixture, branch, 0, 0).astype(b16).reshape(chips, 2, rows, width)
    mixture_far, out_send, out_keep = tie(
        mixture_far, pick(out_term, 1 - c, 1), pick(out_term, c, 1)
    )
    out_got = swap_core(out_send)
    mixture_grad = jnp.concatenate(
        [lax.dynamic_slice_in_dim(mixture_grad, c * half, half, 1), mixture_far], axis=0
    )

    def pair_back(p, deps):
        turned, log = (turned_a, log_a) if p < ahead else (turned_b, log_b)
        at = p if p < ahead else p - ahead
        return attend_back(turned, log, mixture_grad, cosine, sine, at, p, 1, deps)

    grads = [pair_back(0, ())]
    grads.append(pair_back(1, (grads[-1],)))
    down_sum.got[0], down_sum.got[1], grads[-1] = tie(down_sum.got[0], down_sum.got[1], grads[-1])
    down_sum.add_far(True)
    grads[-1], down_sum.got[0] = tie(grads[-1], down_sum.got[0])
    down_sum.scatter_along()
    for p in range(2, pairs - 1):
        grads.append(pair_back(p, (grads[-1],)))
    up_sum.got[0], up_sum.got[1], grads[-1] = tie(up_sum.got[0], up_sum.got[1], grads[-1])
    up_sum.add_near()
    grads.append(pair_back(pairs - 1, (grads[-1], up_sum.keep[0])))
    up_sum.far()
    project_grad = jnp.concatenate(grads, axis=1)
    qkv_term = dot(hidden, project_grad, 0, 0).astype(b16).reshape(chips, 2 * rows, -1)
    qkv_cols = qkv_term.shape[2]
    out_term = add_low(out_keep, out_got)
    out_term = jnp.concatenate([out_term[:, :, :half], out_term[:, :, half:]], axis=1)
    last_sum = Scatter(jnp.concatenate([qkv_term, out_term], axis=2), where, tiled)
    project_grad, last_sum.got[0] = tie(project_grad, last_sum.got[0])
    last_sum.near()
    hidden_part = dot(project_grad, qkv_full, 1, 1)
    hidden_got, hidden_keep, *up_sum.got = tie(
        hidden_part[mine:].astype(b16), hidden_part[:mine], *up_sum.got
    )
    hidden_got = swap_core(hidden_got)
    up_sum.add_far(True)
    up_sum.got[0], hidden_got = tie(up_sum.got[0], hidden_got)
    up_sum.scatter_along()
    hidden_grad = hidden_keep + hidden_got.astype(f32)
    n1, rate1 = stats(source_low.astype(f32))
    input_grad = middle_grad + norm_back(hidden_grad * scale, n1, rate1)

    small = jnp.concatenate(
        [
            jnp.sum(hidden_grad * n1, 0),
            jnp.sum(hidden_grad, 0),
            jnp.sum(second_grad * n2, 0),
            jnp.sum(second_grad, 0),
            jnp.sum(down_in.astype(f32), 0),
            jnp.full((128,), loss_part),
        ]
    )
    small = small.reshape(-1, 128)
    small_got = swap_core(small)
    last_sum.got[0], input_grad = tie(last_sum.got[0], input_grad)
    last_sum.add_near()
    small_got, input_grad, last_sum.got[0] = tie(small_got, input_grad, last_sum.got[0])
    last_sum.far()
    small = small + small_got
    up_bias_part = jnp.sum(inner_grad.astype(f32), 0).reshape(-1, 128)
    fill = jnp.zeros((-(small.shape[0] + up_bias_part.shape[0]) % 8, 128), f32)
    small = jnp.concatenate([small, up_bias_part, fill], axis=0)
    small = gather_small(small)
    up_sum = up_sum.total()
    last_sum.add_far()
    input_far, result_far, last_sum.got[1] = tie(
        input_grad[block:].astype(b16), result_low[block:], last_sum.got[1]
    )
    last_sum.along()
    input_far = swap_x(input_far).astype(f32)
    result_far = swap_x(result_far)

    def spread_out(near, far):
        return jnp.stack([jnp.where(x == 0, near, far), jnp.where(x == 0, far, near)])

    activations = spread_out(result_low[:block], result_far)
    input_grad = spread_out(input_grad[:block], input_far)
    down_sum = down_sum.total()
    index = 2 * k_chip + c
    feature_rows = lax.dynamic_slice_in_dim(features, index * te_rows, te_rows, 1).astype(f32)
    time_sum, time_bias_sum, gain_sum, shift_sum, down_bias_sum, up_bias_sum, loss_sum = finish(
        jnp.stack([index, k_chip]), small, feature_rows.T, 2 * width, rows, ff_rows
    )
    loss = (loss_sum[0] / (valid_total * width)).reshape(1)

    def columns(total, inner_size):
        total = total.reshape(2, rows, -1, inner_size)
        near = pick(total, c)
        far = swap_core(pick(total, 1 - c))
        return jnp.stack(
            [jnp.where(c == 0, near, far), jnp.where(c == 0, far, near)], axis=2
        ).reshape(rows, -1)

    up_sum = columns(up_sum, ff_rows)
    others = (activations, input_grad, up_sum, down_sum, time_sum, loss)
    tied = tie(*last_sum.got, *others)
    last_sum.got = tied[: -len(others)]
    activations, input_grad, up_sum, down_sum, time_sum, loss = tied[-len(others) :]
    last_sum = last_sum.total()
    out_sum = last_sum[:, qkv_cols:]
    out_sum = jnp.concatenate([out_sum[:rows], out_sum[rows:]], axis=1)
    qkv_sum = last_sum[:, :qkv_cols].reshape(2 * rows, pairs, 3, 128)
    qkv_sum = qkv_sum.transpose(0, 2, 1, 3).reshape(2 * rows, -1)
    return (
        activations,
        loss,
        input_grad,
        columns(qkv_sum, half),
        out_sum,
        up_sum,
        down_sum,
        time_sum,
        time_bias_sum,
        gain_sum,
        shift_sum,
        up_bias_sum,
        down_bias_sum,
    )


def solution(mesh):
    split = mesh.devices.reshape(-1, 2, 2, 2)
    finer = jax.sharding.Mesh(split, ("z", "y", "x", "core"))
    both = ("z", "y", "x", "core")
    tokens = P(("z", "y"), ("x", "core"), None)
    weight = P(both, None)
    vector = P(both)
    return jax.shard_map(
        body,
        mesh=finer,
        in_specs=(tokens, tokens, P(("z", "y"), ("x", "core")), P(("z", "y"))) + (weight,) * 5 + (vector,) * 5,
        out_specs=(tokens, P(), tokens) + (weight,) * 5 + (vector,) * 5,
        check_vma=False,
    )
```

```python
import math

import jax
import jax.numpy as jnp
from jax import lax
from jax.experimental import pallas as pl
from jax.experimental.pallas import tpu as pltpu
from jax.sharding import PartitionSpec as P

HD = 64
TE = 256

b16 = jnp.bfloat16
f32 = jnp.float32
highest = lax.Precision.HIGHEST
epsilon = 1e-05
little = pl.CostEstimate(flops=1, transcendentals=0, bytes_accessed=1)


def swap_core(v):
    return lax.ppermute(v, "core", [(0, 1), (1, 0)])


def swap_x(v):
    return lax.ppermute(v, "x", [(0, 1), (1, 0)])


def swap_y(v):
    return lax.ppermute(v, "y", [(0, 1), (1, 0)])


def shift_z(v, k):
    depth = lax.axis_size("z")
    return lax.ppermute(v, "z", [(i, (i + k) % depth) for i in range(depth)])


def place():
    return tuple(lax.axis_index(a) for a in ("x", "core", "y", "z")) + (lax.axis_size("z"),)


def pick(v, index, axis=0):
    return lax.dynamic_index_in_dim(v, index, axis, False)


def unread(deps):
    return [pl.BlockSpec(memory_space=pl.ANY)] * len(deps)


def move(place_of, sources, outs, copies, deps=()):
    def kernel(where, *refs):
        x, c, y, z = (where[i] for i in range(4))
        given = refs[: len(sources)]
        made = refs[len(sources) + len(deps) :]
        for source, read, out, write in copies(x, c, y, z):
            made[out][write] = given[source][read]

    near = pl.BlockSpec(memory_space=pltpu.VMEM)
    return pl.pallas_call(
        kernel,
        in_specs=[pl.BlockSpec(memory_space=pltpu.SMEM)] + [near] * len(sources) + unread(deps),
        out_specs=[near] * len(outs),
        out_shape=outs,
        compiler_params=pltpu.CompilerParams(vmem_limit_bytes=32 << 20),
        cost_estimate=little,
        name="move",
    )(place_of, *sources, *deps)


def tie(*values):
    return lax.optimization_barrier(values)


def gather_z(piece, tiled=False):
    return [piece] + [shift_z(piece, k) for k in range(1, place()[4])]


def stack_z(pieces, tiled=False, deps=()):
    x, c, y, z, depth = place()
    rows, cols = pieces[0].shape
    half = rows // 2
    if tiled:

        def copies(x, c, y, z):
            return [
                (k, pl.ds(h * half, half), h, lax.rem(z - k + depth, depth))
                for k in range(depth)
                for h in range(2)
            ]

        shape = jax.ShapeDtypeStruct((depth, half, cols), b16)
        return list(move(jnp.stack([x, c, y, z]), pieces, [shape, shape], copies, deps))
    stack = jnp.zeros((depth, rows, cols), b16)
    for k in range(depth):
        stack = lax.dynamic_update_slice(stack, pieces[k][None], ((z - k) % depth, 0, 0))
    return [stack[:, :half], stack[:, half:]]


def gather_near(stacks):
    top, low = stacks
    return top, low, swap_x(top), swap_y(low)


def gather_far(near):
    top, low, top_x, low_y = near
    return swap_y(jnp.stack([top, top_x])), swap_x(jnp.stack([low, low_y]))


def assemble(near, far, cuts, tiled=False):
    x, c, y, z, depth = place()
    top, low, top_x, low_y = near
    top_far, low_far = far
    half, cols = top.shape[1:]
    rows = 2 * half
    if tiled:
        every = slice(None)

        def copies(x, c, y, z):
            made = []
            for n in range(len(cuts) - 1):
                run = pl.ds(cuts[n], cuts[n + 1] - cuts[n])
                one = (every, every, run)
                up, down = pl.ds(0, half), pl.ds(half, half)
                made += [
                    (0, one, n, (every, y, x, up)),
                    (2, one, n, (every, y, 1 - x, up)),
                    (4, (0,) + one, n, (every, 1 - y, x, up)),
                    (4, (1,) + one, n, (every, 1 - y, 1 - x, up)),
                    (1, one, n, (every, y, x, down)),
                    (3, one, n, (every, 1 - y, x, down)),
                    (5, (0,) + one, n, (every, y, 1 - x, down)),
                    (5, (1,) + one, n, (every, 1 - y, 1 - x, down)),
                ]
            return made

        shapes = [
            jax.ShapeDtypeStruct((depth, 2, 2, rows, cuts[n + 1] - cuts[n]), top.dtype)
            for n in range(len(cuts) - 1)
        ]
        parts = move(
            jnp.stack([x, c, y, z]), [top, low, top_x, low_y, top_far, low_far], shapes, copies
        )
        return [p.reshape(4 * depth, rows, -1) for p in parts]
    whole = jnp.zeros((depth, 2, 2, rows, cols), top.dtype)

    def put(whole, part, yy, xx, at):
        return lax.dynamic_update_slice(whole, part[:, None, None], (0, yy, xx, at, 0))

    whole = put(whole, top, y, x, 0)
    whole = put(whole, top_x, y, 1 - x, 0)
    whole = put(whole, top_far[0], 1 - y, x, 0)
    whole = put(whole, top_far[1], 1 - y, 1 - x, 0)
    whole = put(whole, low, y, x, half)
    whole = put(whole, low_y, 1 - y, x, half)
    whole = put(whole, low_far[0], y, 1 - x, half)
    whole = put(whole, low_far[1], 1 - y, 1 - x, half)
    whole = whole.reshape(4 * depth, rows, cols)
    return [whole[:, :, cuts[n] : cuts[n + 1]] for n in range(len(cuts) - 1)]


def add_low(a, b):
    return (a.astype(f32) + b.astype(f32)).astype(a.dtype)


def exchange(v, axes):
    return lax.all_to_all(v, axes, 0, 0, tiled=True)


def add_up(v):
    total = v[0].astype(f32)
    for i in range(1, len(v)):
        total = total + v[i].astype(f32)
    return total


def add_near(got, where, tiled):
    depth = got.shape[1]
    if not tiled:
        z = lax.axis_index("z")
        both = add_up(got).astype(b16)
        return [pick(both, (z + k) % depth) for k in range(depth)]

    def kernel(where, got, *outs):
        for k in range(depth):
            at = lax.rem(where[3] + k, depth)
            total = got[0, at].astype(f32)
            for i in range(1, got.shape[0]):
                total = total + got[i, at].astype(f32)
            outs[k][...] = total.astype(b16)

    near = pl.BlockSpec(memory_space=pltpu.VMEM)
    return pl.pallas_call(
        kernel,
        in_specs=[pl.BlockSpec(memory_space=pltpu.SMEM), near],
        out_specs=[near] * depth,
        out_shape=[jax.ShapeDtypeStruct(got.shape[2:], b16)] * depth,
        compiler_params=pltpu.CompilerParams(vmem_limit_bytes=32 << 20),
        cost_estimate=little,
        name="add_near",
    )(where, got)


def stack_terms(first, second):
    chips, top, width = first.shape
    rows, runs = second.shape[1], second.shape[2] // width
    shape = (chips, top + runs * rows, width)
    if top % 16 or rows % 16:
        return jnp.concatenate([first] + jnp.split(second, runs, axis=2), axis=1)

    def kernel(first, second, made):
        made[:, :top] = first[...]
        for n in range(runs):
            made[:, top + n * rows : top + (n + 1) * rows] = second[
                :, :, n * width : (n + 1) * width
            ]

    near = pl.BlockSpec(memory_space=pltpu.VMEM)
    return pl.pallas_call(
        kernel,
        in_specs=[near, near],
        out_specs=near,
        out_shape=jax.ShapeDtypeStruct(shape, first.dtype),
        compiler_params=pltpu.CompilerParams(vmem_limit_bytes=40 << 20),
        cost_estimate=little,
        name="stack_terms",
    )(first, second)


def send_z(parts):
    return [parts[0]] + [shift_z(v, k) for k, v in enumerate(parts) if k]


def regroup(v, cuts):
    runs = [slice(cuts[n], cuts[n + 1]) for n in range(len(cuts) - 1)]
    if v.shape[2] % 16 or v.shape[3] % 128:
        return [jnp.swapaxes(v[..., run], 0, 1) for run in runs]

    def kernel(given, *made):
        for out, run in zip(made, runs):
            for i in range(v.shape[0]):
                for j in range(v.shape[1]):
                    out[j, i] = given[i, j, :, run]

    near = pl.BlockSpec(memory_space=pltpu.VMEM)
    return pl.pallas_call(
        kernel,
        in_specs=[near],
        out_specs=[near] * len(runs),
        out_shape=[
            jax.ShapeDtypeStruct((v.shape[1], v.shape[0], v.shape[2], r.stop - r.start), v.dtype)
            for r in runs
        ],
        compiler_params=pltpu.CompilerParams(vmem_limit_bytes=32 << 20),
        cost_estimate=little,
        name="regroup",
    )(v)


def swap_order(v):
    return regroup(v, [0, v.shape[3]])[0]


def scatter_send(parts, where, tiled, deps=()):
    x, c, y, z, depth = place()
    chips, rows, cols = parts.shape
    half = rows // 2
    if not tiled:
        grid = parts.reshape(depth, 2, 2, rows, cols)
        return [pick(grid[:, :, :, :half], 1 - x, 2), pick(grid[:, :, :, half:], 1 - y, 1)]

    def copies(x, c, y, z):
        return [
            (0, (slice(None), slice(None), 1 - x, 0), 0, slice(None)),
            (0, (slice(None), 1 - y, slice(None), 1), 1, slice(None)),
        ]

    shape = jax.ShapeDtypeStruct((depth, 2, half, cols), parts.dtype)
    grid = parts.reshape(depth, 2, 2, 2, half, cols)
    return list(move(where, [grid], [shape, shape], copies, deps))


def scatter_near(parts, got, where, tiled):
    x, c, y, z, depth = place()
    chips, rows, cols = parts.shape
    half = rows // 2
    if not tiled:
        grid = parts.reshape(depth, 2, 2, rows, cols)
        top = add_low(pick(grid[:, :, :, :half], x, 2), got[0])
        low = add_low(pick(grid[:, :, :, half:], y, 1), got[1])
        return pick(top, y, 1), pick(top, 1 - y, 1), pick(low, x, 1), pick(low, 1 - x, 1)

    def kernel(where, grid, top, low, keep_t, send_t, keep_l, send_l):
        x, y = where[0], where[2]
        for out, yy in ((keep_t, y), (send_t, 1 - y)):
            out[...] = add_low(grid[:, yy, x, 0], top[:, yy])
        for out, xx in ((keep_l, x), (send_l, 1 - x)):
            out[...] = add_low(grid[:, y, xx, 1], low[:, xx])

    near = pl.BlockSpec(memory_space=pltpu.VMEM)
    shape = jax.ShapeDtypeStruct((depth, half, cols), parts.dtype)
    return pl.pallas_call(
        kernel,
        in_specs=[pl.BlockSpec(memory_space=pltpu.SMEM)] + [near] * 3,
        out_specs=[near] * 4,
        out_shape=[shape] * 4,
        compiler_params=pltpu.CompilerParams(vmem_limit_bytes=32 << 20),
        cost_estimate=little,
        name="scatter_near",
    )(where, parts.reshape(depth, 2, 2, 2, half, cols), got[0], got[1])


def scatter_far(keep, got, where, tiled, ordered=False):
    x, c, y, z, depth = place()
    half, cols = keep[0].shape[1:]
    if not tiled:
        both = jnp.concatenate([add_low(k, g) for k, g in zip(keep, got)], axis=1)
        return [both] if ordered else [pick(both, (z + k) % depth) for k in range(depth)]

    def kernel(where, top, low, top_got, low_got, *outs):
        if ordered:
            outs[0][:, :half] = add_low(top[...], top_got[...])
            outs[0][:, half:] = add_low(low[...], low_got[...])
            return
        for k in range(depth):
            at = lax.rem(where[3] + k, depth)
            outs[k][:half] = add_low(top[at], top_got[at])
            outs[k][half:] = add_low(low[at], low_got[at])

    near = pl.BlockSpec(memory_space=pltpu.VMEM)
    shape = jax.ShapeDtypeStruct(((depth,) if ordered else ()) + (2 * half, cols), keep[0].dtype)
    count = 1 if ordered else depth
    return pl.pallas_call(
        kernel,
        in_specs=[pl.BlockSpec(memory_space=pltpu.SMEM)] + [near] * 4,
        out_specs=[near] * count,
        out_shape=[shape] * count,
        compiler_params=pltpu.CompilerParams(vmem_limit_bytes=32 << 20),
        cost_estimate=little,
        name="scatter_far",
    )(where, keep[0], keep[1], got[0], got[1])


class Scatter:
    def __init__(self, parts, where, tiled, deps=()):
        self.parts, self.where, self.tiled = parts, where, tiled
        self.got = scatter_send(parts, where, tiled, deps)

    def near(self):
        top, low = self.got
        self.got = [swap_x(top), swap_y(low)]

    def add_near(self):
        keep_t, send_t, keep_l, send_l = scatter_near(self.parts, self.got, self.where, self.tiled)
        self.keep, self.got = [keep_t, keep_l], [send_t, send_l]

    def far(self):
        self.got = [swap_y(self.got[0]), swap_x(self.got[1])]

    def add_far(self, ordered=False):
        self.got = list(scatter_far(self.keep, self.got, self.where, self.tiled, ordered))

    def scatter_along(self):
        self.got = [lax.psum_scatter(self.got[0], "z", scatter_dimension=0, tiled=True)[0]]

    def along(self):
        self.got = [self.got[0]] + [shift_z(v, k) for k, v in enumerate(self.got) if k]

    def total(self):
        return sum(v.astype(f32) for v in self.got)


def gather_small(v):
    x, c, y, z, depth = place()
    pieces = [v] + [shift_z(v, k) for k in range(1, depth)]
    stack = jnp.zeros((depth,) + v.shape, v.dtype)
    for k in range(depth):
        stack = lax.dynamic_update_slice(stack, pieces[k][None], ((z - k) % depth, 0, 0))
    other = swap_x(stack)
    pair = jnp.stack([jnp.where(x == 0, stack, other), jnp.where(x == 0, other, stack)], axis=1)
    other = swap_y(pair)
    quad = jnp.stack([jnp.where(y == 0, pair, other), jnp.where(y == 0, other, pair)], axis=1)
    return quad.reshape((4 * depth,) + v.shape)


def finish(place_of, small, features, wide, rows, ff_rows):
    chips = small.shape[0]
    te_rows = features.shape[0]
    blocks = wide // 128
    starts = [0, blocks, 3 * blocks // 2, 2 * blocks, 5 * blocks // 2 + 1]
    sizes = [2 * rows, rows, rows, rows, ff_rows]

    def kernel(where, small, features, time_out, *refs):
        outs, loss_out, sums = refs[:5], refs[5], refs[6]
        sums[...] = jnp.sum(small[...], axis=0)
        for n in range(blocks):
            total = features[:, :1] * small[0, n : n + 1]
            for k in range(1, chips):
                total += features[:, k : k + 1] * small[k, n : n + 1]
            time_out[:, n * 128 : (n + 1) * 128] = total
        for start, size, out, at in zip(starts, sizes, outs, (0, 0, 0, 0, 1)):
            first = where[at] * size
            row = sums[pl.ds(start + first // 128, 1)]
            out[...] = pltpu.roll(row, lax.rem(128 - lax.rem(first, 128), 128), 1)[:, :size]
        loss_out[...] = sums[5 * blocks // 2 : 5 * blocks // 2 + 1, :1]

    near = pl.BlockSpec(memory_space=pltpu.VMEM)
    lines = [jax.ShapeDtypeStruct((1, n), f32) for n in sizes + [1]]
    made = pl.pallas_call(
        kernel,
        in_specs=[pl.BlockSpec(memory_space=pltpu.SMEM), near, near],
        out_specs=[near] * 7,
        out_shape=[jax.ShapeDtypeStruct((te_rows, wide), f32)] + lines,
        scratch_shapes=[pltpu.VMEM(small.shape[1:], f32)],
        cost_estimate=little,
        name="finish",
    )(place_of, small, features)
    return [made[0]] + [v.reshape(-1) for v in made[1:]]


def project_kernel(source, scale, shift, weight, hidden_out, project_out):
    v = source[...].astype(f32)
    centre = v - jnp.mean(v, axis=1, keepdims=True)
    rate = lax.rsqrt(jnp.mean(centre * centre, axis=1, keepdims=True) + epsilon)
    hidden = (centre * rate * scale[...] + shift[...]).astype(b16)
    hidden_out[...] = hidden
    project_out[...] = jnp.dot(hidden, weight[...], preferred_element_type=f32)


def project_tokens(source, scale, shift, weight):
    tokens, width = source.shape
    cols = weight.shape[1]
    step = 256
    row = pl.BlockSpec((1, width), lambda i: (0, 0))
    return pl.pallas_call(
        project_kernel,
        grid=(tokens // step,),
        in_specs=[
            pl.BlockSpec((step, width), lambda i: (i, 0)),
            row,
            row,
            pl.BlockSpec((width, cols), lambda i: (0, 0)),
        ],
        out_specs=[
            pl.BlockSpec((step, width), lambda i: (i, 0)),
            pl.BlockSpec((step, cols), lambda i: (i, 0)),
        ],
        out_shape=[
            jax.ShapeDtypeStruct((tokens, width), b16),
            jax.ShapeDtypeStruct((tokens, cols), f32),
        ],
        compiler_params=pltpu.CompilerParams(vmem_limit_bytes=48 << 20),
        cost_estimate=little,
        name="project",
    )(source, scale, shift, weight)


def stats(v):
    mean = jnp.mean(v, axis=-1, keepdims=True)
    centre = v - mean
    rate = lax.rsqrt(jnp.mean(centre * centre, axis=-1, keepdims=True) + epsilon)
    return centre * rate, rate


def norm_back(g, n, rate):
    return (g - jnp.mean(g, -1, keepdims=True) - n * jnp.mean(g * n, -1, keepdims=True)) * rate


def dot(a, b, da, db):
    return lax.dot_general(a, b, (((da,), (db,)), ((), ())), preferred_element_type=f32)


LOG2E = 1.4426950408889634
CHUNK = 512


def nn(a, b):
    return lax.dot_general(a, b, (((1,), (0,)), ((), ())), preferred_element_type=f32)


def nt(a, b):
    return lax.dot_general(a, b, (((1,), (1,)), ((), ())), preferred_element_type=f32)


def lane_halves(v):
    lane = lax.broadcasted_iota(jnp.int32, v.shape, 1)
    zero = jnp.zeros_like(v)
    return jnp.where(lane < HD, v, zero), jnp.where(lane < HD, zero, v)


def turn(v, cosine, sine):
    width = v.shape[1]
    lane = lax.broadcasted_iota(jnp.int32, v.shape, 1)
    swapped = jnp.where(
        lane % HD < HD // 2,
        pltpu.roll(v, width - HD // 2, 1),
        pltpu.roll(v, HD // 2, 1),
    )
    return v * cosine + swapped * sine


def attend_kernel(project_in, cos_in, sin_in, *refs):
    turned_out, mix_out, log_out = refs[-3:]
    cosine = cos_in[...]
    sine = sin_in[...]
    tokens = cosine.shape[0]
    q = turn(project_in[:, :128], cosine, sine).astype(b16)
    k = turn(project_in[:, 128:256], cosine, sine).astype(b16)
    v = project_in[:, 256:].astype(b16)
    turned_out[:, :128] = q
    turned_out[:, 128:256] = k
    turned_out[:, 256:] = v
    keys = lane_halves(k)
    v_turned = v.astype(f32).T.astype(b16)
    for at in range(0, tokens, CHUNK):
        part = q[at : at + CHUNK]
        mixed = []
        for h in range(2):
            scores = nt(keys[h], part) * (0.125 * LOG2E)
            top = jnp.max(scores, axis=0, keepdims=True)
            weight = jnp.exp2(scores - top)
            total = jnp.sum(weight, axis=0, keepdims=True)
            log_out[0, h : h + 1, at : at + CHUNK] = top + jnp.log2(total)
            probs = (weight * (1.0 / total)).astype(b16)
            mixed.append(nn(v_turned[h * HD : (h + 1) * HD], probs))
        mix_out[at : at + CHUNK] = jnp.concatenate(mixed, axis=0).T.astype(b16)


def attend(project, cosine, sine, start, pairs, deps=()):
    tokens = project.shape[0]
    table = pl.BlockSpec((tokens, 128), lambda p: (0, 0))
    return pl.pallas_call(
        attend_kernel,
        grid=(pairs,),
        in_specs=[pl.BlockSpec((tokens, 384), lambda p: (0, start + p)), table, table]
        + unread(deps),
        out_specs=[
            pl.BlockSpec((tokens, 384), lambda p: (0, p)),
            pl.BlockSpec((tokens, 128), lambda p: (0, p)),
            pl.BlockSpec((1, 2, tokens), lambda p: (p, 0, 0)),
        ],
        out_shape=[
            jax.ShapeDtypeStruct((tokens, 384 * pairs), b16),
            jax.ShapeDtypeStruct((tokens, 128 * pairs), b16),
            jax.ShapeDtypeStruct((pairs, 2, tokens), f32),
        ],
        compiler_params=pltpu.CompilerParams(vmem_limit_bytes=48 << 20),
        cost_estimate=little,
        name="attend",
    )(project, cosine, sine, *deps)


def attend_back_kernel(
    turned_in, grad_in, log_in, cos_in, sin_in, *refs
):
    grad_out, dk_sum, dv_sum, dq_turned = refs[-4:]
    q = turned_in[:, :128]
    k = turned_in[:, 128:256]
    tokens = q.shape[0]
    keys = lane_halves(k)
    values = lane_halves(turned_in[:, 256:])
    k_turned = k.astype(f32).T.astype(b16)
    for at in range(0, tokens, CHUNK):
        q_part = q[at : at + CHUNK]
        g_part = grad_in[at : at + CHUNK]
        q_halves = lane_halves(q_part)
        g_halves = lane_halves(g_part)
        for h in range(2):
            scores = nt(keys[h], q_part) * (0.125 * LOG2E)
            full = jnp.exp2(scores - log_in[0, h : h + 1, at : at + CHUNK])
            prob_grad = nt(values[h], g_part)
            product = full * prob_grad
            total = jnp.sum(product, axis=0, keepdims=True)
            score_grad = (product - full * total).astype(b16)
            dv_h = nn(full.astype(b16), g_halves[h])
            dk_h = nn(score_grad, q_halves[h])
            dq_turned[h * HD : (h + 1) * HD, at : at + CHUNK] = nn(
                k_turned[h * HD : (h + 1) * HD], score_grad
            )
            dk = dk_h if h == 0 else dk + dk_h
            dv = dv_h if h == 0 else dv + dv_h
        if at == 0:
            dk_sum[...] = dk
            dv_sum[...] = dv
        else:
            dk_sum[...] += dk
            dv_sum[...] += dv
    cosine = cos_in[...]
    sine = -sin_in[...]
    grad_out[:, :128] = turn(dq_turned[...].T * 0.125, cosine, sine).astype(b16)
    grad_out[:, 128:256] = turn(dk_sum[...] * 0.125, cosine, sine).astype(b16)
    grad_out[:, 256:] = dv_sum[...].astype(b16)


def attend_back(turned, log_total, mixture_grad, cosine, sine, start, grad_start, pairs, deps=()):
    tokens = turned.shape[0]
    table = pl.BlockSpec((tokens, 128), lambda p: (0, 0))
    return pl.pallas_call(
        attend_back_kernel,
        grid=(pairs,),
        in_specs=[
            pl.BlockSpec((tokens, 384), lambda p: (0, start + p)),
            pl.BlockSpec((tokens, 128), lambda p: (0, grad_start + p)),
            pl.BlockSpec((1, 2, tokens), lambda p: (start + p, 0, 0)),
            table,
            table,
        ]
        + unread(deps),
        out_specs=pl.BlockSpec((tokens, 384), lambda p: (0, p)),
        out_shape=jax.ShapeDtypeStruct((tokens, 384 * pairs), b16),
        scratch_shapes=[
            pltpu.VMEM((tokens, 128), f32),
            pltpu.VMEM((tokens, 128), f32),
            pltpu.VMEM((128, tokens), f32),
        ],
        compiler_params=pltpu.CompilerParams(vmem_limit_bytes=48 << 20),
        cost_estimate=little,
        name="attend_back",
    )(turned, mixture_grad, log_total, cosine, sine, *deps)


def prepare_kernel(
    where, steps, bias_time, gain, shift, bias_up, bias_down, mask, qkv, up, out, time,
    own, other, out_low, time_low, lines,
):
    c = where[1]
    rows, width = out.shape
    count = jnp.sum(mask[...].astype(f32), axis=1, keepdims=True)
    count = jnp.sum(count, axis=0, keepdims=True)
    high = jnp.floor(count * (1.0 / 256.0))
    step = steps[where[0]]
    lane = lax.broadcasted_iota(jnp.int32, (1, 128), 1)
    numbers = jnp.where(lane == 0, high, count - 256.0 * high)
    numbers = jnp.where(lane == 2, (step // 32).astype(f32), numbers)
    numbers = jnp.where(lane == 3, lax.rem(step, 32).astype(f32), numbers)
    half = width // 2
    step = 128
    for there, made in ((c, own), (1 - c, other)):
        lines[...] = jnp.zeros((rows, 128), f32)
        for n, v in enumerate((bias_time, gain, shift, bias_up, bias_down)):
            lines[n : n + 1, : v.shape[1]] = v[...]
        lines[5:6] = numbers
        made[:, :128] = lines[...].astype(b16)
        for p in range(half // 128):
            for n in range(3):
                at = pl.multiple_of(n * width + there * half + p * 128, 128)
                to = 128 + (3 * p + n) * 128
                made[:, to : to + 128] = qkv[:, pl.ds(at, 128)].astype(b16)
        to = 128 + 3 * half
        for n in range(up.shape[1] // (2 * step)):
            at = pl.multiple_of((2 * n + there) * step, 128)
            made[:, to + n * step : to + (n + 1) * step] = up[:, pl.ds(at, step)].astype(b16)
    for n in range(2):
        out_low[n * rows : (n + 1) * rows] = out[:, n * half : (n + 1) * half].astype(b16)
    te_rows = time.shape[0]
    folds = 2 * rows // te_rows
    cols = time.shape[1] // folds
    for n in range(0, folds, 2):
        pair = [time[:, (n + i) * cols : (n + i + 1) * cols] for i in range(2)]
        time_low[n * te_rows : (n + 2) * te_rows] = jnp.concatenate(pair, axis=0).astype(b16)


def prepare(where, steps, vectors, mask, qkv, up, out, time):
    rows, width = out.shape
    cols = 128 + 3 * width // 2 + up.shape[1] // 2
    near = pl.BlockSpec(memory_space=pltpu.VMEM)
    return pl.pallas_call(
        prepare_kernel,
        in_specs=[pl.BlockSpec(memory_space=pltpu.SMEM)] * 2 + [near] * 10,
        out_specs=[near] * 4,
        scratch_shapes=[pltpu.VMEM((rows, 128), f32)],
        out_shape=[
            jax.ShapeDtypeStruct((rows, cols), b16),
            jax.ShapeDtypeStruct((rows, cols), b16),
            jax.ShapeDtypeStruct((2 * rows, width // 2), b16),
            jax.ShapeDtypeStruct((2 * rows, time.size // (2 * rows)), b16),
        ],
        cost_estimate=little,
        name="prepare",
    )(where, steps, *[v.reshape(1, -1) for v in vectors], mask, qkv, up, out, time)


def body(
    inputs, teacher, valid_mask, time_steps, qkv_weight, out_weight, up_weight, down_weight,
    time_weight, time_bias, norm_gain, norm_bias, up_bias, down_bias,
):
    x, c, y, z, depth = place()
    chips = 4 * depth
    k_chip = 4 * z + 2 * y + x
    seqs, block, width = inputs.shape
    rows = qkv_weight.shape[0]
    ff_rows = down_weight.shape[0]
    half = width // 2
    tokens = 4 * block
    mine = 2 * block
    ff = up_weight.shape[1] // 2
    pairs = half // 128

    tiled = rows % 32 == 0 and ff_rows % 128 == 0
    where = jnp.stack([x, c, y, z])

    te_rows = time_weight.shape[0]
    te_folds = 2 * rows // te_rows
    cut = 128 + 3 * half
    if tiled:
        own, other, out_low, time_low = prepare(
            where, time_steps, (time_bias, norm_gain, norm_bias, up_bias, down_bias), valid_mask,
            qkv_weight, up_weight, out_weight, time_weight,
        )
    else:

        def own_other(v):
            return [pick(v, i, 2).reshape(rows, -1).astype(b16) for i in (c, 1 - c)]

        def fold(v, n):
            return jnp.concatenate(jnp.split(v.astype(b16), n, axis=1), axis=0)

        count = jnp.sum(valid_mask)
        step = pick(time_steps, x)
        whole_numbers = jnp.stack([count // 256, count % 256, step // 32, step % 32]).astype(f32)
        vector = jnp.concatenate([time_bias, norm_gain, norm_bias, up_bias, down_bias, whole_numbers])
        vector = jnp.pad(vector, (0, 384 - vector.shape[0])).reshape(3, 128)
        vector = jnp.pad(vector.astype(b16), ((0, rows - 3), (0, 0)))
        qkv_cut = qkv_weight.reshape(rows, 3, 2, pairs, 128).transpose(0, 3, 2, 1, 4)
        qkv_own, qkv_other = own_other(qkv_cut.reshape(rows, pairs, 2, 3 * 128))
        up_own, up_other = own_other(up_weight.reshape(rows, -1, 2, ff_rows))
        own = jnp.concatenate([vector, qkv_own, up_own], axis=1)
        other = jnp.concatenate([vector, qkv_other, up_other], axis=1)
        out_low, time_low = fold(out_weight, 2), fold(time_weight, te_folds)
    other = swap_core(other)
    last = own.shape[1]
    if tiled:
        first_half, second_half = pl.ds(0, rows), pl.ds(rows, rows)

        def copies(x, c, y, z):
            made = []
            for source, at in ((0, c), (1, 1 - c)):
                made.append((source, (slice(None), pl.ds(0, cut)), 0, (at, slice(None), pl.ds(0, cut))))
                made.append((source, (slice(None), pl.ds(cut, ff)), 1, (at, slice(None), pl.ds(0, ff))))
            for at, half_rows in enumerate((first_half, second_half)):
                made.append((3, (half_rows,), 0, (at, slice(None), pl.ds(cut, time_low.shape[1]))))
                made.append((2, (half_rows,), 1, (at, slice(None), pl.ds(ff, half))))
            return made

        shapes = [
            jax.ShapeDtypeStruct((2, rows, cut + time_low.shape[1]), b16),
            jax.ShapeDtypeStruct((2, rows, ff + half), b16),
        ]
        piece_1, piece_2 = move(where, [own, other, out_low, time_low], shapes, copies)
        piece_1 = piece_1.reshape(2 * rows, -1)
        piece_2 = piece_2.reshape(2 * rows, -1)
    else:
        chip = jnp.concatenate(
            [jnp.where(c == 0, own, other), jnp.where(c == 0, other, own)], axis=0
        )
        piece_1 = jnp.concatenate([chip[:, :cut], time_low], axis=1)
        piece_2 = jnp.concatenate([chip[:, cut:], out_low], axis=1)
    down_full = lax.all_gather(down_weight.astype(b16), ("z", "y", "x"), axis=0, tiled=True)

    source_far = swap_x(pick(inputs, 1 - x))
    marks = valid_mask.astype(b16)
    target_marks = jnp.concatenate(
        [teacher, jnp.broadcast_to(marks[:, :, None], (seqs, block, 128))], axis=2
    )
    pieces_1 = gather_z(piece_1, tiled)
    stack_1 = stack_z(pieces_1, tiled)
    source_far, stack_1[0] = tie(source_far, stack_1[0])
    piece_2, stack_1[1] = tie(piece_2, stack_1[1])
    pieces_2 = gather_z(piece_2, tiled)
    near_1 = list(gather_near(stack_1))
    near_1[2], near_1[3], pieces_2[1] = tie(near_1[2], near_1[3], pieces_2[1])
    source_far, near_1[0] = tie(source_far, near_1[0])
    source_low = jnp.concatenate([pick(inputs, x), source_far], axis=0)
    source_all = jnp.concatenate([source_low, swap_core(source_low)], axis=0)
    far_1 = list(gather_far(near_1))
    vectors, qkv_full, time_full = assemble(
        near_1, far_1, [0, 128, cut, piece_1.shape[1]], tiled
    )
    qkv_full = qkv_full.reshape(width, 3 * half)
    near_2 = list(gather_near(stack_z(pieces_2, tiled, tuple(far_1))))
    f = 2 * x + c
    blocks = jnp.stack([f, f ^ 2, f ^ 1, f ^ 3])
    positions = (blocks[:, None] * block + jnp.arange(block)[None, :]).reshape(tokens).astype(f32)
    pace = jnp.exp(jnp.arange(HD // 2, dtype=f32) * (-2.0 * math.log(10000.0) / HD))
    angles = positions[:, None] * pace[None, :]
    cosine = jnp.tile(jnp.cos(angles), (1, 4))
    sine = jnp.sin(angles)
    sine = jnp.tile(jnp.concatenate([-sine, sine], axis=1), (1, 2))

    vectors = vectors.reshape(chips, 2, rows, 128).astype(f32)
    packed = vectors[:, :, :3].reshape(chips, 2, 384)
    at = 0

    def take(n):
        nonlocal at
        at += 1 if tiled else n
        return vectors[:, :, at - 1, :n] if tiled else packed[:, :, at - n : at]

    bias_time = take(time_bias.shape[0]).reshape(2 * width)
    gain = take(rows).reshape(width)
    shift = take(rows).reshape(width)
    bias_up = pick(take(ff_rows), c, 1).reshape(ff)
    bias_down = take(rows).reshape(width)
    numbers = take(4)
    valid_total = jnp.sum(numbers[:, :, 0]) * 256.0 + jnp.sum(numbers[:, :, 1])
    steps = numbers[:, 0, 2] * 32.0 + numbers[:, 0, 3]
    token_total = 2 * depth * seqs * tokens
    factor = (token_total * width / 2) / (valid_total * width)

    spread = jnp.exp(jnp.arange(TE // 2, dtype=f32) * (-math.log(10000.0) / (TE // 2)))
    angle = steps[:, None] * spread[None]
    features = jnp.concatenate([jnp.sin(angle), jnp.cos(angle)], axis=1).astype(b16)
    feature_core = pick(pick(features, k_chip).reshape(chips, 2, te_rows), c, 1)
    time_parts = time_full.reshape(chips, te_folds, te_rows, -1).astype(f32)
    part = jnp.sum(feature_core.astype(f32)[:, None, :, None] * time_parts, axis=(0, 2))
    part = part.reshape(-1, 128)
    condition = (part + swap_core(part)).reshape(2, width) + bias_time.reshape(2, width)
    scale = 1.0 + condition[:1]
    hidden, project = project_tokens(source_all, scale, condition[1:], qkv_full)
    near_2[2], near_2[3], project = tie(near_2[2], near_2[3], project)
    far_2 = list(gather_far(near_2))
    ahead = pairs // 2
    turned_a, mixed_a, log_a = attend(project, cosine, sine, 0, ahead)
    turned_b, mixed_b, log_b = attend(project, cosine, sine, ahead, pairs - ahead, (mixed_a,))
    far_2[0], mixed_a, mixed_b = tie(far_2[0], mixed_a, mixed_b)
    target_far, far_2[1] = tie(pick(target_marks, 1 - x), far_2[1])
    target_far = swap_x(target_far)
    up_full, out_half = assemble(near_2, far_2, [0, ff, ff + half], tiled)
    up_full = up_full.reshape(width, ff)
    out_far = swap_core(out_half)
    if tiled:

        def copies(x, c, y, z):
            every = slice(None)
            return [
                (n, (every, pl.ds(h * rows, rows)), 0, (every, at, every, pl.ds(h * half, half)))
                for n, at in ((0, c), (1, 1 - c))
                for h in range(2)
            ]

        shape = jax.ShapeDtypeStruct((chips, 2, rows, width), b16)
        out_full = move(where, [out_half, out_far], [shape], copies)[0]
    else:
        out_both = jnp.stack(
            [jnp.where(c == 0, out_half, out_far), jnp.where(c == 0, out_far, out_half)], axis=1
        ).reshape(chips, 2, 2, rows, half)
        out_full = jnp.concatenate([out_both[:, :, 0], out_both[:, :, 1]], axis=-1)
    out_full = out_full.reshape(width, width)
    mixed = jnp.concatenate([mixed_a, mixed_b], axis=1)
    mixed_far = swap_core(mixed[mine:])
    mixture = jnp.where(
        c == 0,
        jnp.concatenate([mixed[:mine], mixed_far], axis=1),
        jnp.concatenate([mixed_far, mixed[:mine]], axis=1),
    )
    middle = source_low.astype(f32) + dot(mixture, out_full, 1, 0)
    n2, rate2 = stats(middle)
    second = (n2 * gain + shift).astype(b16)
    second_all = jnp.concatenate([second, swap_core(second)], axis=0)
    inner = dot(second_all, up_full, 1, 0) + bias_up
    flat = 0.5 * (1.0 + lax.erf(inner * (2.0**-0.5)))
    active = (inner * flat).astype(b16)
    slope = flat + inner * jnp.exp(-0.5 * inner * inner) * ((2.0 * math.pi) ** -0.5)
    active, target_far = tie(active, target_far)
    down = dot(active, down_full, 1, 0)
    result = middle + (down[:mine] + swap_core(down[mine:].astype(b16)).astype(f32) + bias_down)

    target_marks = jnp.concatenate([pick(target_marks, x), target_far], axis=0)
    target = target_marks[:, :width].astype(f32)
    mark = target_marks[:, width : width + 1].astype(f32)
    differ = result - target
    loss_part = jnp.sum(mark * differ * differ)
    result_grad = 2.0 * mark * differ * factor

    down_in = result_grad.astype(b16)
    down_in_all = jnp.concatenate([down_in, swap_core(down_in)], axis=0)
    near_axes = ("y", "x")
    result_low = result.astype(b16)
    down_term = dot(active, down_in_all, 0, 0).astype(b16)
    down_sum = Scatter(down_term.reshape(chips, -1, width), where, tiled)
    down_in_all, down_sum.got[0] = tie(down_in_all, down_sum.got[0])
    down_sum.near()
    inner_grad = (dot(down_in_all, down_full, 1, 1) * slope).astype(b16)
    second_part = dot(inner_grad, up_full, 1, 1)
    second_send, second_all, *down_sum.got = tie(
        second_part[mine:].astype(b16), second_all, *down_sum.got
    )
    second_got = swap_core(second_send)
    down_sum.add_near()
    second_all, down_sum.got[0] = tie(second_all, down_sum.got[0])
    down_sum.far()
    up_term = dot(second_all, inner_grad, 0, 0).astype(b16)
    up_sum = Scatter(up_term.reshape(chips, -1, ff), where, tiled)
    second_got, up_sum.got[0] = tie(second_got, up_sum.got[0])
    up_sum.near()
    second_grad = second_part[:mine] + second_got.astype(f32)
    middle_grad = result_grad + norm_back(second_grad * gain, n2, rate2)
    branch = middle_grad.astype(b16)
    mixture_grad = dot(branch, out_full, 1, 1).astype(b16)
    mixture_far, branch = tie(
        lax.dynamic_slice_in_dim(mixture_grad, (1 - c) * half, half, 1), branch
    )
    mixture_far = swap_core(mixture_far)
    out_term = dot(mixture, branch, 0, 0).astype(b16).reshape(chips, 2, rows, width)
    mixture_far, out_send, out_keep = tie(
        mixture_far, pick(out_term, 1 - c, 1), pick(out_term, c, 1)
    )
    out_got = swap_core(out_send)
    mixture_grad = jnp.concatenate(
        [lax.dynamic_slice_in_dim(mixture_grad, c * half, half, 1), mixture_far], axis=0
    )

    def pair_back(p, deps):
        turned, log = (turned_a, log_a) if p < ahead else (turned_b, log_b)
        at = p if p < ahead else p - ahead
        return attend_back(turned, log, mixture_grad, cosine, sine, at, p, 1, deps)

    grads = [pair_back(0, ())]
    grads.append(pair_back(1, (grads[-1],)))
    down_sum.got[0], down_sum.got[1], grads[-1] = tie(down_sum.got[0], down_sum.got[1], grads[-1])
    down_sum.add_far(True)
    grads[-1], down_sum.got[0] = tie(grads[-1], down_sum.got[0])
    down_sum.scatter_along()
    for p in range(2, pairs - 1):
        grads.append(pair_back(p, (grads[-1],)))
    up_sum.got[0], up_sum.got[1], grads[-1] = tie(up_sum.got[0], up_sum.got[1], grads[-1])
    up_sum.add_near()
    grads.append(pair_back(pairs - 1, (grads[-1], up_sum.keep[0])))
    up_sum.far()
    project_grad = jnp.concatenate(grads, axis=1)
    qkv_term = dot(hidden, project_grad, 0, 0).astype(b16).reshape(chips, 2 * rows, -1)
    qkv_cols = qkv_term.shape[2]
    out_term = add_low(out_keep, out_got)
    out_term = jnp.concatenate([out_term[:, :, :half], out_term[:, :, half:]], axis=1)
    last_sum = Scatter(jnp.concatenate([qkv_term, out_term], axis=2), where, tiled)
    project_grad, last_sum.got[0] = tie(project_grad, last_sum.got[0])
    last_sum.near()
    hidden_part = dot(project_grad, qkv_full, 1, 1)
    hidden_got, hidden_keep, *up_sum.got = tie(
        hidden_part[mine:].astype(b16), hidden_part[:mine], *up_sum.got
    )
    hidden_got = swap_core(hidden_got)
    up_sum.add_far(True)
    up_sum.got[0], hidden_got = tie(up_sum.got[0], hidden_got)
    up_sum.scatter_along()
    hidden_grad = hidden_keep + hidden_got.astype(f32)
    n1, rate1 = stats(source_low.astype(f32))
    input_grad = middle_grad + norm_back(hidden_grad * scale, n1, rate1)

    small = jnp.concatenate(
        [
            jnp.sum(hidden_grad * n1, 0),
            jnp.sum(hidden_grad, 0),
            jnp.sum(second_grad * n2, 0),
            jnp.sum(second_grad, 0),
            jnp.sum(down_in.astype(f32), 0),
            jnp.full((128,), loss_part),
        ]
    )
    small = small.reshape(-1, 128)
    small_got = swap_core(small)
    last_sum.got[0], input_grad = tie(last_sum.got[0], input_grad)
    last_sum.add_near()
    small_got, input_grad, last_sum.got[0] = tie(small_got, input_grad, last_sum.got[0])
    last_sum.far()
    small = small + small_got
    up_bias_part = jnp.sum(inner_grad.astype(f32), 0).reshape(-1, 128)
    fill = jnp.zeros((-(small.shape[0] + up_bias_part.shape[0]) % 8, 128), f32)
    small = jnp.concatenate([small, up_bias_part, fill], axis=0)
    small = gather_small(small)
    up_sum = up_sum.total()
    last_sum.add_far()
    input_far, result_far, last_sum.got[1] = tie(
        input_grad[block:].astype(b16), result_low[block:], last_sum.got[1]
    )
    last_sum.along()
    input_far = swap_x(input_far).astype(f32)
    result_far = swap_x(result_far)

    def spread_out(near, far):
        return jnp.stack([jnp.where(x == 0, near, far), jnp.where(x == 0, far, near)])

    activations = spread_out(result_low[:block], result_far)
    input_grad = spread_out(input_grad[:block], input_far)
    down_sum = down_sum.total()
    index = 2 * k_chip + c
    feature_rows = lax.dynamic_slice_in_dim(features, index * te_rows, te_rows, 1).astype(f32)
    time_sum, time_bias_sum, gain_sum, shift_sum, down_bias_sum, up_bias_sum, loss_sum = finish(
        jnp.stack([index, k_chip]), small, feature_rows.T, 2 * width, rows, ff_rows
    )
    loss = (loss_sum[0] / (valid_total * width)).reshape(1)

    def columns(total, inner_size):
        total = total.reshape(2, rows, -1, inner_size)
        near = pick(total, c)
        far = swap_core(pick(total, 1 - c))
        return jnp.stack(
            [jnp.where(c == 0, near, far), jnp.where(c == 0, far, near)], axis=2
        ).reshape(rows, -1)

    up_sum = columns(up_sum, ff_rows)
    others = (activations, input_grad, up_sum, down_sum, time_sum, loss)
    tied = tie(*last_sum.got, *others)
    last_sum.got = tied[: -len(others)]
    activations, input_grad, up_sum, down_sum, time_sum, loss = tied[-len(others) :]
    last_sum = last_sum.total()
    out_sum = last_sum[:, qkv_cols:]
    out_sum = jnp.concatenate([out_sum[:rows], out_sum[rows:]], axis=1)
    qkv_sum = last_sum[:, :qkv_cols].reshape(2 * rows, pairs, 3, 128)
    qkv_sum = qkv_sum.transpose(0, 2, 1, 3).reshape(2 * rows, -1)
    return (
        activations,
        loss,
        input_grad,
        columns(qkv_sum, half),
        out_sum,
        up_sum,
        down_sum,
        time_sum,
        time_bias_sum,
        gain_sum,
        shift_sum,
        up_bias_sum,
        down_bias_sum,
    )


def solution(mesh):
    split = mesh.devices.reshape(-1, 2, 2, 2)
    finer = jax.sharding.Mesh(split, ("z", "y", "x", "core"))
    both = ("z", "y", "x", "core")
    tokens = P(("z", "y"), ("x", "core"), None)
    weight = P(both, None)
    vector = P(both)
    return jax.shard_map(
        body,
        mesh=finer,
        in_specs=(tokens, tokens, P(("z", "y"), ("x", "core")), P(("z", "y"))) + (weight,) * 5 + (vector,) * 5,
        out_specs=(tokens, P(), tokens) + (weight,) * 5 + (vector,) * 5,
        check_vma=False,
    )
```

```python
import math

import jax
import jax.numpy as jnp
from jax import lax
from jax.experimental import pallas as pl
from jax.experimental.pallas import tpu as pltpu
from jax.sharding import PartitionSpec as P

HD = 64
TE = 256

b16 = jnp.bfloat16
f32 = jnp.float32
highest = lax.Precision.HIGHEST
epsilon = 1e-05
little = pl.CostEstimate(flops=1, transcendentals=0, bytes_accessed=1)


def swap_core(v):
    return lax.ppermute(v, "core", [(0, 1), (1, 0)])


def swap_x(v):
    return lax.ppermute(v, "x", [(0, 1), (1, 0)])


def swap_y(v):
    return lax.ppermute(v, "y", [(0, 1), (1, 0)])


def shift_z(v, k):
    depth = lax.axis_size("z")
    return lax.ppermute(v, "z", [(i, (i + k) % depth) for i in range(depth)])


def place():
    return tuple(lax.axis_index(a) for a in ("x", "core", "y", "z")) + (lax.axis_size("z"),)


def pick(v, index, axis=0):
    return lax.dynamic_index_in_dim(v, index, axis, False)


def unread(deps):
    return [pl.BlockSpec(memory_space=pl.ANY)] * len(deps)


def move(place_of, sources, outs, copies, deps=()):
    def kernel(where, *refs):
        x, c, y, z = (where[i] for i in range(4))
        given = refs[: len(sources)]
        made = refs[len(sources) + len(deps) :]
        for source, read, out, write in copies(x, c, y, z):
            made[out][write] = given[source][read]

    near = pl.BlockSpec(memory_space=pltpu.VMEM)
    return pl.pallas_call(
        kernel,
        in_specs=[pl.BlockSpec(memory_space=pltpu.SMEM)] + [near] * len(sources) + unread(deps),
        out_specs=[near] * len(outs),
        out_shape=outs,
        compiler_params=pltpu.CompilerParams(vmem_limit_bytes=32 << 20),
        cost_estimate=little,
        name="move",
    )(place_of, *sources, *deps)


def tie(*values):
    return lax.optimization_barrier(values)


def gather_z(piece, tiled=False):
    return [piece] + [shift_z(piece, k) for k in range(1, place()[4])]


def stack_z(pieces, tiled=False, deps=()):
    x, c, y, z, depth = place()
    rows, cols = pieces[0].shape
    half = rows // 2
    if tiled:

        def copies(x, c, y, z):
            return [
                (k, pl.ds(h * half, half), h, lax.rem(z - k + depth, depth))
                for k in range(depth)
                for h in range(2)
            ]

        shape = jax.ShapeDtypeStruct((depth, half, cols), b16)
        return list(move(jnp.stack([x, c, y, z]), pieces, [shape, shape], copies, deps))
    stack = jnp.zeros((depth, rows, cols), b16)
    for k in range(depth):
        stack = lax.dynamic_update_slice(stack, pieces[k][None], ((z - k) % depth, 0, 0))
    return [stack[:, :half], stack[:, half:]]


def gather_near(stacks):
    top, low = stacks
    return top, low, swap_x(top), swap_y(low)


def gather_far(near):
    top, low, top_x, low_y = near
    return swap_y(jnp.stack([top, top_x])), swap_x(jnp.stack([low, low_y]))


def assemble(near, far, cuts, tiled=False):
    x, c, y, z, depth = place()
    top, low, top_x, low_y = near
    top_far, low_far = far
    half, cols = top.shape[1:]
    rows = 2 * half
    if tiled:
        every = slice(None)

        def copies(x, c, y, z):
            made = []
            for n in range(len(cuts) - 1):
                run = pl.ds(cuts[n], cuts[n + 1] - cuts[n])
                one = (every, every, run)
                up, down = pl.ds(0, half), pl.ds(half, half)
                made += [
                    (0, one, n, (every, y, x, up)),
                    (2, one, n, (every, y, 1 - x, up)),
                    (4, (0,) + one, n, (every, 1 - y, x, up)),
                    (4, (1,) + one, n, (every, 1 - y, 1 - x, up)),
                    (1, one, n, (every, y, x, down)),
                    (3, one, n, (every, 1 - y, x, down)),
                    (5, (0,) + one, n, (every, y, 1 - x, down)),
                    (5, (1,) + one, n, (every, 1 - y, 1 - x, down)),
                ]
            return made

        shapes = [
            jax.ShapeDtypeStruct((depth, 2, 2, rows, cuts[n + 1] - cuts[n]), top.dtype)
            for n in range(len(cuts) - 1)
        ]
        parts = move(
            jnp.stack([x, c, y, z]), [top, low, top_x, low_y, top_far, low_far], shapes, copies
        )
        return [p.reshape(4 * depth, rows, -1) for p in parts]
    whole = jnp.zeros((depth, 2, 2, rows, cols), top.dtype)

    def put(whole, part, yy, xx, at):
        return lax.dynamic_update_slice(whole, part[:, None, None], (0, yy, xx, at, 0))

    whole = put(whole, top, y, x, 0)
    whole = put(whole, top_x, y, 1 - x, 0)
    whole = put(whole, top_far[0], 1 - y, x, 0)
    whole = put(whole, top_far[1], 1 - y, 1 - x, 0)
    whole = put(whole, low, y, x, half)
    whole = put(whole, low_y, 1 - y, x, half)
    whole = put(whole, low_far[0], y, 1 - x, half)
    whole = put(whole, low_far[1], 1 - y, 1 - x, half)
    whole = whole.reshape(4 * depth, rows, cols)
    return [whole[:, :, cuts[n] : cuts[n + 1]] for n in range(len(cuts) - 1)]


def add_low(a, b):
    return (a.astype(f32) + b.astype(f32)).astype(a.dtype)


def exchange(v, axes):
    return lax.all_to_all(v, axes, 0, 0, tiled=True)


def add_up(v):
    total = v[0].astype(f32)
    for i in range(1, len(v)):
        total = total + v[i].astype(f32)
    return total


def add_near(got, where, tiled):
    depth = got.shape[1]
    if not tiled:
        z = lax.axis_index("z")
        both = add_up(got).astype(b16)
        return [pick(both, (z + k) % depth) for k in range(depth)]

    def kernel(where, got, *outs):
        for k in range(depth):
            at = lax.rem(where[3] + k, depth)
            total = got[0, at].astype(f32)
            for i in range(1, got.shape[0]):
                total = total + got[i, at].astype(f32)
            outs[k][...] = total.astype(b16)

    near = pl.BlockSpec(memory_space=pltpu.VMEM)
    return pl.pallas_call(
        kernel,
        in_specs=[pl.BlockSpec(memory_space=pltpu.SMEM), near],
        out_specs=[near] * depth,
        out_shape=[jax.ShapeDtypeStruct(got.shape[2:], b16)] * depth,
        compiler_params=pltpu.CompilerParams(vmem_limit_bytes=32 << 20),
        cost_estimate=little,
        name="add_near",
    )(where, got)


def stack_terms(first, second):
    chips, top, width = first.shape
    rows, runs = second.shape[1], second.shape[2] // width
    shape = (chips, top + runs * rows, width)
    if top % 16 or rows % 16:
        return jnp.concatenate([first] + jnp.split(second, runs, axis=2), axis=1)

    def kernel(first, second, made):
        made[:, :top] = first[...]
        for n in range(runs):
            made[:, top + n * rows : top + (n + 1) * rows] = second[
                :, :, n * width : (n + 1) * width
            ]

    near = pl.BlockSpec(memory_space=pltpu.VMEM)
    return pl.pallas_call(
        kernel,
        in_specs=[near, near],
        out_specs=near,
        out_shape=jax.ShapeDtypeStruct(shape, first.dtype),
        compiler_params=pltpu.CompilerParams(vmem_limit_bytes=40 << 20),
        cost_estimate=little,
        name="stack_terms",
    )(first, second)


def send_z(parts):
    return [parts[0]] + [shift_z(v, k) for k, v in enumerate(parts) if k]


def regroup(v, cuts):
    runs = [slice(cuts[n], cuts[n + 1]) for n in range(len(cuts) - 1)]
    if v.shape[2] % 16 or v.shape[3] % 128:
        return [jnp.swapaxes(v[..., run], 0, 1) for run in runs]

    def kernel(given, *made):
        for out, run in zip(made, runs):
            for i in range(v.shape[0]):
                for j in range(v.shape[1]):
                    out[j, i] = given[i, j, :, run]

    near = pl.BlockSpec(memory_space=pltpu.VMEM)
    return pl.pallas_call(
        kernel,
        in_specs=[near],
        out_specs=[near] * len(runs),
        out_shape=[
            jax.ShapeDtypeStruct((v.shape[1], v.shape[0], v.shape[2], r.stop - r.start), v.dtype)
            for r in runs
        ],
        compiler_params=pltpu.CompilerParams(vmem_limit_bytes=32 << 20),
        cost_estimate=little,
        name="regroup",
    )(v)


def swap_order(v):
    return regroup(v, [0, v.shape[3]])[0]


def scatter_send(parts, where, tiled, deps=()):
    x, c, y, z, depth = place()
    chips, rows, cols = parts.shape
    half = rows // 2
    if not tiled:
        grid = parts.reshape(depth, 2, 2, rows, cols)
        return [pick(grid[:, :, :, :half], 1 - x, 2), pick(grid[:, :, :, half:], 1 - y, 1)]

    def copies(x, c, y, z):
        return [
            (0, (slice(None), slice(None), 1 - x, 0), 0, slice(None)),
            (0, (slice(None), 1 - y, slice(None), 1), 1, slice(None)),
        ]

    shape = jax.ShapeDtypeStruct((depth, 2, half, cols), parts.dtype)
    grid = parts.reshape(depth, 2, 2, 2, half, cols)
    return list(move(where, [grid], [shape, shape], copies, deps))


def scatter_near(parts, got, where, tiled):
    x, c, y, z, depth = place()
    chips, rows, cols = parts.shape
    half = rows // 2
    if not tiled:
        grid = parts.reshape(depth, 2, 2, rows, cols)
        top = add_low(pick(grid[:, :, :, :half], x, 2), got[0])
        low = add_low(pick(grid[:, :, :, half:], y, 1), got[1])
        return pick(top, y, 1), pick(top, 1 - y, 1), pick(low, x, 1), pick(low, 1 - x, 1)

    def kernel(where, grid, top, low, keep_t, send_t, keep_l, send_l):
        x, y = where[0], where[2]
        for out, yy in ((keep_t, y), (send_t, 1 - y)):
            out[...] = add_low(grid[:, yy, x, 0], top[:, yy])
        for out, xx in ((keep_l, x), (send_l, 1 - x)):
            out[...] = add_low(grid[:, y, xx, 1], low[:, xx])

    near = pl.BlockSpec(memory_space=pltpu.VMEM)
    shape = jax.ShapeDtypeStruct((depth, half, cols), parts.dtype)
    return pl.pallas_call(
        kernel,
        in_specs=[pl.BlockSpec(memory_space=pltpu.SMEM)] + [near] * 3,
        out_specs=[near] * 4,
        out_shape=[shape] * 4,
        compiler_params=pltpu.CompilerParams(vmem_limit_bytes=32 << 20),
        cost_estimate=little,
        name="scatter_near",
    )(where, parts.reshape(depth, 2, 2, 2, half, cols), got[0], got[1])


def scatter_far(keep, got, where, tiled, ordered=False):
    x, c, y, z, depth = place()
    half, cols = keep[0].shape[1:]
    if not tiled:
        both = jnp.concatenate([add_low(k, g) for k, g in zip(keep, got)], axis=1)
        return [both] if ordered else [pick(both, (z + k) % depth) for k in range(depth)]

    def kernel(where, top, low, top_got, low_got, *outs):
        if ordered:
            outs[0][:, :half] = add_low(top[...], top_got[...])
            outs[0][:, half:] = add_low(low[...], low_got[...])
            return
        for k in range(depth):
            at = lax.rem(where[3] + k, depth)
            outs[k][:half] = add_low(top[at], top_got[at])
            outs[k][half:] = add_low(low[at], low_got[at])

    near = pl.BlockSpec(memory_space=pltpu.VMEM)
    shape = jax.ShapeDtypeStruct(((depth,) if ordered else ()) + (2 * half, cols), keep[0].dtype)
    count = 1 if ordered else depth
    return pl.pallas_call(
        kernel,
        in_specs=[pl.BlockSpec(memory_space=pltpu.SMEM)] + [near] * 4,
        out_specs=[near] * count,
        out_shape=[shape] * count,
        compiler_params=pltpu.CompilerParams(vmem_limit_bytes=32 << 20),
        cost_estimate=little,
        name="scatter_far",
    )(where, keep[0], keep[1], got[0], got[1])


class Scatter:
    def __init__(self, parts, where, tiled, deps=()):
        self.parts, self.where, self.tiled = parts, where, tiled
        self.got = scatter_send(parts, where, tiled, deps)

    def near(self):
        top, low = self.got
        self.got = [swap_x(top), swap_y(low)]

    def add_near(self):
        keep_t, send_t, keep_l, send_l = scatter_near(self.parts, self.got, self.where, self.tiled)
        self.keep, self.got = [keep_t, keep_l], [send_t, send_l]

    def far(self):
        self.got = [swap_y(self.got[0]), swap_x(self.got[1])]

    def add_far(self, ordered=False):
        self.got = list(scatter_far(self.keep, self.got, self.where, self.tiled, ordered))

    def scatter_along(self):
        self.got = [lax.psum_scatter(self.got[0], "z", scatter_dimension=0, tiled=True)[0]]

    def along(self):
        self.got = [self.got[0]] + [shift_z(v, k) for k, v in enumerate(self.got) if k]

    def total(self):
        return sum(v.astype(f32) for v in self.got)


def gather_small(v):
    x, c, y, z, depth = place()
    pieces = [v] + [shift_z(v, k) for k in range(1, depth)]
    stack = jnp.zeros((depth,) + v.shape, v.dtype)
    for k in range(depth):
        stack = lax.dynamic_update_slice(stack, pieces[k][None], ((z - k) % depth, 0, 0))
    other = swap_x(stack)
    pair = jnp.stack([jnp.where(x == 0, stack, other), jnp.where(x == 0, other, stack)], axis=1)
    other = swap_y(pair)
    quad = jnp.stack([jnp.where(y == 0, pair, other), jnp.where(y == 0, other, pair)], axis=1)
    return quad.reshape((4 * depth,) + v.shape)


def finish(place_of, small, features, wide, rows, ff_rows):
    chips = small.shape[0]
    te_rows = features.shape[0]
    blocks = wide // 128
    starts = [0, blocks, 3 * blocks // 2, 2 * blocks, 5 * blocks // 2 + 1]
    sizes = [2 * rows, rows, rows, rows, ff_rows]

    def kernel(where, small, features, time_out, *refs):
        outs, loss_out, sums = refs[:5], refs[5], refs[6]
        sums[...] = jnp.sum(small[...], axis=0)
        for n in range(blocks):
            total = features[:, :1] * small[0, n : n + 1]
            for k in range(1, chips):
                total += features[:, k : k + 1] * small[k, n : n + 1]
            time_out[:, n * 128 : (n + 1) * 128] = total
        for start, size, out, at in zip(starts, sizes, outs, (0, 0, 0, 0, 1)):
            first = where[at] * size
            row = sums[pl.ds(start + first // 128, 1)]
            out[...] = pltpu.roll(row, lax.rem(128 - lax.rem(first, 128), 128), 1)[:, :size]
        loss_out[...] = sums[5 * blocks // 2 : 5 * blocks // 2 + 1, :1]

    near = pl.BlockSpec(memory_space=pltpu.VMEM)
    lines = [jax.ShapeDtypeStruct((1, n), f32) for n in sizes + [1]]
    made = pl.pallas_call(
        kernel,
        in_specs=[pl.BlockSpec(memory_space=pltpu.SMEM), near, near],
        out_specs=[near] * 7,
        out_shape=[jax.ShapeDtypeStruct((te_rows, wide), f32)] + lines,
        scratch_shapes=[pltpu.VMEM(small.shape[1:], f32)],
        cost_estimate=little,
        name="finish",
    )(place_of, small, features)
    return [made[0]] + [v.reshape(-1) for v in made[1:]]


def project_kernel(source, scale, shift, weight, hidden_out, project_out):
    v = source[...].astype(f32)
    centre = v - jnp.mean(v, axis=1, keepdims=True)
    rate = lax.rsqrt(jnp.mean(centre * centre, axis=1, keepdims=True) + epsilon)
    hidden = (centre * rate * scale[...] + shift[...]).astype(b16)
    hidden_out[...] = hidden
    project_out[...] = jnp.dot(hidden, weight[...], preferred_element_type=f32)


def project_tokens(source, scale, shift, weight):
    tokens, width = source.shape
    cols = weight.shape[1]
    step = 256
    row = pl.BlockSpec((1, width), lambda i: (0, 0))
    return pl.pallas_call(
        project_kernel,
        grid=(tokens // step,),
        in_specs=[
            pl.BlockSpec((step, width), lambda i: (i, 0)),
            row,
            row,
            pl.BlockSpec((width, cols), lambda i: (0, 0)),
        ],
        out_specs=[
            pl.BlockSpec((step, width), lambda i: (i, 0)),
            pl.BlockSpec((step, cols), lambda i: (i, 0)),
        ],
        out_shape=[
            jax.ShapeDtypeStruct((tokens, width), b16),
            jax.ShapeDtypeStruct((tokens, cols), f32),
        ],
        compiler_params=pltpu.CompilerParams(vmem_limit_bytes=48 << 20),
        cost_estimate=little,
        name="project",
    )(source, scale, shift, weight)


def stats(v):
    mean = jnp.mean(v, axis=-1, keepdims=True)
    centre = v - mean
    rate = lax.rsqrt(jnp.mean(centre * centre, axis=-1, keepdims=True) + epsilon)
    return centre * rate, rate


def norm_back(g, n, rate):
    return (g - jnp.mean(g, -1, keepdims=True) - n * jnp.mean(g * n, -1, keepdims=True)) * rate


def dot(a, b, da, db):
    return lax.dot_general(a, b, (((da,), (db,)), ((), ())), preferred_element_type=f32)


LOG2E = 1.4426950408889634
CHUNK = 512


def nn(a, b):
    return lax.dot_general(a, b, (((1,), (0,)), ((), ())), preferred_element_type=f32)


def nt(a, b):
    return lax.dot_general(a, b, (((1,), (1,)), ((), ())), preferred_element_type=f32)


def lane_halves(v):
    lane = lax.broadcasted_iota(jnp.int32, v.shape, 1)
    zero = jnp.zeros_like(v)
    return jnp.where(lane < HD, v, zero), jnp.where(lane < HD, zero, v)


def turn(v, cosine, sine):
    width = v.shape[1]
    lane = lax.broadcasted_iota(jnp.int32, v.shape, 1)
    swapped = jnp.where(
        lane % HD < HD // 2,
        pltpu.roll(v, width - HD // 2, 1),
        pltpu.roll(v, HD // 2, 1),
    )
    return v * cosine + swapped * sine


def attend_kernel(project_in, cos_in, sin_in, *refs):
    turned_out, mix_out, log_out = refs[-3:]
    cosine = cos_in[...]
    sine = sin_in[...]
    tokens = cosine.shape[0]
    q = turn(project_in[:, :128], cosine, sine).astype(b16)
    k = turn(project_in[:, 128:256], cosine, sine).astype(b16)
    v = project_in[:, 256:].astype(b16)
    turned_out[:, :128] = q
    turned_out[:, 128:256] = k
    turned_out[:, 256:] = v
    keys = lane_halves(k)
    v_turned = v.astype(f32).T.astype(b16)
    for at in range(0, tokens, CHUNK):
        part = q[at : at + CHUNK]
        mixed = []
        for h in range(2):
            scores = nt(keys[h], part) * (0.125 * LOG2E)
            top = jnp.max(scores, axis=0, keepdims=True)
            weight = jnp.exp2(scores - top)
            total = jnp.sum(weight, axis=0, keepdims=True)
            log_out[0, h : h + 1, at : at + CHUNK] = top + jnp.log2(total)
            probs = (weight * (1.0 / total)).astype(b16)
            mixed.append(nn(v_turned[h * HD : (h + 1) * HD], probs))
        mix_out[at : at + CHUNK] = jnp.concatenate(mixed, axis=0).T.astype(b16)


def attend(project, cosine, sine, start, pairs, deps=()):
    tokens = project.shape[0]
    table = pl.BlockSpec((tokens, 128), lambda p: (0, 0))
    return pl.pallas_call(
        attend_kernel,
        grid=(pairs,),
        in_specs=[pl.BlockSpec((tokens, 384), lambda p: (0, start + p)), table, table]
        + unread(deps),
        out_specs=[
            pl.BlockSpec((tokens, 384), lambda p: (0, p)),
            pl.BlockSpec((tokens, 128), lambda p: (0, p)),
            pl.BlockSpec((1, 2, tokens), lambda p: (p, 0, 0)),
        ],
        out_shape=[
            jax.ShapeDtypeStruct((tokens, 384 * pairs), b16),
            jax.ShapeDtypeStruct((tokens, 128 * pairs), b16),
            jax.ShapeDtypeStruct((pairs, 2, tokens), f32),
        ],
        compiler_params=pltpu.CompilerParams(vmem_limit_bytes=48 << 20),
        cost_estimate=little,
        name="attend",
    )(project, cosine, sine, *deps)


def attend_back_kernel(
    turned_in, grad_in, log_in, cos_in, sin_in, *refs
):
    grad_out, dk_sum, dv_sum, dq_turned = refs[-4:]
    q = turned_in[:, :128]
    k = turned_in[:, 128:256]
    tokens = q.shape[0]
    keys = lane_halves(k)
    values = lane_halves(turned_in[:, 256:])
    k_turned = k.astype(f32).T.astype(b16)
    for at in range(0, tokens, CHUNK):
        q_part = q[at : at + CHUNK]
        g_part = grad_in[at : at + CHUNK]
        q_halves = lane_halves(q_part)
        g_halves = lane_halves(g_part)
        for h in range(2):
            scores = nt(keys[h], q_part) * (0.125 * LOG2E)
            full = jnp.exp2(scores - log_in[0, h : h + 1, at : at + CHUNK])
            prob_grad = nt(values[h], g_part)
            product = full * prob_grad
            total = jnp.sum(product, axis=0, keepdims=True)
            score_grad = (product - full * total).astype(b16)
            dv_h = nn(full.astype(b16), g_halves[h])
            dk_h = nn(score_grad, q_halves[h])
            dq_turned[h * HD : (h + 1) * HD, at : at + CHUNK] = nn(
                k_turned[h * HD : (h + 1) * HD], score_grad
            )
            dk = dk_h if h == 0 else dk + dk_h
            dv = dv_h if h == 0 else dv + dv_h
        if at == 0:
            dk_sum[...] = dk
            dv_sum[...] = dv
        else:
            dk_sum[...] += dk
            dv_sum[...] += dv
    cosine = cos_in[...]
    sine = -sin_in[...]
    grad_out[:, :128] = turn(dq_turned[...].T * 0.125, cosine, sine).astype(b16)
    grad_out[:, 128:256] = turn(dk_sum[...] * 0.125, cosine, sine).astype(b16)
    grad_out[:, 256:] = dv_sum[...].astype(b16)


def attend_back(turned, log_total, mixture_grad, cosine, sine, start, grad_start, pairs, deps=()):
    tokens = turned.shape[0]
    table = pl.BlockSpec((tokens, 128), lambda p: (0, 0))
    return pl.pallas_call(
        attend_back_kernel,
        grid=(pairs,),
        in_specs=[
            pl.BlockSpec((tokens, 384), lambda p: (0, start + p)),
            pl.BlockSpec((tokens, 128), lambda p: (0, grad_start + p)),
            pl.BlockSpec((1, 2, tokens), lambda p: (start + p, 0, 0)),
            table,
            table,
        ]
        + unread(deps),
        out_specs=pl.BlockSpec((tokens, 384), lambda p: (0, p)),
        out_shape=jax.ShapeDtypeStruct((tokens, 384 * pairs), b16),
        scratch_shapes=[
            pltpu.VMEM((tokens, 128), f32),
            pltpu.VMEM((tokens, 128), f32),
            pltpu.VMEM((128, tokens), f32),
        ],
        compiler_params=pltpu.CompilerParams(vmem_limit_bytes=48 << 20),
        cost_estimate=little,
        name="attend_back",
    )(turned, mixture_grad, log_total, cosine, sine, *deps)


def prepare_kernel(
    where, steps, bias_time, gain, shift, bias_up, bias_down, mask, qkv, up, out, time,
    own, other, out_low, time_low, lines,
):
    c = where[1]
    rows, width = out.shape
    count = jnp.sum(mask[...].astype(f32), axis=1, keepdims=True)
    count = jnp.sum(count, axis=0, keepdims=True)
    high = jnp.floor(count * (1.0 / 256.0))
    step = steps[where[0]]
    lane = lax.broadcasted_iota(jnp.int32, (1, 128), 1)
    numbers = jnp.where(lane == 0, high, count - 256.0 * high)
    numbers = jnp.where(lane == 2, (step // 32).astype(f32), numbers)
    numbers = jnp.where(lane == 3, lax.rem(step, 32).astype(f32), numbers)
    half = width // 2
    step = 128
    for there, made in ((c, own), (1 - c, other)):
        lines[...] = jnp.zeros((rows, 128), f32)
        for n, v in enumerate((bias_time, gain, shift, bias_up, bias_down)):
            lines[n : n + 1, : v.shape[1]] = v[...]
        lines[5:6] = numbers
        made[:, :128] = lines[...].astype(b16)
        for p in range(half // 128):
            for n in range(3):
                at = pl.multiple_of(n * width + there * half + p * 128, 128)
                to = 128 + (3 * p + n) * 128
                made[:, to : to + 128] = qkv[:, pl.ds(at, 128)].astype(b16)
        to = 128 + 3 * half
        for n in range(up.shape[1] // (2 * step)):
            at = pl.multiple_of((2 * n + there) * step, 128)
            made[:, to + n * step : to + (n + 1) * step] = up[:, pl.ds(at, step)].astype(b16)
    for n in range(2):
        out_low[n * rows : (n + 1) * rows] = out[:, n * half : (n + 1) * half].astype(b16)
    te_rows = time.shape[0]
    folds = 2 * rows // te_rows
    cols = time.shape[1] // folds
    for n in range(0, folds, 2):
        pair = [time[:, (n + i) * cols : (n + i + 1) * cols] for i in range(2)]
        time_low[n * te_rows : (n + 2) * te_rows] = jnp.concatenate(pair, axis=0).astype(b16)


def prepare(where, steps, vectors, mask, qkv, up, out, time):
    rows, width = out.shape
    cols = 128 + 3 * width // 2 + up.shape[1] // 2
    near = pl.BlockSpec(memory_space=pltpu.VMEM)
    return pl.pallas_call(
        prepare_kernel,
        in_specs=[pl.BlockSpec(memory_space=pltpu.SMEM)] * 2 + [near] * 10,
        out_specs=[near] * 4,
        scratch_shapes=[pltpu.VMEM((rows, 128), f32)],
        out_shape=[
            jax.ShapeDtypeStruct((rows, cols), b16),
            jax.ShapeDtypeStruct((rows, cols), b16),
            jax.ShapeDtypeStruct((2 * rows, width // 2), b16),
            jax.ShapeDtypeStruct((2 * rows, time.size // (2 * rows)), b16),
        ],
        cost_estimate=little,
        name="prepare",
    )(where, steps, *[v.reshape(1, -1) for v in vectors], mask, qkv, up, out, time)


def body(
    inputs, teacher, valid_mask, time_steps, qkv_weight, out_weight, up_weight, down_weight,
    time_weight, time_bias, norm_gain, norm_bias, up_bias, down_bias,
):
    x, c, y, z, depth = place()
    chips = 4 * depth
    k_chip = 4 * z + 2 * y + x
    seqs, block, width = inputs.shape
    rows = qkv_weight.shape[0]
    ff_rows = down_weight.shape[0]
    half = width // 2
    tokens = 4 * block
    mine = 2 * block
    ff = up_weight.shape[1] // 2
    pairs = half // 128

    tiled = rows % 32 == 0 and ff_rows % 128 == 0
    where = jnp.stack([x, c, y, z])

    te_rows = time_weight.shape[0]
    te_folds = 2 * rows // te_rows
    cut = 128 + 3 * half
    if tiled:
        own, other, out_low, time_low = prepare(
            where, time_steps, (time_bias, norm_gain, norm_bias, up_bias, down_bias), valid_mask,
            qkv_weight, up_weight, out_weight, time_weight,
        )
    else:

        def own_other(v):
            return [pick(v, i, 2).reshape(rows, -1).astype(b16) for i in (c, 1 - c)]

        def fold(v, n):
            return jnp.concatenate(jnp.split(v.astype(b16), n, axis=1), axis=0)

        count = jnp.sum(valid_mask)
        step = pick(time_steps, x)
        whole_numbers = jnp.stack([count // 256, count % 256, step // 32, step % 32]).astype(f32)
        vector = jnp.concatenate([time_bias, norm_gain, norm_bias, up_bias, down_bias, whole_numbers])
        vector = jnp.pad(vector, (0, 384 - vector.shape[0])).reshape(3, 128)
        vector = jnp.pad(vector.astype(b16), ((0, rows - 3), (0, 0)))
        qkv_cut = qkv_weight.reshape(rows, 3, 2, pairs, 128).transpose(0, 3, 2, 1, 4)
        qkv_own, qkv_other = own_other(qkv_cut.reshape(rows, pairs, 2, 3 * 128))
        up_own, up_other = own_other(up_weight.reshape(rows, -1, 2, ff_rows))
        own = jnp.concatenate([vector, qkv_own, up_own], axis=1)
        other = jnp.concatenate([vector, qkv_other, up_other], axis=1)
        out_low, time_low = fold(out_weight, 2), fold(time_weight, te_folds)
    other = swap_core(other)
    last = own.shape[1]
    if tiled:
        first_half, second_half = pl.ds(0, rows), pl.ds(rows, rows)

        def copies(x, c, y, z):
            made = []
            for source, at in ((0, c), (1, 1 - c)):
                made.append((source, (slice(None), pl.ds(0, cut)), 0, (at, slice(None), pl.ds(0, cut))))
                made.append((source, (slice(None), pl.ds(cut, ff)), 1, (at, slice(None), pl.ds(0, ff))))
            for at, half_rows in enumerate((first_half, second_half)):
                made.append((3, (half_rows,), 0, (at, slice(None), pl.ds(cut, time_low.shape[1]))))
                made.append((2, (half_rows,), 1, (at, slice(None), pl.ds(ff, half))))
            return made

        shapes = [
            jax.ShapeDtypeStruct((2, rows, cut + time_low.shape[1]), b16),
            jax.ShapeDtypeStruct((2, rows, ff + half), b16),
        ]
        piece_1, piece_2 = move(where, [own, other, out_low, time_low], shapes, copies)
        piece_1 = piece_1.reshape(2 * rows, -1)
        piece_2 = piece_2.reshape(2 * rows, -1)
    else:
        chip = jnp.concatenate(
            [jnp.where(c == 0, own, other), jnp.where(c == 0, other, own)], axis=0
        )
        piece_1 = jnp.concatenate([chip[:, :cut], time_low], axis=1)
        piece_2 = jnp.concatenate([chip[:, cut:], out_low], axis=1)
    down_full = lax.all_gather(down_weight.astype(b16), ("z", "y", "x"), axis=0, tiled=True)

    source_far = swap_x(pick(inputs, 1 - x))
    marks = valid_mask.astype(b16)
    target_marks = jnp.concatenate(
        [teacher, jnp.broadcast_to(marks[:, :, None], (seqs, block, 128))], axis=2
    )
    pieces_1 = gather_z(piece_1, tiled)
    stack_1 = stack_z(pieces_1, tiled)
    source_far, stack_1[0] = tie(source_far, stack_1[0])
    piece_2, stack_1[1] = tie(piece_2, stack_1[1])
    pieces_2 = gather_z(piece_2, tiled)
    near_1 = list(gather_near(stack_1))
    near_1[2], near_1[3], pieces_2[1] = tie(near_1[2], near_1[3], pieces_2[1])
    source_far, near_1[0] = tie(source_far, near_1[0])
    source_low = jnp.concatenate([pick(inputs, x), source_far], axis=0)
    source_all = jnp.concatenate([source_low, swap_core(source_low)], axis=0)
    far_1 = list(gather_far(near_1))
    vectors, qkv_full, time_full = assemble(
        near_1, far_1, [0, 128, cut, piece_1.shape[1]], tiled
    )
    qkv_full = qkv_full.reshape(width, 3 * half)
    near_2 = list(gather_near(stack_z(pieces_2, tiled, tuple(far_1))))
    f = 2 * x + c
    blocks = jnp.stack([f, f ^ 2, f ^ 1, f ^ 3])
    positions = (blocks[:, None] * block + jnp.arange(block)[None, :]).reshape(tokens).astype(f32)
    pace = jnp.exp(jnp.arange(HD // 2, dtype=f32) * (-2.0 * math.log(10000.0) / HD))
    angles = positions[:, None] * pace[None, :]
    cosine = jnp.tile(jnp.cos(angles), (1, 4))
    sine = jnp.sin(angles)
    sine = jnp.tile(jnp.concatenate([-sine, sine], axis=1), (1, 2))

    vectors = vectors.reshape(chips, 2, rows, 128).astype(f32)
    packed = vectors[:, :, :3].reshape(chips, 2, 384)
    at = 0

    def take(n):
        nonlocal at
        at += 1 if tiled else n
        return vectors[:, :, at - 1, :n] if tiled else packed[:, :, at - n : at]

    bias_time = take(time_bias.shape[0]).reshape(2 * width)
    gain = take(rows).reshape(width)
    shift = take(rows).reshape(width)
    bias_up = pick(take(ff_rows), c, 1).reshape(ff)
    bias_down = take(rows).reshape(width)
    numbers = take(4)
    valid_total = jnp.sum(numbers[:, :, 0]) * 256.0 + jnp.sum(numbers[:, :, 1])
    steps = numbers[:, 0, 2] * 32.0 + numbers[:, 0, 3]
    token_total = 2 * depth * seqs * tokens
    factor = (token_total * width / 2) / (valid_total * width)

    spread = jnp.exp(jnp.arange(TE // 2, dtype=f32) * (-math.log(10000.0) / (TE // 2)))
    angle = steps[:, None] * spread[None]
    features = jnp.concatenate([jnp.sin(angle), jnp.cos(angle)], axis=1).astype(b16)
    feature_core = pick(pick(features, k_chip).reshape(chips, 2, te_rows), c, 1)
    time_parts = time_full.reshape(chips, te_folds, te_rows, -1).astype(f32)
    part = jnp.sum(feature_core.astype(f32)[:, None, :, None] * time_parts, axis=(0, 2))
    part = part.reshape(-1, 128)
    condition = (part + swap_core(part)).reshape(2, width) + bias_time.reshape(2, width)
    scale = 1.0 + condition[:1]
    hidden, project = project_tokens(source_all, scale, condition[1:], qkv_full)
    near_2[2], near_2[3], project = tie(near_2[2], near_2[3], project)
    far_2 = list(gather_far(near_2))
    ahead = pairs // 2
    turned_a, mixed_a, log_a = attend(project, cosine, sine, 0, ahead)
    turned_b, mixed_b, log_b = attend(project, cosine, sine, ahead, pairs - ahead, (mixed_a,))
    far_2[0], mixed_a, mixed_b = tie(far_2[0], mixed_a, mixed_b)
    target_far, far_2[1] = tie(pick(target_marks, 1 - x), far_2[1])
    target_far = swap_x(target_far)
    up_full, out_half = assemble(near_2, far_2, [0, ff, ff + half], tiled)
    up_full = up_full.reshape(width, ff)
    out_far = swap_core(out_half)
    if tiled:

        def copies(x, c, y, z):
            every = slice(None)
            return [
                (n, (every, pl.ds(h * rows, rows)), 0, (every, at, every, pl.ds(h * half, half)))
                for n, at in ((0, c), (1, 1 - c))
                for h in range(2)
            ]

        shape = jax.ShapeDtypeStruct((chips, 2, rows, width), b16)
        out_full = move(where, [out_half, out_far], [shape], copies)[0]
    else:
        out_both = jnp.stack(
            [jnp.where(c == 0, out_half, out_far), jnp.where(c == 0, out_far, out_half)], axis=1
        ).reshape(chips, 2, 2, rows, half)
        out_full = jnp.concatenate([out_both[:, :, 0], out_both[:, :, 1]], axis=-1)
    out_full = out_full.reshape(width, width)
    mixed = jnp.concatenate([mixed_a, mixed_b], axis=1)
    mixed_far = swap_core(mixed[mine:])
    mixture = jnp.where(
        c == 0,
        jnp.concatenate([mixed[:mine], mixed_far], axis=1),
        jnp.concatenate([mixed_far, mixed[:mine]], axis=1),
    )
    middle = source_low.astype(f32) + dot(mixture, out_full, 1, 0)
    n2, rate2 = stats(middle)
    second = (n2 * gain + shift).astype(b16)
    second_all = jnp.concatenate([second, swap_core(second)], axis=0)
    inner = dot(second_all, up_full, 1, 0) + bias_up
    flat = 0.5 * (1.0 + lax.erf(inner * (2.0**-0.5)))
    active = (inner * flat).astype(b16)
    slope = flat + inner * jnp.exp(-0.5 * inner * inner) * ((2.0 * math.pi) ** -0.5)
    active, target_far = tie(active, target_far)
    down = dot(active, down_full, 1, 0)
    result = middle + (down[:mine] + swap_core(down[mine:].astype(b16)).astype(f32) + bias_down)

    target_marks = jnp.concatenate([pick(target_marks, x), target_far], axis=0)
    target = target_marks[:, :width].astype(f32)
    mark = target_marks[:, width : width + 1].astype(f32)
    differ = result - target
    loss_part = jnp.sum(mark * differ * differ)
    result_grad = 2.0 * mark * differ * factor

    down_in = result_grad.astype(b16)
    down_in_all = jnp.concatenate([down_in, swap_core(down_in)], axis=0)
    near_axes = ("y", "x")
    result_low = result.astype(b16)
    down_term = dot(active, down_in_all, 0, 0).astype(b16)
    down_sum = Scatter(down_term.reshape(chips, -1, width), where, tiled)
    down_in_all, down_sum.got[0] = tie(down_in_all, down_sum.got[0])
    down_sum.near()
    inner_grad = (dot(down_in_all, down_full, 1, 1) * slope).astype(b16)
    second_part = dot(inner_grad, up_full, 1, 1)
    second_send, second_all, *down_sum.got = tie(
        second_part[mine:].astype(b16), second_all, *down_sum.got
    )
    second_got = swap_core(second_send)
    down_sum.add_near()
    second_all, down_sum.got[0] = tie(second_all, down_sum.got[0])
    down_sum.far()
    up_term = dot(second_all, inner_grad, 0, 0).astype(b16)
    up_sum = Scatter(up_term.reshape(chips, -1, ff), where, tiled)
    second_got, up_sum.got[0] = tie(second_got, up_sum.got[0])
    up_sum.near()
    second_grad = second_part[:mine] + second_got.astype(f32)
    middle_grad = result_grad + norm_back(second_grad * gain, n2, rate2)
    branch = middle_grad.astype(b16)
    mixture_grad = dot(branch, out_full, 1, 1).astype(b16)
    mixture_far, branch = tie(
        lax.dynamic_slice_in_dim(mixture_grad, (1 - c) * half, half, 1), branch
    )
    mixture_far = swap_core(mixture_far)
    out_term = dot(mixture, branch, 0, 0).astype(b16).reshape(chips, 2, rows, width)
    mixture_far, out_send, out_keep = tie(
        mixture_far, pick(out_term, 1 - c, 1), pick(out_term, c, 1)
    )
    out_got = swap_core(out_send)
    mixture_grad = jnp.concatenate(
        [lax.dynamic_slice_in_dim(mixture_grad, c * half, half, 1), mixture_far], axis=0
    )

    def pair_back(p, deps):
        turned, log = (turned_a, log_a) if p < ahead else (turned_b, log_b)
        at = p if p < ahead else p - ahead
        return attend_back(turned, log, mixture_grad, cosine, sine, at, p, 1, deps)

    grads = [pair_back(0, ())]
    grads.append(pair_back(1, (grads[-1],)))
    down_sum.got[0], down_sum.got[1], grads[-1] = tie(down_sum.got[0], down_sum.got[1], grads[-1])
    down_sum.add_far(True)
    grads[-1], down_sum.got[0] = tie(grads[-1], down_sum.got[0])
    down_sum.scatter_along()
    for p in range(2, pairs - 1):
        grads.append(pair_back(p, (grads[-1],)))
    up_sum.got[0], up_sum.got[1], grads[-1] = tie(up_sum.got[0], up_sum.got[1], grads[-1])
    up_sum.add_near()
    grads.append(pair_back(pairs - 1, (grads[-1], up_sum.keep[0])))
    up_sum.far()
    project_grad = jnp.concatenate(grads, axis=1)
    qkv_term = dot(hidden, project_grad, 0, 0).astype(b16).reshape(chips, 2 * rows, -1)
    qkv_cols = qkv_term.shape[2]
    out_term = add_low(out_keep, out_got)
    out_term = jnp.concatenate([out_term[:, :, :half], out_term[:, :, half:]], axis=1)
    last_sum = Scatter(jnp.concatenate([qkv_term, out_term], axis=2), where, tiled)
    project_grad, last_sum.got[0] = tie(project_grad, last_sum.got[0])
    last_sum.near()
    hidden_part = dot(project_grad, qkv_full, 1, 1)
    hidden_got, hidden_keep, *up_sum.got = tie(
        hidden_part[mine:].astype(b16), hidden_part[:mine], *up_sum.got
    )
    hidden_got = swap_core(hidden_got)
    up_sum.add_far(True)
    up_sum.got[0], hidden_got = tie(up_sum.got[0], hidden_got)
    up_sum.scatter_along()
    hidden_grad = hidden_keep + hidden_got.astype(f32)
    n1, rate1 = stats(source_low.astype(f32))
    input_grad = middle_grad + norm_back(hidden_grad * scale, n1, rate1)

    small = jnp.concatenate(
        [
            jnp.sum(hidden_grad * n1, 0),
            jnp.sum(hidden_grad, 0),
            jnp.sum(second_grad * n2, 0),
            jnp.sum(second_grad, 0),
            jnp.sum(down_in.astype(f32), 0),
            jnp.full((128,), loss_part),
        ]
    )
    small = small.reshape(-1, 128)
    small_got = swap_core(small)
    last_sum.got[0], input_grad = tie(last_sum.got[0], input_grad)
    last_sum.add_near()
    input_grad, last_sum.got[0] = tie(input_grad, last_sum.got[0])
    last_sum.far()
    small = small + small_got
    up_bias_part = jnp.sum(inner_grad.astype(f32), 0).reshape(-1, 128)
    fill = jnp.zeros((-(small.shape[0] + up_bias_part.shape[0]) % 8, 128), f32)
    small = jnp.concatenate([small, up_bias_part, fill], axis=0)
    small = gather_small(small)
    up_sum = up_sum.total()
    last_sum.add_far()
    input_far, result_far, last_sum.got[1] = tie(
        input_grad[block:].astype(b16), result_low[block:], last_sum.got[1]
    )
    last_sum.along()
    input_far = swap_x(input_far).astype(f32)
    result_far = swap_x(result_far)

    def spread_out(near, far):
        return jnp.stack([jnp.where(x == 0, near, far), jnp.where(x == 0, far, near)])

    activations = spread_out(result_low[:block], result_far)
    input_grad = spread_out(input_grad[:block], input_far)
    down_sum = down_sum.total()
    index = 2 * k_chip + c
    feature_rows = lax.dynamic_slice_in_dim(features, index * te_rows, te_rows, 1).astype(f32)
    time_sum, time_bias_sum, gain_sum, shift_sum, down_bias_sum, up_bias_sum, loss_sum = finish(
        jnp.stack([index, k_chip]), small, feature_rows.T, 2 * width, rows, ff_rows
    )
    loss = (loss_sum[0] / (valid_total * width)).reshape(1)

    def columns(total, inner_size):
        total = total.reshape(2, rows, -1, inner_size)
        near = pick(total, c)
        far = swap_core(pick(total, 1 - c))
        return jnp.stack(
            [jnp.where(c == 0, near, far), jnp.where(c == 0, far, near)], axis=2
        ).reshape(rows, -1)

    up_sum = columns(up_sum, ff_rows)
    others = (activations, input_grad, up_sum, down_sum, time_sum, loss)
    tied = tie(*last_sum.got, *others)
    last_sum.got = tied[: -len(others)]
    activations, input_grad, up_sum, down_sum, time_sum, loss = tied[-len(others) :]
    last_sum = last_sum.total()
    out_sum = last_sum[:, qkv_cols:]
    out_sum = jnp.concatenate([out_sum[:rows], out_sum[rows:]], axis=1)
    qkv_sum = last_sum[:, :qkv_cols].reshape(2 * rows, pairs, 3, 128)
    qkv_sum = qkv_sum.transpose(0, 2, 1, 3).reshape(2 * rows, -1)
    return (
        activations,
        loss,
        input_grad,
        columns(qkv_sum, half),
        out_sum,
        up_sum,
        down_sum,
        time_sum,
        time_bias_sum,
        gain_sum,
        shift_sum,
        up_bias_sum,
        down_bias_sum,
    )


def solution(mesh):
    split = mesh.devices.reshape(-1, 2, 2, 2)
    finer = jax.sharding.Mesh(split, ("z", "y", "x", "core"))
    both = ("z", "y", "x", "core")
    tokens = P(("z", "y"), ("x", "core"), None)
    weight = P(both, None)
    vector = P(both)
    return jax.shard_map(
        body,
        mesh=finer,
        in_specs=(tokens, tokens, P(("z", "y"), ("x", "core")), P(("z", "y"))) + (weight,) * 5 + (vector,) * 5,
        out_specs=(tokens, P(), tokens) + (weight,) * 5 + (vector,) * 5,
        check_vma=False,
    )
```
